32 devices in a mesh: views: 8 (over y, x, core), heads: 4 (over z).
Axes of the slice: x: 2, y: 2, z: 4, core: 2. Of those that a mesh axis runs over, the one named last changes fastest.
Arguments:
- latents: bfloat16 [32, 256, 1024], P('views'), may hold values from -6 to 6
- norm_gain: float32 [1024], replicated, may hold values from 0.25 to 1.75
- w_qkv: bfloat16 [3, 1024, 1024], P(None, None, 'heads'), may hold values from -0.1875 to 0.1875
- w_out: bfloat16 [1024, 1024], P('heads'), may hold values from -0.1875 to 0.1875
- intersection: int32 [32, 2], replicated, may hold values 0 or 1
- match_block: int32 [8192, 1], P('views'), may hold values from 0 to 7; in each aligned block of 1024 rows (0 to 1023, 1024 to 2047, ...) at most 256 rows name the same one
- match_row: int32 [8192], P('views'), may hold values from 0 to 1023
- confidence: float32 [8192], P('views'), may hold values from 0.2 to 1
Outputs:
- refined: float32 [32, 256, 1024], P('views', None, 'heads')
The draws below stay inside these ranges and needn't reach their ends.
Inputs may be any that keep to these rules, and one draw needn't show every extreme that they name: `match_block`: among the rows of one device (1024 aligned rows), at most 256 name the same block, and some block is named by exactly 256 of them.
All inputs are finite; a program needn't handle non-finite values.
Results may differ from the reference program's by a relative error of at most 0.012.
The reference program's roundings to bfloat16 on the way (of `normed`, `attended`, `layer_out` and `fetched`) count: a program that leaves them out, or rounds other values in their place, can miss the bound.
Values may be sent and summed in bfloat16 or wider, within the bound.
No kernel may reach another device: no remote copies, remote signals or barrier semaphores. Data moves between devices by JAX's collectives and lax.ppermute only.
A program may use at most 128 MiB of HBM per device.

```python
import math
import jax
import jax.numpy as jnp
import numpy as np
from jax import lax

D = 1024
HEADS = 16
TOK = 256
V_DEV = 4
WINDOW = 2
HEAD_DIM = 64
VIEWS = 32
ROWS = 8192
CAP = 256
N_VIEWS = 8
N_HEADS = 4


def draw_w_qkv(key, part):
    width = D
    limit = 6.0 / math.sqrt(width)
    pieces = jax.random.split(jax.random.fold_in(key, 7), 1)
    full = jax.random.normal(pieces[0], (3, width, width), jnp.float32) / math.sqrt(width)
    return jnp.clip(full, -limit, limit).astype(jnp.bfloat16)


def touch_ends(values, key, smallest, high):
    longest = values.shape.index(max(values.shape))
    spots = []
    for shift in (0, 1):
        where = [jax.random.randint(jax.random.fold_in(key, axis), (), 0, length) for axis, length in enumerate(values.shape)]
        where[longest] = (where[longest] + shift) % values.shape[longest]
        spots.append(tuple(where))
    return values.at[spots[0]].set(smallest).at[spots[1]].set(high)


def levels(own_key, dims, shards, low, top_value):
    loudness, own = 1.0, jax.random.fold_in(own_key, 6)
    for dim, shards_of in shards:
        draws = jnp.exp(jax.random.uniform(jax.random.fold_in(own, dim), (shards_of,), jnp.float32, low / len(shards), top_value / len(shards)))
        loudness = loudness * jnp.repeat(draws, dims[dim] // shards_of).reshape([-1 if axis == dim else 1 for axis in range(len(dims))])
    return loudness


def shared_out(stream_key, own, number, rows, amount, top, most, lean):
    ranking = jax.random.permutation(stream_key, amount)
    heavy_load, ordinary = shares(amount, rows * top, most, lean, True), shares(amount, rows * top, most, lean, False)
    places = jnp.arange(amount)

    def named(tallies, turn):
        used = int((tallies > 0).sum())
        fixed = max(1, used // 4)
        shifted = fixed + (places - fixed + turn * (used - fixed)) % max(1, amount - fixed)
        return jnp.zeros((amount,), jnp.int32).at[ranking[jnp.where(places < fixed, places, shifted)]].set(jnp.asarray(tallies, jnp.int32))

    tallies = jnp.where(number % 4 == 0, named(heavy_load, number // 4), named(ordinary, number - number // 4 - 1))
    mixed = jax.random.permutation(jax.random.fold_in(own, 3), amount)
    source_of, receiver = mixed[0:amount // 2 * 2:2], mixed[1:amount // 2 * 2:2]
    room = jnp.minimum(tallies[source_of] - 1, most - tallies[receiver]) // 2
    room = jnp.where((source_of == ranking[0]) | (receiver == ranking[0]) | (tallies[receiver] == 0), 0, jnp.maximum(room, 0))
    shifted = jax.random.randint(jax.random.fold_in(own, 4), (amount // 2,), 0, 1 << 20) % (room + 1)
    tallies = tallies.at[source_of].add(-shifted).at[receiver].add(shifted)
    items = jnp.searchsorted(jnp.cumsum(tallies), jnp.arange(rows * top), side="right").astype(jnp.int32)
    table = items.reshape(top, rows).T
    table = table[jax.random.permutation(jax.random.fold_in(own, 1), rows)]
    turn = jax.random.randint(jax.random.fold_in(own, 2), (rows, 1), 0, top)
    return jnp.take_along_axis(table, (jnp.arange(top)[None, :] + turn) % top, axis=1)


def shares(count, total, most, lean, full):
    weights = [(1 << 20) // math.isqrt(rank ** lean) + 1 for rank in range(1, count + 1)]
    largest = most if full else min(most, max(-(-total // count), total * weights[0] // sum(weights)))
    least = 1 if total - largest >= count - 1 else 0
    given, rest = [largest] + [least] * (count - 1), total - largest - least * (count - 1)
    while rest > 0:
        free = [i for i in range(1, count) if given[i] < largest] or [i for i in range(1, count) if given[i] < most]
        pool, left = sum([weights[i] for i in free]), rest
        for i in free:
            more = min(most - given[i], max(1, left * weights[i] // pool), rest)
            given[i] = given[i] + more
            rest = rest - more
    return np.array(given)


def bell_draw(stream_key, extent, scale, bound, cuts=(), kind=jnp.bfloat16):
    loudness = levels(stream_key, extent, cuts, -0.22, 0.18) if cuts else 1.0
    drawn = jax.random.normal(stream_key, extent, jnp.float32) * scale * loudness
    return jnp.minimum(jnp.maximum(drawn, -bound), bound).astype(kind)


def setup_inputs(seed: int = 0) -> dict:
    streams_of = jax.random.split(jax.random.key(seed), 9)
    latents = bell_draw(streams_of[0], (VIEWS, TOK, D), 1.0, 6.0, ((0, 8),))
    norm_gain = jnp.clip(1.0 + 0.15 * jax.random.normal(streams_of[1], (D,), jnp.float32), 0.25, 1.75)
    w_qkv = draw_w_qkv(jax.random.fold_in(streams_of[8], 71), 0)
    w_out = bell_draw(streams_of[3], (D, D), D ** -0.5, 0.1875, ((0, 4),))
    intersection = touch_ends((jax.random.randint(streams_of[4], (VIEWS, WINDOW), 0, 3) < 2).astype(jnp.int32), jax.random.fold_in(streams_of[4], 1), 0, 1)
    match_block_keys = jax.random.split(jax.random.fold_in(streams_of[5], 1), ROWS // (V_DEV * TOK))
    match_block_turns = jax.random.permutation(jax.random.fold_in(streams_of[5], 3), ROWS // (V_DEV * TOK))
    match_block = jax.vmap(lambda own, number: shared_out(jax.random.fold_in(streams_of[5], 2), own, number, V_DEV * TOK, N_VIEWS, 1, CAP, 2))(match_block_keys, match_block_turns).reshape((ROWS, 1))
    match_row = touch_ends(jax.random.randint(streams_of[6], (ROWS,), 0, V_DEV * TOK), jax.random.fold_in(streams_of[6], 1), 0, (V_DEV * TOK) - 1).astype(jnp.int32)
    confidence = jnp.clip(jnp.exp(math.log(1.0) - 1.609438 * jax.random.uniform(streams_of[7], (ROWS,), jnp.float32) ** levels(streams_of[7], (ROWS,), ((0, 8),), -0.2, 0.2)), 0.2, 1.0)
    return dict(latents=latents, norm_gain=norm_gain, w_qkv=w_qkv, w_out=w_out, intersection=intersection, match_block=match_block, match_row=match_row, confidence=confidence)


neg_large = -1e+30
coupling = 0.5
epsilon = 1e-06

def partial_block(queries, keys, values):
    query_heads = queries.reshape(TOK, HEADS, HEAD_DIM).astype(jnp.float32)
    key_heads = keys.reshape(TOK, HEADS, HEAD_DIM).astype(jnp.float32)
    value_heads = values.reshape(TOK, HEADS, HEAD_DIM).astype(jnp.float32)
    scores = jnp.einsum('qhd,khd->hqk', query_heads, key_heads) * HEAD_DIM ** (-0.5)
    maximum = lax.optimization_barrier(jnp.max(scores, axis=-1))
    weights = jnp.exp(scores - maximum[..., None])
    totals = lax.optimization_barrier(jnp.sum(weights, axis=-1))
    rounded = weights.astype(jnp.bfloat16).astype(jnp.float32)
    numerator = jnp.einsum('hqk,khd->hqd', rounded, value_heads)
    return (maximum, totals, numerator)

def merge_into(running, piece_part, present):
    maximum, totals, numerator = running
    other_max, other_tot, other_num = piece_part
    other_max = jnp.where(present > 0, other_max, neg_large)
    highest = jnp.maximum(maximum, other_max)
    old_scale = jnp.exp(maximum - highest)
    new_scale = jnp.exp(other_max - highest) * present
    return (highest, totals * old_scale + other_tot * new_scale, numerator * old_scale[..., None] + other_num * new_scale[..., None])

def reference(latents, norm_gain, w_qkv, w_out, intersection, match_block, match_row, confidence):
    wide_latents = latents.astype(jnp.float32)
    mean_square = lax.optimization_barrier(jnp.mean(wide_latents * wide_latents, axis=-1, keepdims=True))
    normed = (wide_latents * lax.rsqrt(mean_square + epsilon) * norm_gain).astype(jnp.bfloat16)
    flat_normed = normed.reshape(ROWS, D)
    all_queries = jnp.dot(flat_normed, w_qkv[0], preferred_element_type=jnp.float32).astype(jnp.bfloat16).reshape(VIEWS, TOK, D)
    all_keys = jnp.dot(flat_normed, w_qkv[1], preferred_element_type=jnp.float32).astype(jnp.bfloat16).reshape(VIEWS, TOK, D)
    all_values = jnp.dot(flat_normed, w_qkv[2], preferred_element_type=jnp.float32).astype(jnp.bfloat16).reshape(VIEWS, TOK, D)

    def view_attention(view_index):
        queries = all_queries[view_index]
        running = partial_block(queries, all_keys[view_index], all_values[view_index])
        for offset in range(WINDOW):
            forward = (view_index + offset + 1) % VIEWS
            present = intersection[view_index, offset].astype(jnp.float32)
            running = merge_into(running, partial_block(queries, all_keys[forward], all_values[forward]), present)
        for offset in range(WINDOW):
            backward = (view_index - offset - 1) % VIEWS
            present = intersection[backward, offset].astype(jnp.float32)
            running = merge_into(running, partial_block(queries, all_keys[backward], all_values[backward]), present)
        maximum, totals, numerator = running
        result = numerator / totals[..., None]
        return jnp.transpose(result, (1, 0, 2)).reshape(TOK, D).astype(jnp.bfloat16)
    attended = lax.map(view_attention, jnp.arange(VIEWS, dtype=jnp.int32)).reshape(ROWS, D)
    group_width = D // N_HEADS
    projected = jnp.zeros((ROWS, D), jnp.float32)
    for head_group in range(N_HEADS):
        group_part = jnp.dot(attended[:, head_group * group_width:(head_group + 1) * group_width], w_out[head_group * group_width:(head_group + 1) * group_width], preferred_element_type=jnp.float32).astype(jnp.bfloat16)
        group_part = lax.optimization_barrier(group_part)
        projected = projected + group_part.astype(jnp.float32)
    layer_out = (latents.reshape(ROWS, D).astype(jnp.float32) + projected).astype(jnp.bfloat16)
    layer_out = lax.optimization_barrier(layer_out)
    target_rows = (match_block[:, 0] * (V_DEV * TOK) + match_row).astype(jnp.int32)
    fetched = layer_out[target_rows].astype(jnp.float32)
    layer_wide = layer_out.astype(jnp.float32)
    refined = layer_wide + coupling * confidence[:, None] * (fetched - layer_wide)
    return refined.astype(jnp.float32).reshape(VIEWS, TOK, D)
```

```python
import functools

import jax
import jax.numpy as jnp
from jax import lax
from jax.experimental import pallas as pl
from jax.experimental.pallas import tpu as pltpu
from jax.sharding import PartitionSpec as P

HEAD_DIM = 64
LANES = 128

neg_large = -1e30
coupling = 0.5
epsilon = 1e-06

bf16 = jnp.bfloat16
f32 = jnp.float32


def cost(flops, bytes_accessed, transcendentals=0):
    return pl.CostEstimate(
        flops=int(flops), bytes_accessed=int(bytes_accessed), transcendentals=int(transcendentals)
    )


def dot(a, b):
    return jnp.dot(a, b, preferred_element_type=f32)


def whole(*shape):
    return pl.BlockSpec(shape, lambda *_: (0,) * len(shape))


SMEM_SPEC = pl.BlockSpec(memory_space=pltpu.SMEM)


def qkv_kernel(count, lats, gain_ref, w_ref, outs):
    scale = HEAD_DIM ** (-0.5)
    for i in range(count):
        wide = lats[i][0].astype(f32)
        mean_square = jnp.mean(wide * wide, axis=-1, keepdims=True)
        normed = (wide * lax.rsqrt(mean_square + epsilon) * gain_ref[...]).astype(bf16)
        keys = dot(normed, w_ref[1]).astype(bf16)
        outs[2 * i + 1][0] = keys
        values = dot(normed, w_ref[2])
        outs[2 * i + 1][1] = jnp.transpose(values).astype(bf16)
        queries = dot(normed, w_ref[0])
        outs[2 * i][...] = jnp.transpose(queries).astype(bf16) * jnp.asarray(scale, bf16)


def project_views(latents, gain, w_qkv, which):
    _, tokens, width = latents.shape
    sub = w_qkv.shape[2]
    count = len(which)

    def body(*refs):
        qkv_kernel(count, refs[:count], refs[count], refs[count + 1], refs[count + 2 :])

    in_specs = [pl.BlockSpec((1, tokens, width), functools.partial(lambda v, i: (v, 0, 0), v)) for v in which]
    in_specs += [whole(1, width), whole(3, width, sub)]
    out_shape, out_specs = [], []
    for _ in which:
        out_shape += [
            jax.ShapeDtypeStruct((sub, tokens), bf16),
            jax.ShapeDtypeStruct((2, tokens, sub), bf16),
        ]
        out_specs += [whole(sub, tokens), whole(2, tokens, sub)]
    outs = pl.pallas_call(
        body,
        grid=(1,),
        in_specs=in_specs,
        out_specs=out_specs,
        out_shape=out_shape,
        name="project_views",
        cost_estimate=cost(
            count * 6 * tokens * width * sub, count * tokens * (width + 3 * sub) * 2 + 6 * width * sub
        ),
    )(*([latents] * count), gain, w_qkv)
    return {v: (outs[2 * i], outs[2 * i + 1]) for i, v in enumerate(which)}


def head_scores(q_ref, k_ref, h):
    per = LANES // HEAD_DIM
    j, slot = h // per, h % per
    own = q_ref[h * HEAD_DIM : (h + 1) * HEAD_DIM, :]
    zero = jnp.zeros_like(own)
    padded = jnp.concatenate([own if s == slot else zero for s in range(per)], axis=0)
    return dot(k_ref[0, :, j * LANES : (j + 1) * LANES], padded)


def weighted(v_ref, weights, h):
    return dot(v_ref[1, h * HEAD_DIM : (h + 1) * HEAD_DIM, :], weights.astype(bf16))


def start_view(q_ref, kv_ref, acc_ref, stat_ref, heads):
    for h in range(heads):
        scores = head_scores(q_ref, kv_ref, h)
        top = jnp.max(scores, axis=0, keepdims=True)
        weights = jnp.exp(scores - top)
        stat_ref[h : h + 1, :] = top
        stat_ref[heads + h : heads + h + 1, :] = jnp.sum(weights, axis=0, keepdims=True)
        acc_ref[h * HEAD_DIM : (h + 1) * HEAD_DIM, :] = weighted(kv_ref, weights, h)


def add_view(q_ref, kv_ref, acc_ref, stat_ref, heads):
    for h in range(heads):
        scores = head_scores(q_ref, kv_ref, h)
        old = stat_ref[h : h + 1, :]
        top = jnp.maximum(old, jnp.max(scores, axis=0, keepdims=True))
        weights = jnp.exp(scores - top)
        fade = jnp.exp(old - top)
        stat_ref[h : h + 1, :] = top
        total = stat_ref[heads + h : heads + h + 1, :]
        stat_ref[heads + h : heads + h + 1, :] = total * fade + jnp.sum(weights, axis=0, keepdims=True)
        rows = slice(h * HEAD_DIM, (h + 1) * HEAD_DIM)
        acc_ref[rows, :] = acc_ref[rows, :] * fade + weighted(kv_ref, weights, h)


def attention_cost(tokens, sub, pairs):
    heads = sub // HEAD_DIM
    return cost(
        pairs * heads * tokens * tokens * 4 * LANES,
        pairs * tokens * sub * 8,
        pairs * heads * tokens * tokens,
    )


def local_attention(meta, intersection, blocks, local_views, window):
    q0, kv0 = blocks[0]
    sub, tokens = q0.shape
    heads = sub // HEAD_DIM
    views_total = intersection.shape[0]

    def body(meta_ref, inter_ref, *refs):
        qs, kvs = refs[:local_views], refs[local_views : 2 * local_views]
        acc, stat = refs[2 * local_views :]
        first = meta_ref[0] * local_views
        for v in range(local_views):
            start_view(qs[v], kvs[v], acc.at[v], stat.at[v], heads)
        for v in range(local_views):
            for o in range(window):
                t = v + o + 1
                if t < local_views:

                    @pl.when(inter_ref[first + v, o] > 0)
                    def _(v=v, t=t):
                        add_view(qs[v], kvs[t], acc.at[v], stat.at[v], heads)
                        add_view(qs[t], kvs[v], acc.at[t], stat.at[t], heads)

    pairs = local_views * (2 * window + 1) - window * (window + 1)
    return pl.pallas_call(
        body,
        grid=(1,),
        in_specs=[SMEM_SPEC, SMEM_SPEC]
        + [whole(sub, tokens)] * local_views
        + [whole(2, tokens, sub)] * local_views,
        out_specs=[whole(local_views, sub, tokens), whole(local_views, 2 * heads, tokens)],
        out_shape=[
            jax.ShapeDtypeStruct((local_views, sub, tokens), f32),
            jax.ShapeDtypeStruct((local_views, 2 * heads, tokens), f32),
        ],
        name="local_attention",
        cost_estimate=attention_cost(tokens, sub, pairs),
    )(
        meta,
        intersection,
        *[blocks[v][0] for v in range(local_views)],
        *[blocks[v][1] for v in range(local_views)],
    )


def finish_attention(meta, intersection, acc, stat, local_views, plan, queries, remote):
    _, sub, tokens = acc.shape
    heads = sub // HEAD_DIM
    views_total = intersection.shape[0]
    names = sorted(remote)
    count = len(plan)

    def body(meta_ref, inter_ref, *refs):
        accs, stats = refs[:count], refs[count : 2 * count]
        qs = refs[2 * count : 3 * count]
        kvs = dict(zip(names, refs[3 * count : 3 * count + len(names)]))
        out, work, work_stat = refs[3 * count + len(names) :]
        first = meta_ref[0] * local_views
        for i, (view, sources) in enumerate(plan):
            work[i] = accs[i][0]
            work_stat[i] = stats[i][0]
            for name, source, offset in sources:
                at = first + source
                if source < 0:
                    at = jnp.where(at < 0, at + views_total, at)

                @pl.when(inter_ref[at, offset] > 0)
                def _(i=i, name=name):
                    add_view(qs[i], kvs[name], work.at[i], work_stat.at[i], heads)

        for i in range(count):
            parts = []
            for h in range(heads):
                total = work_stat[i, heads + h : heads + h + 1, :]
                parts.append(work[i, h * HEAD_DIM : (h + 1) * HEAD_DIM, :] / total)
            out[i] = jnp.transpose(jnp.concatenate(parts, axis=0)).astype(bf16)

    def view_spec(shape, v):
        return pl.BlockSpec((1,) + shape, lambda i: (v, 0, 0))

    pairs = sum(len(s) for _, s in plan)
    return pl.pallas_call(
        body,
        grid=(1,),
        in_specs=[SMEM_SPEC, SMEM_SPEC]
        + [view_spec((sub, tokens), v) for v, _ in plan]
        + [view_spec((2 * heads, tokens), v) for v, _ in plan]
        + [whole(sub, tokens)] * count
        + [whole(2, tokens, sub)] * len(names),
        out_specs=whole(count, tokens, sub),
        out_shape=jax.ShapeDtypeStruct((count, tokens, sub), bf16),
        scratch_shapes=[
            pltpu.VMEM((count, sub, tokens), f32),
            pltpu.VMEM((count, 2 * heads, tokens), f32),
        ],
        name="finish_attention",
        cost_estimate=attention_cost(tokens, sub, pairs),
    )(meta, intersection, *([acc] * count), *([stat] * count), *queries, *[remote[n] for n in names])


def project_out(meta, attended, weights, latents, view_of):
    count, tokens, sub = attended[0].shape
    groups = len(attended)

    def body(meta_ref, *refs):
        att, ws = refs[:groups], refs[groups : 2 * groups]
        lat, own, other = refs[2 * groups :]
        total = None
        for a, w in zip(att, ws):
            part = dot(a[0], w[...]).astype(bf16).astype(f32)
            total = part if total is None else total + part
        layer = (lat[0].astype(f32) + total).astype(bf16)
        low, high = layer[:, :sub], layer[:, sub:]
        odd = lax.rem(meta_ref[1], 2) == 1
        own[0] = jnp.where(odd, high, low)
        other[0] = jnp.where(odd, low, high)

    att_spec = pl.BlockSpec((1, tokens, sub), lambda i, m: (i, 0, 0))
    return pl.pallas_call(
        body,
        grid_spec=pltpu.PrefetchScalarGridSpec(
            num_scalar_prefetch=1,
            grid=(count,),
            in_specs=[att_spec] * groups
            + [whole(sub, 2 * sub)] * groups
            + [pl.BlockSpec((1, tokens, 2 * sub), lambda i, m: (view_of(i), 0, m[1] // 2))],
            out_specs=[att_spec, att_spec],
        ),
        out_shape=[jax.ShapeDtypeStruct((count, tokens, sub), bf16)] * 2,
        name="project_out",
        cost_estimate=cost(
            groups * count * tokens * sub * 4 * sub,
            groups * (count * tokens * sub + 2 * sub * sub) * 2 + count * tokens * sub * 8,
        ),
    )(meta, *attended, *weights, latents)


def prepare_requests(block_rows, token_rows, peers, capacity):
    strips, lanes = block_rows.shape

    def body(block_ref, token_ref, wanted_ref, code_ref):
        before = (
            lax.broadcasted_iota(jnp.int32, (lanes, lanes), 0)
            < lax.broadcasted_iota(jnp.int32, (lanes, lanes), 1)
        ).astype(bf16)
        peer_ids = lax.broadcasted_iota(jnp.int32, (peers, lanes), 0)
        carry = jnp.zeros((peers, 1), f32)
        slots, lefts = [], []
        for i in range(strips):
            block = block_ref[i : i + 1, :]
            hit = (peer_ids == block).astype(f32)
            rank = dot(hit.astype(bf16), before) + carry
            carry = carry + jnp.sum(hit, axis=1, keepdims=True)
            slot = jnp.sum(rank * hit, axis=0, keepdims=True)
            slots.append(slot)
            code_ref[i : i + 1, :] = block * capacity + slot.astype(jnp.int32)
            token = token_ref[i : i + 1, :]
            coarse = (token // 32).astype(f32)
            fine = (token % 32).astype(f32)
            lefts.append(jnp.concatenate([hit * coarse, hit * fine], axis=0).astype(bf16))
        columns = jnp.transpose(jnp.concatenate(slots, axis=0))
        place = lax.broadcasted_iota(jnp.int32, (lanes, capacity), 1).astype(f32)
        total = jnp.zeros((2 * peers, capacity), f32)
        for i in range(strips):
            spot = (columns[:, i : i + 1] == place).astype(bf16)
            total = total + dot(lefts[i], spot)
        wanted_ref[...] = (total[:peers] * 32.0 + total[peers:]).astype(jnp.int32)

    return pl.pallas_call(
        body,
        out_shape=[
            jax.ShapeDtypeStruct((peers, capacity), jnp.int32),
            jax.ShapeDtypeStruct((strips, lanes), jnp.int32),
        ],
        name="prepare_requests",
        cost_estimate=cost(2 * strips * lanes * lanes * capacity, 3 * strips * lanes * 4),
    )(block_rows, token_rows)


def gather_rows(meta, wanted, pieces, place_of):
    peers, capacity = wanted.shape
    _, tokens, sub = pieces[0][0].shape
    local_views = len(place_of)
    rows = local_views * tokens
    flat = [p for pair in pieces for p in pair]

    def body(meta_ref, wanted_ref, *refs):
        ins = refs[: len(flat)]
        layer, outs = refs[len(flat)], refs[len(flat) + 1 :]
        end = jnp.logical_or(meta_ref[1] == 0, meta_ref[1] == meta_ref[2] - 1)
        for v, (c, i) in enumerate(place_of):
            layer[v * tokens : (v + 1) * tokens, :] = jnp.where(
                end, ins[2 * c + 1][i], ins[2 * c][i]
            )
        full = layer[...]
        row_ids = lax.broadcasted_iota(jnp.int32, (capacity, rows), 1)
        for mask in range(peers):
            peer = lax.bitwise_xor(meta_ref[0], mask)
            line = wanted_ref[pl.ds(peer, 1), :]
            column = jnp.transpose(jnp.broadcast_to(line, (8, capacity)))[:, :1]
            pick = jnp.where(column == row_ids, 1.0, 0.0).astype(bf16)
            outs[mask][...] = dot(pick, full).astype(bf16)

    return pl.pallas_call(
        body,
        grid=(1,),
        in_specs=[SMEM_SPEC, whole(peers, capacity)] + [whole(*p.shape) for p in flat],
        out_specs=[whole(rows, sub)] + [whole(capacity, sub)] * peers,
        out_shape=[jax.ShapeDtypeStruct((rows, sub), bf16)]
        + [jax.ShapeDtypeStruct((capacity, sub), bf16)] * peers,
        name="gather_rows",
        cost_estimate=cost(2 * peers * capacity * rows * sub, 2 * (rows + peers * capacity) * sub * 2),
    )(meta, wanted, *flat)


def finish_rows(meta, code, confidence, layer, replies, tokens):
    rows, sub = layer.shape
    peers = len(replies)
    capacity = replies[0].shape[0]
    strips, lanes = code.shape
    blocks = rows // tokens
    per = tokens // lanes

    def column_of(rows_ref, g):
        turned = jnp.transpose(rows_ref[...].astype(f32))
        lane = lax.broadcasted_iota(jnp.int32, turned.shape, 1)
        parts = [
            jnp.sum(jnp.where(lane == g * per + j, turned, 0.0), axis=1, keepdims=True)
            for j in range(per)
        ]
        return jnp.concatenate(parts, axis=0)

    def body(meta_ref, code_ref, conf_ref, layer_ref, *refs):
        reps, out = refs[:peers], refs[peers]
        g = pl.program_id(0)
        codes = column_of(code_ref, g)
        weight = column_of(conf_ref, g) * coupling
        place = lax.broadcasted_iota(jnp.int32, (tokens, capacity), 1).astype(f32)
        fetched = None
        for mask in range(peers):
            peer = lax.bitwise_xor(meta_ref[0], mask)
            shifted = codes - (peer * capacity).astype(f32)
            pick = jnp.where(shifted == place, 1.0, 0.0).astype(bf16)
            part = dot(pick, reps[mask][...])
            fetched = part if fetched is None else fetched + part
        wide = layer_ref[...].astype(f32)
        out[...] = wide + weight * (fetched - wide)

    row_spec = pl.BlockSpec((tokens, sub), lambda g: (g, 0))
    return pl.pallas_call(
        body,
        grid=(blocks,),
        in_specs=[SMEM_SPEC, whole(strips, lanes), whole(strips, lanes), row_spec]
        + [whole(capacity, sub)] * peers,
        out_specs=row_spec,
        out_shape=jax.ShapeDtypeStruct((rows, sub), f32),
        name="finish_rows",
        cost_estimate=cost(2 * peers * capacity * rows * sub, rows * sub * 6 + peers * capacity * sub * 2),
    )(meta, code, confidence, layer, *replies)


def per_device(latents, norm_gain, w_qkv, w_out, intersection, match_block, match_row, confidence):
    local_views, tokens, width = latents.shape
    window = intersection.shape[1]
    sub = w_qkv.shape[2]
    peers = lax.axis_size("views")
    ends = lax.axis_size("heads")
    rows = local_views * tokens
    capacity = 2 * rows // peers
    assert local_views == 4 and window == 2 and ends == 4 and tokens == sub
    view_at, head_at = lax.axis_index("views"), lax.axis_index("heads")
    spot = jnp.arange(4, dtype=jnp.int32)
    meta = jnp.where(spot == 0, view_at, jnp.where(spot == 1, head_at, ends)).astype(jnp.int32)

    def along(x, by):
        return lax.ppermute(x, "views", [(i, (i + by) % peers) for i in range(peers)])

    def across(x, pairs):
        return lax.ppermute(x, "heads", pairs)

    beside, middle, beyond, back = (
        [(0, 1), (3, 2)],
        [(1, 2), (2, 1)],
        [(0, 2), (3, 1)],
        [(1, 0), (2, 3)],
    )
    gain = norm_gain.reshape(1, width)
    blocks = project_views(latents, gain, w_qkv, (0, local_views - 1))
    next_first = along(blocks[0][1], -1)
    prev_last = along(blocks[3][1], 1)
    blocks.update(project_views(latents, gain, w_qkv, (1, 2)))
    next_second = along(blocks[1][1], -1)
    prev_second = along(blocks[2][1], 1)

    half = 2 * sub
    low_end = head_at // 2
    own_half = lax.dynamic_slice_in_dim(w_out, low_end * half, half, 1)
    other_half = lax.dynamic_slice_in_dim(w_out, (1 - low_end) * half, half, 1)
    weights = [
        own_half,
        across(own_half, beside),
        across(other_half, middle),
        across(other_half, beyond),
    ]

    strips = rows // LANES
    wanted, code = prepare_requests(
        match_block.reshape(strips, LANES), match_row.reshape(strips, LANES), peers, capacity
    )
    wanted = lax.all_to_all(wanted, "views", split_axis=0, concat_axis=0, tiled=True)

    acc, stat = local_attention(meta, intersection, blocks, local_views, window)
    finish = functools.partial(finish_attention, meta, intersection, acc, stat, local_views)
    inner = finish(
        [(1, [("prev_last", -1, 1)]), (2, [("next_first", 2, 1)])],
        [blocks[1][0], blocks[2][0]],
        dict(prev_last=prev_last, next_first=next_first),
    )
    outer = finish(
        [
            (0, [("prev_last", -1, 0), ("prev_second", -2, 1)]),
            (3, [("next_first", 3, 0), ("next_second", 3, 1)]),
        ],
        [blocks[0][0], blocks[3][0]],
        dict(
            prev_last=prev_last,
            next_first=next_first,
            prev_second=prev_second,
            next_second=next_second,
        ),
    )
    pieces = []
    for chunk, view_of in ((inner, lambda i: i + 1), (outer, lambda i: 3 * i)):
        attended = [chunk, across(chunk, beside), across(chunk, middle), across(chunk, beyond)]
        own, other = project_out(meta, attended, weights, latents, view_of)
        pieces.append((own, across(other, back)))

    place_of = [(1, 0), (0, 0), (0, 1), (1, 1)]
    layer, *outgoing = gather_rows(meta, wanted, pieces, place_of)
    replies = [outgoing[0]]
    for mask in range(1, peers):
        replies.append(lax.ppermute(outgoing[mask], "views", [(i, i ^ mask) for i in range(peers)]))
    refined = finish_rows(
        meta, code, confidence.reshape(strips, LANES), layer, replies, tokens
    )
    return refined.reshape(local_views, tokens, sub)


def solution(mesh):
    in_specs = (
        P("views", None, None),
        P(),
        P(None, None, "heads"),
        P("heads", None),
        P(),
        P("views", None),
        P("views"),
        P("views"),
    )
    out_specs = P("views", None, "heads")
    return jax.shard_map(
        per_device, mesh=mesh, in_specs=in_specs, out_specs=out_specs, check_vma=False
    )
```

```python
import functools

import jax
import jax.numpy as jnp
from jax import lax
from jax.experimental import pallas as pl
from jax.experimental.pallas import tpu as pltpu
from jax.sharding import PartitionSpec as P


HEAD_DIM = 64
LANES = 128

neg_large = -1e30
coupling = 0.5
epsilon = 1e-06

bf16 = jnp.bfloat16
f32 = jnp.float32


def cost(flops, bytes_accessed, transcendentals=0):
    return pl.CostEstimate(
        flops=int(flops), bytes_accessed=int(bytes_accessed), transcendentals=int(transcendentals)
    )


def dot(a, b):
    return jnp.dot(a, b, preferred_element_type=f32)


VMEM_SPEC = pl.BlockSpec(memory_space=pltpu.VMEM)
SMEM_SPEC = pl.BlockSpec(memory_space=pltpu.SMEM)
ANY_SPEC = pl.BlockSpec(memory_space=pl.ANY)


def grant(mib):
    return pltpu.CompilerParams(vmem_limit_bytes=mib << 20)


def many(spec, count):
    return [spec] * count


def project_views(latents, gain, w_qkv, which):
    _, tokens, width = latents.shape
    sub = w_qkv.shape[2]
    count = len(which)
    scale = HEAD_DIM ** (-0.5)

    def body(lat_hbm, gain_ref, w_ref, *refs):
        outs, (buffer, sems) = refs[: 2 * count], refs[2 * count :]
        copies = [
            pltpu.make_async_copy(lat_hbm.at[v], buffer.at[i], sems.at[i])
            for i, v in enumerate(which)
        ]
        for copy in copies:
            copy.start()
        for i in range(count):
            copies[i].wait()
            wide = buffer[i].astype(f32)
            mean_square = jnp.mean(wide * wide, axis=-1, keepdims=True)
            normed = (wide * lax.rsqrt(mean_square + epsilon) * gain_ref[...]).astype(bf16)
            values = dot(normed, w_ref[2])
            queries = dot(normed, w_ref[0])
            outs[2 * i + 1][0] = dot(normed, w_ref[1]).astype(bf16)
            outs[2 * i + 1][1] = jnp.transpose(values).astype(bf16)
            outs[2 * i][...] = jnp.transpose(queries).astype(bf16) * jnp.asarray(scale, bf16)

    out_shape = []
    for _ in which:
        out_shape += [
            jax.ShapeDtypeStruct((sub, tokens), bf16),
            jax.ShapeDtypeStruct((2, tokens, sub), bf16),
        ]
    outs = pl.pallas_call(
        body,
        in_specs=[ANY_SPEC, VMEM_SPEC, VMEM_SPEC],
        out_specs=many(VMEM_SPEC, 2 * count),
        out_shape=out_shape,
        scratch_shapes=[
            pltpu.VMEM((count, tokens, width), bf16),
            pltpu.SemaphoreType.DMA((count,)),
        ],
        name="project_views",
        compiler_params=grant(12),
        cost_estimate=cost(
            count * 6 * tokens * width * sub, count * tokens * (width + 3 * sub) * 2 + 6 * width * sub
        ),
    )(latents, gain, w_qkv)
    return {v: (outs[2 * i], outs[2 * i + 1]) for i, v in enumerate(which)}


ONES = 16
SAFE_TOTAL = 1e30
FAR = 1e30


def head_scores(q_ref, kv_ref, h):
    per = LANES // HEAD_DIM
    j, slot = h // per, h % per
    own = q_ref[h * HEAD_DIM : (h + 1) * HEAD_DIM, :]
    zero = jnp.zeros_like(own)
    padded = jnp.concatenate([own if s == slot else zero for s in range(per)], axis=0)
    return dot(kv_ref[0, :, j * LANES : (j + 1) * LANES], padded)


def head_values(kv_ref, h):
    rows = kv_ref[1, h * HEAD_DIM : (h + 1) * HEAD_DIM, :]
    return jnp.concatenate([rows, jnp.ones((ONES, rows.shape[1]), bf16)], axis=0)


def attention_cost(tokens, sub, pairs):
    heads = sub // HEAD_DIM
    return cost(
        pairs * heads * tokens * tokens * 4 * LANES,
        pairs * tokens * sub * 8,
        pairs * heads * tokens * tokens,
    )


def far_if_absent(inter_ref, at, offset):
    return jnp.where(inter_ref[at, offset] > 0, 0.0, FAR).astype(f32)


def local_attention(meta, intersection, blocks, local_views, window):
    sub, tokens = blocks[0][0].shape
    heads = sub // HEAD_DIM
    tall = HEAD_DIM + ONES

    def body(meta_ref, inter_ref, *refs):
        qs, kvs = refs[:local_views], refs[local_views : 2 * local_views]
        acc, stat = refs[2 * local_views :]
        first = meta_ref[0] * local_views
        groups = [(v, h) for v in range(local_views) for h in range(heads)]

        def others(v):
            found = []
            for o in range(window):
                if v + o + 1 < local_views:
                    found.append((v + o + 1, v, o))
                if v - o - 1 >= 0:
                    found.append((v - o - 1, v - o - 1, o))
            return found

        far = {
            (v, t): far_if_absent(inter_ref, first + source, o)
            for v in range(local_views)
            for t, source, o in others(v)
        }
        following = head_scores(qs[0], kvs[0], 0)
        for n, (v, h) in enumerate(groups):
            scores = following
            top = jnp.max(scores, axis=0, keepdims=True)
            stat[v, h : h + 1, :] = top
            keys = [t for t, _, _ in others(v)]
            upcoming = head_scores(qs[v], kvs[keys[0]], h)
            weights = [jnp.exp(scores - top).astype(bf16)]
            for i, t in enumerate(keys):
                scores = upcoming
                if i + 1 < len(keys):
                    upcoming = head_scores(qs[v], kvs[keys[i + 1]], h)
                elif n + 1 < len(groups):
                    nv, nh = groups[n + 1]
                    following = head_scores(qs[nv], kvs[nv], nh)
                weights.append(jnp.exp(scores - (top + far[v, t])).astype(bf16))
            values = jnp.concatenate([head_values(kvs[t], h) for t in [v] + keys], axis=1)
            acc[v, h * tall : (h + 1) * tall, :] = dot(values, jnp.concatenate(weights, axis=0))

    pairs = local_views * (2 * window + 1) - window * (window + 1)
    return pl.pallas_call(
        body,
        in_specs=[SMEM_SPEC, SMEM_SPEC] + many(VMEM_SPEC, 2 * local_views),
        out_specs=[VMEM_SPEC, VMEM_SPEC],
        out_shape=[
            jax.ShapeDtypeStruct((local_views, heads * tall, tokens), f32),
            jax.ShapeDtypeStruct((local_views, heads, tokens), f32),
        ],
        name="local_attention",
        compiler_params=grant(12),
        cost_estimate=attention_cost(tokens, sub, pairs),
    )(
        meta,
        intersection,
        *[blocks[v][0] for v in range(local_views)],
        *[blocks[v][1] for v in range(local_views)],
    )


def finish_attention(meta, intersection, acc, stat, blocks, window, plan, remote):
    local_views, tall_all, tokens = acc.shape
    heads = stat.shape[1]
    tall = tall_all // heads
    sub = heads * HEAD_DIM
    views_total = intersection.shape[0]
    names = sorted(remote)
    count = len(plan)

    def body(meta_ref, inter_ref, acc_ref, stat_ref, *refs):
        qs, refs = refs[:count], refs[count:]
        kvs, refs = refs[:local_views], refs[local_views:]
        far_kvs = dict(zip(names, refs[: len(names)]))
        out, work, work_stat = refs[len(names) :]
        first = meta_ref[0] * local_views

        def global_view(source):
            at = first + source
            return jnp.where(at < 0, at + views_total, at) if source < 0 else at

        units = [
            (i, h, name, global_view(source), offset)
            for i, (_, sources) in enumerate(plan)
            for h in range(heads)
            for name, source, offset in sources
        ]
        upcoming = head_scores(qs[units[0][0]], far_kvs[units[0][2]], units[0][1])
        worst = jnp.zeros((1, tokens), f32)
        n = 0
        for i, (view, sources) in enumerate(plan):
            parts = []
            for h in range(heads):
                top = stat_ref[view, h : h + 1, :]
                weights = []
                for _ in sources:
                    scores = upcoming
                    far = far_if_absent(inter_ref, units[n][3], units[n][4])
                    n += 1
                    if n < len(units):
                        upcoming = head_scores(qs[units[n][0]], far_kvs[units[n][2]], units[n][1])
                    weights.append(jnp.exp(scores - (top + far)).astype(bf16))
                values = jnp.concatenate([head_values(far_kvs[s[0]], h) for s in sources], axis=1)
                sums = acc_ref[view, h * tall : (h + 1) * tall, :] + dot(
                    values, jnp.concatenate(weights, axis=0)
                )
                total = sums[HEAD_DIM : HEAD_DIM + 1, :]
                worst = jnp.maximum(worst, jnp.where(total < SAFE_TOTAL, 0.0, 1.0))
                parts.append(sums[:HEAD_DIM, :] * (1.0 / total))
            out[i] = jnp.transpose(jnp.concatenate(parts, axis=0)).astype(bf16)

        @pl.when(jnp.max(worst) > 0.0)
        def _():
            for i, (view, sources) in enumerate(plan):
                every = [(kvs[view], None, None)]
                for o in range(window):
                    if view + o + 1 < local_views:
                        every.append((kvs[view + o + 1], first + view, o))
                    if view - o - 1 >= 0:
                        every.append((kvs[view - o - 1], first + view - o - 1, o))
                for name, source, o in sources:
                    every.append((far_kvs[name], global_view(source), o))
                for e, (kv, at, o) in enumerate(every):
                    if e == 0:
                        exact_add(qs[i], kv, work, work_stat, heads, True)
                    else:

                        @pl.when(inter_ref[at, o] > 0)
                        def _(i=i, kv=kv):
                            exact_add(qs[i], kv, work, work_stat, heads, False)

                parts = []
                for h in range(heads):
                    total = work_stat[h, 1:2, :]
                    parts.append(work[h * HEAD_DIM : (h + 1) * HEAD_DIM, :] * (1.0 / total))
                out[i] = jnp.transpose(jnp.concatenate(parts, axis=0)).astype(bf16)

    pairs = sum(len(s) for _, s in plan)
    return pl.pallas_call(
        body,
        in_specs=[SMEM_SPEC, SMEM_SPEC]
        + many(VMEM_SPEC, 2 + count + local_views + len(names)),
        out_specs=VMEM_SPEC,
        out_shape=jax.ShapeDtypeStruct((count, tokens, sub), bf16),
        scratch_shapes=[
            pltpu.VMEM((sub, tokens), f32),
            pltpu.VMEM((heads, 8, tokens), f32),
        ],
        name="finish_attention",
        compiler_params=grant(12),
        cost_estimate=attention_cost(tokens, sub, pairs),
    )(
        meta,
        intersection,
        acc,
        stat,
        *[blocks[v][0] for v, _ in plan],
        *[blocks[v][1] for v in range(local_views)],
        *[remote[name] for name in names],
    )


def exact_add(q_ref, kv_ref, work, work_stat, heads, start):
    per = LANES // HEAD_DIM

    def one_head(h, _):
        base = pl.multiple_of((h // per) * LANES, LANES)
        queries = q_ref[pl.ds(base, LANES), :]
        owner = lax.broadcasted_iota(jnp.int32, queries.shape, 0) // HEAD_DIM
        queries = jnp.where(owner == h % per, queries.astype(f32), 0.0).astype(bf16)
        scores = dot(kv_ref[0, :, pl.ds(base, LANES)], queries)
        top = jnp.max(scores, axis=0, keepdims=True)
        rows = pl.ds(pl.multiple_of(h * HEAD_DIM, HEAD_DIM), HEAD_DIM)
        values = kv_ref[1, rows, :]
        if not start:
            old = work_stat[h, 0:1, :]
            top = jnp.maximum(old, top)
        weights = jnp.exp(scores - top)
        total = jnp.sum(weights, axis=0, keepdims=True)
        sums = dot(values, weights.astype(bf16))
        if not start:
            fade = jnp.exp(old - top)
            total = total + work_stat[h, 1:2, :] * fade
            sums = sums + work[rows, :] * fade
        work_stat[h, 0:1, :] = top
        work_stat[h, 1:2, :] = total
        work[rows, :] = sums
        return 0

    lax.fori_loop(0, heads, one_head, 0)


def project_out(meta, attended, weights, latents, views):
    count, tokens, sub = attended[0].shape
    groups = len(attended)

    def body(meta_ref, *refs):
        att, ws = refs[:groups], refs[groups : 2 * groups]
        lat_hbm, own, other, buffer, sems = refs[2 * groups :]
        columns = pl.ds(pl.multiple_of((meta_ref[1] // 2) * 2 * sub, 2 * sub), 2 * sub)
        copies = [
            pltpu.make_async_copy(lat_hbm.at[v, :, columns], buffer.at[i], sems.at[i])
            for i, v in enumerate(views)
        ]
        for copy in copies:
            copy.start()
        odd = meta_ref[1] % 2 == 1
        matrix = jnp.concatenate([w[...] for w in ws], axis=0)
        for i in range(count):
            rows = jnp.concatenate([a[i] for a in att], axis=1)
            total = dot(rows, matrix)
            copies[i].wait()
            layer = (buffer[i].astype(f32) + total).astype(bf16)
            low, high = layer[:, :sub], layer[:, sub:]
            own[i] = jnp.where(odd, high, low)
            other[i] = jnp.where(odd, low, high)

    return pl.pallas_call(
        body,
        in_specs=[SMEM_SPEC] + many(VMEM_SPEC, 2 * groups) + [ANY_SPEC],
        out_specs=[VMEM_SPEC, VMEM_SPEC],
        out_shape=[jax.ShapeDtypeStruct((count, tokens, sub), bf16)] * 2,
        scratch_shapes=[
            pltpu.VMEM((count, tokens, 2 * sub), bf16),
            pltpu.SemaphoreType.DMA((count,)),
        ],
        name="project_out",
        compiler_params=grant(12),
        cost_estimate=cost(
            groups * count * tokens * sub * 4 * sub,
            groups * (count * tokens * sub + 2 * sub * sub) * 2 + count * tokens * sub * 8,
        ),
    )(meta, *attended, *weights, latents)


def prepare_requests(block_rows, token_rows, peers, capacity):
    strips, lanes = block_rows.shape

    def body(block_ref, token_ref, wanted_ref, code_ref):
        before = (
            lax.broadcasted_iota(jnp.int32, (lanes, lanes), 0)
            < lax.broadcasted_iota(jnp.int32, (lanes, lanes), 1)
        ).astype(bf16)
        peer_ids = lax.broadcasted_iota(jnp.int32, (peers, lanes), 0)
        carry = jnp.zeros((peers, 1), f32)
        slots, lefts = [], []
        for i in range(strips):
            block = block_ref[i : i + 1, :]
            hit = (peer_ids == block).astype(f32)
            rank = dot(hit.astype(bf16), before) + carry
            carry = carry + jnp.sum(hit, axis=1, keepdims=True)
            slot = jnp.sum(rank * hit, axis=0, keepdims=True)
            slots.append(slot)
            code_ref[i : i + 1, :] = block * capacity + slot.astype(jnp.int32)
            token = token_ref[i : i + 1, :]
            coarse = (token // 32).astype(f32)
            fine = (token % 32).astype(f32)
            lefts.append(jnp.concatenate([hit * coarse, hit * fine], axis=0).astype(bf16))
        columns = jnp.transpose(jnp.concatenate(slots, axis=0))
        place = lax.broadcasted_iota(jnp.int32, (lanes, capacity), 1).astype(f32)
        total = jnp.zeros((2 * peers, capacity), f32)
        for i in range(strips):
            spot = (columns[:, i : i + 1] == place).astype(bf16)
            total = total + dot(lefts[i], spot)
        wanted_ref[...] = (total[:peers] * 32.0 + total[peers:]).astype(jnp.int32)

    return pl.pallas_call(
        body,
        in_specs=[VMEM_SPEC, VMEM_SPEC],
        out_specs=[VMEM_SPEC, VMEM_SPEC],
        out_shape=[
            jax.ShapeDtypeStruct((peers, capacity), jnp.int32),
            jax.ShapeDtypeStruct((strips, lanes), jnp.int32),
        ],
        name="prepare_requests",
        compiler_params=grant(8),
        cost_estimate=cost(2 * strips * lanes * lanes * capacity, 3 * strips * lanes * 4),
    )(block_rows, token_rows)


def picks(offsets, width):
    clamped = jnp.minimum(jnp.maximum(offsets, -1.0), float(width)).astype(bf16)
    place = lax.broadcasted_iota(jnp.int32, (offsets.shape[0], width), 1).astype(f32).astype(bf16)
    spread = jnp.broadcast_to(clamped, place.shape)
    return jnp.where(spread == place, jnp.ones_like(place), jnp.zeros_like(place))


def gather_rows(meta, wanted, pieces, place_of):
    peers, capacity = wanted.shape
    _, tokens, sub = pieces[0][0].shape
    local_views = len(place_of)
    rows = local_views * tokens
    flat = [p for pair in pieces for p in pair]

    def body(meta_ref, wanted_ref, *refs):
        ins = refs[: len(flat)]
        layer, outs = refs[len(flat)], refs[len(flat) + 1 :]
        end = jnp.logical_or(meta_ref[1] == 0, meta_ref[1] == meta_ref[2] - 1)
        for v, (c, i) in enumerate(place_of):
            layer[v * tokens : (v + 1) * tokens, :] = jnp.where(
                end, ins[2 * c + 1][i], ins[2 * c][i]
            )
        lines = [wanted_ref[pl.ds(lax.bitwise_xor(meta_ref[0], m), 1), :] for m in range(peers)]
        columns = jnp.transpose(jnp.concatenate(lines, axis=0).astype(f32))
        for mask in range(peers):
            column = columns[:, mask : mask + 1]
            pick = jnp.concatenate(
                [picks(column - float(v * tokens), tokens) for v in range(local_views)], axis=1
            )
            outs[mask][...] = dot(pick, layer[...]).astype(bf16)

    return pl.pallas_call(
        body,
        in_specs=[SMEM_SPEC] + many(VMEM_SPEC, 1 + len(flat)),
        out_specs=many(VMEM_SPEC, 1 + peers),
        out_shape=[jax.ShapeDtypeStruct((rows, sub), bf16)]
        + [jax.ShapeDtypeStruct((capacity, sub), bf16)] * peers,
        name="gather_rows",
        compiler_params=grant(12),
        cost_estimate=cost(2 * peers * capacity * rows * sub, 2 * (rows + peers * capacity) * sub * 2),
    )(meta, wanted, *flat)


def finish_rows(meta, code, confidence, layer, replies, tokens):
    rows, sub = layer.shape
    peers = len(replies)
    capacity = replies[0].shape[0]
    strips, lanes = code.shape
    blocks = rows // tokens
    per = tokens // lanes

    def body(meta_ref, code_ref, conf_ref, layer_ref, *refs):
        reps, (out_hbm, buffer, sems) = refs[:peers], refs[peers:]
        codes = jnp.transpose(code_ref[...].astype(f32))
        confs = jnp.transpose(conf_ref[...]) * coupling
        copies = []
        for g in range(blocks):

            def column(turned):
                return jnp.concatenate(
                    [turned[:, g * per + j : g * per + j + 1] for j in range(per)], axis=0
                )

            code_column = column(codes)
            pick = jnp.concatenate(
                [
                    picks(
                        code_column
                        - (lax.bitwise_xor(meta_ref[0], mask) * capacity).astype(f32),
                        capacity,
                    )
                    for mask in range(peers)
                ],
                axis=1,
            )
            fetched = dot(pick, jnp.concatenate([r[...] for r in reps], axis=0))
            wide = layer_ref[g * tokens : (g + 1) * tokens, :].astype(f32)
            buffer[g] = wide + column(confs) * (fetched - wide)
            copies.append(
                pltpu.make_async_copy(
                    buffer.at[g], out_hbm.at[pl.ds(g * tokens, tokens), :], sems.at[g]
                )
            )
            copies[-1].start()
        for copy in copies:
            copy.wait()

    return pl.pallas_call(
        body,
        in_specs=[SMEM_SPEC] + many(VMEM_SPEC, 3 + peers),
        out_specs=ANY_SPEC,
        out_shape=jax.ShapeDtypeStruct((rows, sub), f32),
        scratch_shapes=[
            pltpu.VMEM((blocks, tokens, sub), f32),
            pltpu.SemaphoreType.DMA((blocks,)),
        ],
        name="finish_rows",
        compiler_params=grant(12),
        cost_estimate=cost(2 * peers * capacity * rows * sub, rows * sub * 6 + peers * capacity * sub * 2),
    )(meta, code, confidence, layer, *replies)


def per_device(latents, norm_gain, w_qkv, w_out, intersection, match_block, match_row, confidence):
    local_views, tokens, width = latents.shape
    window = intersection.shape[1]
    sub = w_qkv.shape[2]
    peers = lax.axis_size("views")
    ends = lax.axis_size("heads")
    rows = local_views * tokens
    capacity = 2 * rows // peers
    assert local_views == 4 and window == 2 and ends == 4 and tokens == sub
    view_at, head_at = lax.axis_index("views"), lax.axis_index("heads")
    spot = jnp.arange(4, dtype=jnp.int32)
    meta = jnp.where(spot == 0, view_at, jnp.where(spot == 1, head_at, ends)).astype(jnp.int32)

    def along(x, by):
        return lax.ppermute(x, "views", [(i, (i + by) % peers) for i in range(peers)])

    def across(x, pairs):
        return lax.ppermute(x, "heads", pairs)

    beside, middle, beyond, back = (
        [(0, 1), (3, 2)],
        [(1, 2), (2, 1)],
        [(0, 2), (3, 1)],
        [(1, 0), (2, 3)],
    )
    gain = norm_gain.reshape(1, width)
    blocks = project_views(latents, gain, w_qkv, (0, local_views - 1))
    next_first = along(blocks[0][1], -1)
    prev_last = along(blocks[3][1], 1)
    blocks.update(project_views(latents, gain, w_qkv, (1, 2)))
    next_second = along(blocks[1][1], -1)
    prev_second = along(blocks[2][1], 1)

    half = 2 * sub
    low_end = head_at // 2
    own_half = lax.dynamic_slice_in_dim(w_out, low_end * half, half, 1)
    other_half = lax.dynamic_slice_in_dim(w_out, (1 - low_end) * half, half, 1)
    weights = [
        own_half,
        across(own_half, beside),
        across(other_half, middle),
        across(other_half, beyond),
    ]

    strips = rows // LANES
    wanted, code = prepare_requests(
        match_block.reshape(strips, LANES), match_row.reshape(strips, LANES), peers, capacity
    )
    wanted = lax.all_to_all(wanted, "views", split_axis=0, concat_axis=0, tiled=True)

    acc, stat = local_attention(meta, intersection, blocks, local_views, window)
    finish = functools.partial(finish_attention, meta, intersection, acc, stat, blocks, window)
    inner = finish(
        [(1, [("prev_last", -1, 1)]), (2, [("next_first", 2, 1)])],
        dict(prev_last=prev_last, next_first=next_first),
    )
    outer = finish(
        [
            (0, [("prev_last", -1, 0), ("prev_second", -2, 1)]),
            (3, [("next_first", 3, 0), ("next_second", 3, 1)]),
        ],
        dict(
            prev_last=prev_last,
            next_first=next_first,
            prev_second=prev_second,
            next_second=next_second,
        ),
    )
    pieces = []
    for chunk, views in ((inner, (1, 2)), (outer, (0, 3))):
        attended = [chunk, across(chunk, beside), across(chunk, middle), across(chunk, beyond)]
        if not pieces:
            attended[0], wanted = lax.optimization_barrier((attended[0], wanted))
        own, other = project_out(meta, attended, weights, latents, views)
        pieces.append((own, across(other, back)))

    place_of = [(1, 0), (0, 0), (0, 1), (1, 1)]
    layer, *outgoing = gather_rows(meta, wanted, pieces, place_of)
    replies = [outgoing[0]]
    for mask in range(1, peers):
        replies.append(lax.ppermute(outgoing[mask], "views", [(i, i ^ mask) for i in range(peers)]))
    refined = finish_rows(
        meta, code, confidence.reshape(strips, LANES), layer, replies, tokens
    )
    return refined.reshape(local_views, tokens, sub)


def solution(mesh):
    in_specs = (
        P("views", None, None),
        P(),
        P(None, None, "heads"),
        P("heads", None),
        P(),
        P("views", None),
        P("views"),
        P("views"),
    )
    out_specs = P("views", None, "heads")
    return jax.shard_map(
        per_device, mesh=mesh, in_specs=in_specs, out_specs=out_specs, check_vma=False
    )
```

```python
import jax
import jax.numpy as jnp
from jax import lax
from jax.experimental import pallas as pl
from jax.experimental.pallas import tpu as pltpu
from jax.sharding import PartitionSpec as P


HEAD_DIM = 64
LANES = 128

coupling = 0.5
epsilon = 1e-06

bf16 = jnp.bfloat16
f32 = jnp.float32


def cost(flops, bytes_accessed, transcendentals=0):
    return pl.CostEstimate(
        flops=int(flops), bytes_accessed=int(bytes_accessed), transcendentals=int(transcendentals)
    )


def dot(a, b):
    return jnp.dot(a, b, preferred_element_type=f32)


VMEM_SPEC = pl.BlockSpec(memory_space=pltpu.VMEM)
SMEM_SPEC = pl.BlockSpec(memory_space=pltpu.SMEM)
ANY_SPEC = pl.BlockSpec(memory_space=pl.ANY)


def grant(mib):
    return pltpu.CompilerParams(vmem_limit_bytes=mib << 20)


def many(spec, count):
    return [spec] * count


def project_views(meta, latents, gain, w_qkv, which, w_out=None):
    _, tokens, width = latents.shape
    sub = w_qkv.shape[2]
    count = len(which)
    scale = HEAD_DIM ** (-0.5)
    order = (2, 0, 1)

    extra = 0 if w_out is None else 1
    strip = sub // 2

    def body(meta_ref, lat_hbm, gain_hbm, w_hbm, *refs):
        outs, (buffer, gains, ws, sems) = refs[extra : 2 * count + extra], refs[-4:]
        splits = []
        if extra:
            own, pair, other = refs[2 * count + 1 : 2 * count + 4]
            side = meta_ref[1] // 2
            near = pl.ds(pl.multiple_of(side * 2 * sub, 2 * sub), 2 * sub)
            away = pl.ds(pl.multiple_of((1 - side) * 2 * sub, 2 * sub), 2 * sub)
            mine = pl.ds(pl.multiple_of((meta_ref[0] % 2) * strip, strip), strip)
            for i, (source, target) in enumerate(
                (
                    (refs[0].at[:, near], own),
                    (refs[0].at[mine, near], pair.at[0]),
                    (refs[0].at[mine, away], pair.at[1]),
                    (refs[0].at[mine, away], other),
                )
            ):
                splits.append(pltpu.make_async_copy(source, target, sems.at[count + 4 + i]))
        copies = [
            pltpu.make_async_copy(lat_hbm.at[v], buffer.at[i], sems.at[i])
            for i, v in enumerate(which)
        ]
        copies.insert(1, pltpu.make_async_copy(gain_hbm, gains, sems.at[count]))
        w_copies = {
            part: pltpu.make_async_copy(w_hbm.at[part], ws.at[part], sems.at[count + 1 + part])
            for part in order
        }
        copies[0].start()
        copies[1].start()
        for part in order:
            w_copies[part].start()
        for copy in copies[2:] + splits:
            copy.start()
        for i in range(count):
            copies[i if i == 0 else i + 1].wait()
            if i == 0:
                copies[1].wait()
            wide = buffer[i].astype(f32)
            mean_square = jnp.mean(wide * wide, axis=-1, keepdims=True)
            normed = (wide * lax.rsqrt(mean_square + epsilon) * gains[...]).astype(bf16)
            if i == 0:
                w_copies[2].wait()
            values = dot(normed, ws[2])
            if i == 0:
                w_copies[0].wait()
            queries = dot(normed, ws[0])
            if i == 0:
                w_copies[1].wait()
            outs[2 * i + 1][0] = dot(normed, ws[1]).astype(bf16)
            outs[2 * i + 1][1] = jnp.transpose(values).astype(bf16)
            outs[2 * i][...] = jnp.transpose(queries).astype(bf16) * jnp.asarray(scale, bf16)
        for copy in splits:
            copy.wait()

    out_shape = []
    for _ in which:
        out_shape += [
            jax.ShapeDtypeStruct((sub, tokens), bf16),
            jax.ShapeDtypeStruct((2, tokens, sub), bf16),
        ]
    if extra:
        out_shape += [
            jax.ShapeDtypeStruct((sub, 2 * sub), bf16),
            jax.ShapeDtypeStruct((2, strip, 2 * sub), bf16),
            jax.ShapeDtypeStruct((strip, 2 * sub), bf16),
        ]
    outs = pl.pallas_call(
        body,
        in_specs=[SMEM_SPEC] + many(ANY_SPEC, 3 + extra),
        out_specs=many(VMEM_SPEC, len(out_shape)),
        out_shape=out_shape,
        scratch_shapes=[
            pltpu.VMEM((count, tokens, width), bf16),
            pltpu.VMEM((1, width), f32),
            pltpu.VMEM((3, width, sub), bf16),
            pltpu.SemaphoreType.DMA((count + 8,)),
        ],
        name="project_views",
        compiler_params=grant(52),
        cost_estimate=cost(
            count * 6 * tokens * width * sub, count * tokens * (width + 3 * sub) * 2 + 6 * width * sub
        ),
    )(meta, latents, gain, w_qkv, *([w_out] if extra else []))
    return {v: (outs[2 * i], outs[2 * i + 1]) for i, v in enumerate(which)}, outs[2 * count :]


ONES = 16
SAFE_TOTAL = 1e30
FAR = 1e30


def head_scores(q_ref, kv_ref, h):
    per = LANES // HEAD_DIM
    j, slot = h // per, h % per
    own = q_ref[h * HEAD_DIM : (h + 1) * HEAD_DIM, :]
    zero = jnp.zeros_like(own)
    padded = jnp.concatenate([own if s == slot else zero for s in range(per)], axis=0)
    return dot(kv_ref[0, :, j * LANES : (j + 1) * LANES], padded)


def head_values(kv_ref, h):
    rows = kv_ref[1, h * HEAD_DIM : (h + 1) * HEAD_DIM, :]
    return jnp.concatenate([rows, jnp.ones((ONES, rows.shape[1]), bf16)], axis=0)


def attention_cost(tokens, sub, pairs):
    heads = sub // HEAD_DIM
    return cost(
        pairs * heads * tokens * tokens * 4 * LANES,
        pairs * tokens * sub * 8,
        pairs * heads * tokens * tokens,
    )


def far_if_absent(inter_ref, at, offset):
    return jnp.where(inter_ref[offset, at] > 0, 0.0, FAR).astype(f32)


def sources_of(view, local_views, window):
    found = []
    for o in range(window):
        if view + o + 1 < local_views:
            found.append((view + o + 1, view, o))
        if view - o - 1 >= 0:
            found.append((view - o - 1, view - o - 1, o))
    return found


def attend(
    meta, inter, queries, blocks, remote, plan, window, earlier=None, last=True, merged=False
):
    local_views = len(blocks)
    sub, tokens = queries[0].shape
    heads = sub // HEAD_DIM
    tall = HEAD_DIM + ONES
    views_total = inter.shape[1]
    names = sorted(remote)
    count = len(plan)
    held = 0 if earlier is None else 2

    def body(meta_ref, inter_ref, *refs):
        before, refs = refs[:held], refs[held:]
        qs, refs = refs[:count], refs[count:]
        kvs, refs = refs[:local_views], refs[local_views:]
        far_kvs, refs = dict(zip(names, refs[: len(names)])), refs[len(names) :]
        first = meta_ref[0] * local_views

        def global_view(source):
            at = first + source
            return jnp.where(at < 0, at + views_total, at) if source < 0 else at

        def keys_of(i):
            view, sources = plan[i]
            keys = [] if held else [(kvs[view], None, None)]
            if not held:
                keys += [(kvs[t], source, o) for t, source, o in sources_of(view, local_views, window)]
            return keys + [(far_kvs[name], source, o) for name, source, o in sources]

        if last:
            outs = [refs[0].at[i] for i in range(count)] if merged else refs[:count]
        units = [(i, h, k) for i in range(count) for h in range(heads) for k in keys_of(i)]
        far = {}
        for _, _, (_, source, o) in units:
            if source is not None and (source, o) not in far:
                far[source, o] = far_if_absent(inter_ref, global_view(source), o)
        upcoming = head_scores(qs[units[0][0]], units[0][2][0], units[0][1])
        worst = jnp.zeros((1, tokens), f32)
        n = 0
        for i, (view, _) in enumerate(plan):
            parts = []
            for h in range(heads):
                keys = keys_of(i)
                weights = []
                top = before[1][i, h : h + 1, :] if held else None
                for _, source, o in keys:
                    scores = upcoming
                    n += 1
                    if n < len(units):
                        ni, nh, (nk, _, _) = units[n]
                        upcoming = head_scores(qs[ni], nk, nh)
                    if source is None:
                        top = jnp.max(scores, axis=0, keepdims=True)
                        shift = top
                    else:
                        shift = top + far[source, o]
                    weights.append(jnp.exp(scores - shift).astype(bf16))
                values = jnp.concatenate([head_values(k[0], h) for k in keys], axis=1)
                sums = dot(values, jnp.concatenate(weights, axis=0))
                if held:
                    sums = sums + before[0][i, h * tall : (h + 1) * tall, :]
                if not last:
                    refs[0][i, h * tall : (h + 1) * tall, :] = sums
                    refs[1][i, h : h + 1, :] = top
                    continue
                total = sums[HEAD_DIM : HEAD_DIM + 1, :]
                worst = jnp.maximum(worst, jnp.where(total < SAFE_TOTAL, 0.0, 1.0))
                parts.append(sums[:HEAD_DIM, :] * (1.0 / total))
            if last:
                outs[i][...] = jnp.transpose(jnp.concatenate(parts, axis=0)).astype(bf16)
        if not last:
            return
        work, work_stat = refs[-2:]

        @pl.when(jnp.max(worst) > 0.0)
        def _():
            for i, (view, sources) in enumerate(plan):
                exact_add(qs[i], kvs[view], work, work_stat, heads, True)
                every = [(kvs[t], s, o) for t, s, o in sources_of(view, local_views, window)]
                every += [(far_kvs[name], s, o) for name, s, o in sources]
                for kv, source, o in every:

                    @pl.when(inter_ref[o, global_view(source)] > 0)
                    def _(i=i, kv=kv):
                        exact_add(qs[i], kv, work, work_stat, heads, False)

                parts = []
                for h in range(heads):
                    total = work_stat[h, 1:2, :]
                    parts.append(work[h * HEAD_DIM : (h + 1) * HEAD_DIM, :] * (1.0 / total))
                outs[i][...] = jnp.transpose(jnp.concatenate(parts, axis=0)).astype(bf16)

    if last:
        out_shape = [jax.ShapeDtypeStruct((tokens, sub), bf16)] * count
        if merged:
            out_shape = [jax.ShapeDtypeStruct((count, tokens, sub), bf16)]
        scratch = [pltpu.VMEM((sub, tokens), f32), pltpu.VMEM((heads, 8, tokens), f32)]
    else:
        out_shape = [
            jax.ShapeDtypeStruct((count, heads * tall, tokens), f32),
            jax.ShapeDtypeStruct((count, heads, tokens), f32),
        ]
        scratch = []
    pairs = sum(len(s) for _, s in plan)
    if not held:
        pairs += sum(1 + len(sources_of(v, local_views, window)) for v, _ in plan)
    return pl.pallas_call(
        body,
        in_specs=[SMEM_SPEC, SMEM_SPEC]
        + many(VMEM_SPEC, held + count + local_views + len(names)),
        out_specs=many(VMEM_SPEC, len(out_shape)),
        out_shape=out_shape,
        scratch_shapes=scratch,
        name="attend" if last else "attend_local",
        compiler_params=grant(12),
        cost_estimate=attention_cost(tokens, sub, pairs),
    )(
        meta,
        inter,
        *(earlier or ()),
        *queries,
        *[blocks[v] for v in range(local_views)],
        *[remote[name] for name in names],
    )


def exact_add(q_ref, kv_ref, work, work_stat, heads, start):
    per = LANES // HEAD_DIM

    def one_head(h, _):
        base = pl.multiple_of((h // per) * LANES, LANES)
        queries = q_ref[pl.ds(base, LANES), :]
        owner = lax.broadcasted_iota(jnp.int32, queries.shape, 0) // HEAD_DIM
        queries = jnp.where(owner == h % per, queries.astype(f32), 0.0).astype(bf16)
        scores = dot(kv_ref[0, :, pl.ds(base, LANES)], queries)
        top = jnp.max(scores, axis=0, keepdims=True)
        rows = pl.ds(pl.multiple_of(h * HEAD_DIM, HEAD_DIM), HEAD_DIM)
        values = kv_ref[1, rows, :]
        if not start:
            old = work_stat[h, 0:1, :]
            top = jnp.maximum(old, top)
        weights = jnp.exp(scores - top)
        total = jnp.sum(weights, axis=0, keepdims=True)
        sums = dot(values, weights.astype(bf16))
        if not start:
            fade = jnp.exp(old - top)
            total = total + work_stat[h, 1:2, :] * fade
            sums = sums + work[rows, :] * fade
        work_stat[h, 0:1, :] = top
        work_stat[h, 1:2, :] = total
        work[rows, :] = sums
        return 0

    lax.fori_loop(0, heads, one_head, 0)


def project_out(meta, attended, weights, latents, views):
    count = len(attended)
    groups = len(attended[0])
    arrays = []
    for row in attended:
        for array, _ in row:
            if not any(array is a for a in arrays):
                arrays.append(array)
    spots = [
        [([a is array for a in arrays].index(True), index) for array, index in row] for row in attended
    ]
    tokens, sub = arrays[0].shape[-2:]

    def pick(refs, spot):
        ref, index = refs[spot[0]], spot[1]
        return ref[...] if index is None else ref[index]

    def body(meta_ref, *refs):
        att, refs = refs[: len(arrays)], refs[len(arrays) :]
        ws, refs = refs[: len(weights)], refs[len(weights) :]
        lat_hbm, refs = refs[0], refs[1:]
        owns, others = refs[:count], refs[count : 2 * count]
        buffer, sems = refs[2 * count :]
        columns = pl.ds(pl.multiple_of((meta_ref[1] // 2) * 2 * sub, 2 * sub), 2 * sub)
        copies = [
            pltpu.make_async_copy(lat_hbm.at[v, :, columns], buffer.at[i], sems.at[i])
            for i, v in enumerate(views)
        ]
        for copy in copies:
            copy.start()
        odd = meta_ref[1] % 2 == 1
        second = meta_ref[0] % 2 == 1
        rows = [ws[0][...]]
        for mine, theirs in zip(ws[1 : 1 + groups - 1], ws[groups:]):
            mine, theirs = mine[...], theirs[...]
            if len(mine.shape) == 3:
                mine, theirs = mine[0], theirs[0]
            rows.append(jnp.where(second, theirs, mine))
            rows.append(jnp.where(second, mine, theirs))
        matrix = jnp.concatenate(rows, axis=0)
        for i in range(count):
            total = dot(jnp.concatenate([pick(att, spot) for spot in spots[i]], axis=1), matrix)
            copies[i].wait()
            layer = (buffer[i].astype(f32) + total).astype(bf16)
            low, high = layer[:, :sub], layer[:, sub:]
            owns[i][...] = jnp.where(odd, high, low)
            others[i][...] = jnp.where(odd, low, high)

    outs = pl.pallas_call(
        body,
        in_specs=[SMEM_SPEC]
        + many(VMEM_SPEC, len(arrays) + len(weights))
        + [ANY_SPEC],
        out_specs=many(VMEM_SPEC, 2 * count),
        out_shape=[jax.ShapeDtypeStruct((tokens, sub), bf16)] * (2 * count),
        scratch_shapes=[
            pltpu.VMEM((count, tokens, 2 * sub), bf16),
            pltpu.SemaphoreType.DMA((count,)),
        ],
        name="project_out",
        compiler_params=grant(12),
        cost_estimate=cost(
            groups * count * tokens * sub * 4 * sub,
            groups * (count * tokens * sub + 2 * sub * sub) * 2 + count * tokens * sub * 8,
        ),
    )(meta, *arrays, *weights, latents)
    return outs[:count], outs[count:]


def prepare_requests(block_rows, token_rows, peers, capacity):
    strips, lanes = block_rows.shape

    def body(block_ref, token_ref, wanted_ref, code_ref):
        before = (
            lax.broadcasted_iota(jnp.int32, (lanes, lanes), 0)
            < lax.broadcasted_iota(jnp.int32, (lanes, lanes), 1)
        ).astype(bf16)
        peer_ids = lax.broadcasted_iota(jnp.int32, (peers, lanes), 0)
        carry = jnp.zeros((peers, 1), f32)
        slots, lefts = [], []
        for i in range(strips):
            block = block_ref[i : i + 1, :]
            hit = (peer_ids == block).astype(f32)
            rank = dot(hit.astype(bf16), before) + carry
            carry = carry + jnp.sum(hit, axis=1, keepdims=True)
            slot = jnp.sum(rank * hit, axis=0, keepdims=True)
            slots.append(slot)
            code_ref[i : i + 1, :] = block * capacity + slot.astype(jnp.int32)
            token = token_ref[i : i + 1, :]
            coarse = (token // 32).astype(f32)
            fine = (token % 32).astype(f32)
            lefts.append(jnp.concatenate([hit * coarse, hit * fine], axis=0).astype(bf16))
        columns = jnp.transpose(jnp.concatenate(slots, axis=0))
        place = lax.broadcasted_iota(jnp.int32, (lanes, capacity), 1).astype(f32)
        total = jnp.zeros((2 * peers, capacity), f32)
        for i in range(strips):
            spot = (columns[:, i : i + 1] == place).astype(bf16)
            total = total + dot(lefts[i], spot)
        wanted_ref[...] = (total[:peers] * 32.0 + total[peers:]).astype(jnp.int32)

    return pl.pallas_call(
        body,
        in_specs=[VMEM_SPEC, VMEM_SPEC],
        out_specs=[VMEM_SPEC, VMEM_SPEC],
        out_shape=[
            jax.ShapeDtypeStruct((peers, capacity), jnp.int32),
            jax.ShapeDtypeStruct((strips, lanes), jnp.int32),
        ],
        name="prepare_requests",
        compiler_params=grant(8),
        cost_estimate=cost(2 * strips * lanes * lanes * capacity, 3 * strips * lanes * 4),
    )(block_rows, token_rows)


def picks(offsets, width):
    clamped = jnp.minimum(jnp.maximum(offsets, -1.0), float(width)).astype(bf16)
    place = lax.broadcasted_iota(jnp.int32, (offsets.shape[0], width), 1).astype(f32).astype(bf16)
    spread = jnp.broadcast_to(clamped, place.shape)
    return jnp.where(spread == place, jnp.ones_like(place), jnp.zeros_like(place))


def gather_rows(meta, wanted, pieces):
    peers, capacity = wanted.shape
    tokens, sub = pieces[0][0].shape
    local_views = len(pieces)
    rows = local_views * tokens
    flat = [p for pair in pieces for p in pair]

    def body(meta_ref, wanted_ref, *refs):
        ins = refs[: len(flat)]
        layer, outs = refs[len(flat)], refs[len(flat) + 1 :]
        end = jnp.logical_or(meta_ref[1] == 0, meta_ref[1] == meta_ref[2] - 1)
        for v in range(local_views):
            layer[v * tokens : (v + 1) * tokens, :] = jnp.where(
                end, ins[2 * v + 1][...], ins[2 * v][...]
            )
        lines = [wanted_ref[pl.ds(lax.bitwise_xor(meta_ref[0], m), 1), :] for m in range(peers)]
        columns = jnp.transpose(jnp.concatenate(lines, axis=0).astype(f32))
        for mask in range(peers):
            column = columns[:, mask : mask + 1]
            pick = jnp.concatenate(
                [picks(column - float(v * tokens), tokens) for v in range(local_views)], axis=1
            )
            outs[mask][...] = dot(pick, layer[...]).astype(bf16)

    return pl.pallas_call(
        body,
        in_specs=[SMEM_SPEC] + many(VMEM_SPEC, 1 + len(flat)),
        out_specs=many(VMEM_SPEC, 1 + peers),
        out_shape=[jax.ShapeDtypeStruct((rows, sub), bf16)]
        + [jax.ShapeDtypeStruct((capacity, sub), bf16)] * peers,
        name="gather_rows",
        compiler_params=grant(12),
        cost_estimate=cost(2 * peers * capacity * rows * sub, 2 * (rows + peers * capacity) * sub * 2),
    )(meta, wanted, *flat)


def finish_rows(meta, code, confidence, layer, replies, tokens):
    rows, sub = layer.shape
    peers = len(replies)
    capacity = replies[0].shape[0]
    _, lanes = code.shape
    blocks = rows // tokens
    per = tokens // lanes

    def body(meta_ref, code_ref, conf_ref, layer_ref, *refs):
        reps, (out_hbm, buffer, sems) = refs[:peers], refs[peers:]
        codes = jnp.transpose(code_ref[...].astype(f32))
        confs = jnp.transpose(conf_ref[...]) * coupling
        copies = []
        for g in range(blocks):

            def column(turned):
                return jnp.concatenate(
                    [turned[:, g * per + j : g * per + j + 1] for j in range(per)], axis=0
                )

            code_column = column(codes)
            pick = jnp.concatenate(
                [
                    picks(
                        code_column
                        - (lax.bitwise_xor(meta_ref[0], mask) * capacity).astype(f32),
                        capacity,
                    )
                    for mask in range(peers)
                ],
                axis=1,
            )
            fetched = dot(pick, jnp.concatenate([r[...] for r in reps], axis=0))
            wide = layer_ref[g * tokens : (g + 1) * tokens, :].astype(f32)
            buffer[g] = wide + column(confs) * (fetched - wide)
            copies.append(
                pltpu.make_async_copy(
                    buffer.at[g], out_hbm.at[pl.ds(g * tokens, tokens), :], sems.at[g]
                )
            )
            copies[-1].start()
        for copy in copies:
            copy.wait()

    return pl.pallas_call(
        body,
        in_specs=[SMEM_SPEC] + many(VMEM_SPEC, 3 + peers),
        out_specs=ANY_SPEC,
        out_shape=jax.ShapeDtypeStruct((rows, sub), f32),
        scratch_shapes=[
            pltpu.VMEM((blocks, tokens, sub), f32),
            pltpu.SemaphoreType.DMA((blocks,)),
        ],
        name="finish_rows",
        compiler_params=grant(12),
        cost_estimate=cost(2 * peers * capacity * rows * sub, rows * sub * 6 + peers * capacity * sub * 2),
    )(meta, code, confidence, layer, *replies)


def per_device(latents, norm_gain, w_qkv, w_out, intersection, match_block, match_row, confidence):
    local_views, tokens, width = latents.shape
    window = intersection.shape[1]
    sub = w_qkv.shape[2]
    peers = lax.axis_size("views")
    ends = lax.axis_size("heads")
    rows = local_views * tokens
    capacity = 2 * rows // peers
    assert local_views == 4 and window == 2 and ends == 4 and tokens == sub
    view_at, head_at = lax.axis_index("views"), lax.axis_index("heads")
    spot = jnp.arange(4, dtype=jnp.int32)
    meta = jnp.where(spot == 0, view_at, jnp.where(spot == 1, head_at, ends)).astype(jnp.int32)

    def along(x, by):
        return lax.ppermute(x, "views", [(i, (i + by) % peers) for i in range(peers)])

    def partner(x, mask):
        return lax.ppermute(x, "views", [(i, i ^ mask) for i in range(peers)])

    def across(x, pairs):
        return lax.ppermute(x, "heads", pairs)

    def after(x, done):
        return lax.optimization_barrier((x, done))[0]

    beside, middle, back = [(0, 1), (3, 2)], [(1, 2), (2, 1)], [(1, 0), (2, 3)]
    gain = norm_gain.reshape(1, width)
    inter = intersection.T
    projected, _ = project_views(meta, latents, gain, w_qkv, (0, local_views - 1))
    next_first = along(projected[0][1], -1)
    prev_last = along(projected[3][1], 1)
    more, (own_half, w_pair, w_other) = project_views(
        meta, latents, gain, w_qkv, (1, 2), after(w_out, projected[0][0])
    )
    projected.update(more)
    queries = {v: projected[v][0] for v in range(local_views)}
    blocks = {v: projected[v][1] for v in range(local_views)}
    w_beside = across(w_pair, beside)
    w_middle = across(w_other, middle)

    inner_plan = [(1, [("prev_last", -1, 1)]), (2, [("next_first", 2, 1)])]
    inner_queries = [queries[1], queries[2]]
    local = attend(
        meta, inter, inner_queries, blocks, {}, [(v, []) for v, _ in inner_plan], window, last=False
    )
    next_second = along(after(blocks[1], local[0]), -1)
    prev_second = along(after(blocks[2], local[0]), 1)
    remote = dict(prev_last=prev_last, next_first=next_first)
    (inner,) = attend(
        meta,
        inter,
        inner_queries,
        blocks,
        remote,
        inner_plan,
        window,
        earlier=tuple(local),
        merged=True,
    )
    inner_beside = across(inner, beside)
    inner_middle = across(inner, middle)
    w_far = across(after(w_beside[1], inner), middle)

    remote.update(prev_second=prev_second, next_second=next_second)
    outer_plan = [
        (0, [("prev_last", -1, 0), ("prev_second", -2, 1)]),
        (3, [("next_first", 3, 0), ("next_second", 3, 1)]),
    ]
    outer_queries = [after(queries[0], inner), queries[3]]
    outer = attend(meta, inter, outer_queries, blocks, remote, outer_plan, window)
    strips = rows // LANES
    wanted, code = prepare_requests(
        after(match_block.reshape(strips, LANES), outer[0]),
        match_row.reshape(strips, LANES),
        peers,
        capacity,
    )
    wanted = lax.all_to_all(wanted, "views", split_axis=0, concat_axis=0, tiled=True)

    outer_beside, outer_middle, outer_far = [None] * 2, [None] * 2, [None] * 2
    for i in range(2):
        outer_beside[i] = across(outer[i], beside)
        outer_middle[i] = across(outer[i], middle)
    inner_far = across(inner_beside, middle)
    for i in range(2):
        outer_far[i] = across(outer_beside[i], middle)
    w_mine = [w_beside, w_middle, w_far]
    w_theirs = [partner(w, 1) for w in w_mine]
    weights = [own_half, *w_mine, *w_theirs]
    formed = {}
    for views, attended in (
        ((1, 2), [[(x, i) for x in (inner, inner_beside, inner_middle, inner_far)] for i in (0, 1)]),
        ((0,), [[(x[0], None) for x in (outer, outer_beside, outer_middle, outer_far)]]),
        ((3,), [[(x[1], None) for x in (outer, outer_beside, outer_middle, outer_far)]]),
    ):
        if not formed:
            weights[0] = after(weights[0], wanted)
        owns, others = project_out(meta, attended, weights, latents, views)
        returned = [across(x, back) for x in others]
        for v, own, got in zip(views, owns, returned):
            formed[v] = (own, got)

    pieces = [formed[v] for v in range(local_views)]
    layer, *outgoing = gather_rows(meta, wanted, pieces)
    replies = [outgoing[0]]
    for mask in range(1, peers):
        replies.append(partner(outgoing[mask], mask))
    refined = finish_rows(
        meta, code, confidence.reshape(strips, LANES), layer, replies, tokens
    )
    return refined.reshape(local_views, tokens, sub)


def solution(mesh):
    in_specs = (
        P("views", None, None),
        P(),
        P(None, None, "heads"),
        P("heads", None),
        P(),
        P("views", None),
        P("views"),
        P("views"),
    )
    out_specs = P("views", None, "heads")
    return jax.shard_map(
        per_device, mesh=mesh, in_specs=in_specs, out_specs=out_specs, check_vma=False
    )
```

```python
import jax
import jax.numpy as jnp
from jax import lax
from jax.experimental import pallas as pl
from jax.experimental.pallas import tpu as pltpu
from jax.sharding import PartitionSpec as P


HEAD_DIM = 64
LANES = 128
VIEW_ORDER = (1, 2, 0, 3)

coupling = 0.5
epsilon = 1e-06

bf16 = jnp.bfloat16
f32 = jnp.float32


def cost(flops, bytes_accessed, transcendentals=0):
    return pl.CostEstimate(
        flops=int(flops), bytes_accessed=int(bytes_accessed), transcendentals=int(transcendentals)
    )


def dot(a, b):
    return jnp.dot(a, b, preferred_element_type=f32)


VMEM_SPEC = pl.BlockSpec(memory_space=pltpu.VMEM)
SMEM_SPEC = pl.BlockSpec(memory_space=pltpu.SMEM)
ANY_SPEC = pl.BlockSpec(memory_space=pl.ANY)


def grant(mib):
    return pltpu.CompilerParams(vmem_limit_bytes=mib << 20)


def many(spec, count):
    return [spec] * count


def project_views(meta, latents, gain, w_qkv, which):
    _, tokens, width = latents.shape
    sub = w_qkv.shape[2]
    count = len(which)
    scale = HEAD_DIM ** (-0.5)
    order = (2, 0, 1)

    def body(meta_ref, lat_hbm, gain_hbm, w_hbm, *refs):
        outs, (halves, buffer, gains, ws, sems) = refs[: 2 * count], refs[2 * count :]
        here = pl.ds(pl.multiple_of((meta_ref[1] // 2) * (width // 2), width // 2), width // 2)
        kept = [
            pltpu.make_async_copy(buffer.at[i, :, here], halves.at[i], sems.at[count + 4 + i])
            for i in range(count)
        ]
        copies = [
            pltpu.make_async_copy(lat_hbm.at[v], buffer.at[i], sems.at[i])
            for i, v in enumerate(which)
        ]
        gain_copy = pltpu.make_async_copy(gain_hbm, gains, sems.at[count])
        w_copies = {
            part: pltpu.make_async_copy(w_hbm.at[part], ws.at[part], sems.at[count + 1 + part])
            for part in order
        }
        for copy in [copies[0], gain_copy] + [w_copies[p] for p in order] + copies[1:]:
            copy.start()
        for i in range(count):
            copies[i].wait()
            kept[i].start()
            if i == 0:
                gain_copy.wait()
            wide = buffer[i].astype(f32)
            mean_square = jnp.mean(wide * wide, axis=-1, keepdims=True)
            normed = (wide * lax.rsqrt(mean_square + epsilon) * gains[...]).astype(bf16)
            if i == 0:
                w_copies[2].wait()
            values = dot(normed, ws[2])
            if i == 0:
                w_copies[0].wait()
            queries = dot(normed, ws[0])
            if i == 0:
                w_copies[1].wait()
            outs[2 * i + 1][0] = dot(normed, ws[1]).astype(bf16)
            outs[2 * i + 1][1] = jnp.transpose(values).astype(bf16)
            outs[2 * i][...] = jnp.transpose(queries).astype(bf16) * jnp.asarray(scale, bf16)
        for copy in kept:
            copy.wait()

    out_shape = []
    for _ in which:
        out_shape += [
            jax.ShapeDtypeStruct((sub, tokens), bf16),
            jax.ShapeDtypeStruct((2, tokens, sub), bf16),
        ]
    out_shape.append(jax.ShapeDtypeStruct((count, tokens, width // 2), bf16))
    outs = pl.pallas_call(
        body,
        in_specs=[SMEM_SPEC] + many(ANY_SPEC, 3),
        out_specs=many(VMEM_SPEC, len(out_shape)),
        out_shape=out_shape,
        scratch_shapes=[
            pltpu.VMEM((count, tokens, width), bf16),
            pltpu.VMEM((1, width), f32),
            pltpu.VMEM((3, width, sub), bf16),
            pltpu.SemaphoreType.DMA((2 * count + 4,)),
        ],
        name="project_views",
        compiler_params=grant(50),
        cost_estimate=cost(
            count * 6 * tokens * width * sub, count * tokens * (width + 3 * sub) * 2 + 6 * width * sub
        ),
    )(meta, latents, gain, w_qkv)
    return {v: (outs[2 * i], outs[2 * i + 1]) for i, v in enumerate(which)}, outs[-1]


ONES = 16
SAFE_TOTAL = 1e30
FAR = 1e30


def head_scores(q_ref, kv_ref, h):
    per = LANES // HEAD_DIM
    j, slot = h // per, h % per
    own = q_ref[h * HEAD_DIM : (h + 1) * HEAD_DIM, :]
    zero = jnp.zeros_like(own)
    padded = jnp.concatenate([own if s == slot else zero for s in range(per)], axis=0)
    return dot(kv_ref[0, :, j * LANES : (j + 1) * LANES], padded)


def head_values(kv_ref, h):
    rows = kv_ref[1, h * HEAD_DIM : (h + 1) * HEAD_DIM, :]
    return jnp.concatenate([rows, jnp.ones((ONES, rows.shape[1]), bf16)], axis=0)


def attention_cost(tokens, sub, pairs):
    heads = sub // HEAD_DIM
    return cost(
        pairs * heads * tokens * tokens * 4 * LANES,
        pairs * tokens * sub * 8,
        pairs * heads * tokens * tokens,
    )


def far_if_absent(inter_ref, at, offset):
    return jnp.where(inter_ref[offset, at] > 0, 0.0, FAR).astype(f32)


def sources_of(view, local_views, window):
    found = []
    for o in range(window):
        if view + o + 1 < local_views:
            found.append((view + o + 1, view, o))
        if view - o - 1 >= 0:
            found.append((view - o - 1, view - o - 1, o))
    return found


def attend(
    meta, inter, queries, blocks, remote, plan, window, earlier=None, last=True, merged=False
):
    local_views = len(blocks)
    sub, tokens = queries[0].shape
    heads = sub // HEAD_DIM
    tall = HEAD_DIM + ONES
    views_total = inter.shape[1]
    names = sorted(remote)
    count = len(plan)
    held = 0 if earlier is None else 2

    def body(meta_ref, inter_ref, *refs):
        before, refs = refs[:held], refs[held:]
        qs, refs = refs[:count], refs[count:]
        kvs, refs = refs[:local_views], refs[local_views:]
        far_kvs, refs = dict(zip(names, refs[: len(names)])), refs[len(names) :]
        first = meta_ref[0] * local_views

        def global_view(source):
            at = first + source
            return jnp.where(at < 0, at + views_total, at) if source < 0 else at

        def keys_of(i):
            view, sources = plan[i]
            keys = [] if held else [(kvs[view], None, None)]
            if not held:
                keys += [(kvs[t], source, o) for t, source, o in sources_of(view, local_views, window)]
            return keys + [(far_kvs[name], source, o) for name, source, o in sources]

        if last:
            outs = [refs[0].at[i] for i in range(count)] if merged else refs[:count]
        units = [(i, h, k) for i in range(count) for h in range(heads) for k in keys_of(i)]
        far = {}
        for _, _, (_, source, o) in units:
            if source is not None and (source, o) not in far:
                far[source, o] = far_if_absent(inter_ref, global_view(source), o)
        upcoming = head_scores(qs[units[0][0]], units[0][2][0], units[0][1])
        worst = jnp.zeros((1, tokens), f32)
        n = 0
        for i, (view, _) in enumerate(plan):
            parts = []
            for h in range(heads):
                keys = keys_of(i)
                weights = []
                top = before[1][i, h : h + 1, :] if held else None
                for _, source, o in keys:
                    scores = upcoming
                    n += 1
                    if n < len(units):
                        ni, nh, (nk, _, _) = units[n]
                        upcoming = head_scores(qs[ni], nk, nh)
                    if source is None:
                        top = jnp.max(scores, axis=0, keepdims=True)
                        shift = top
                    else:
                        shift = top + far[source, o]
                    weights.append(jnp.exp(scores - shift).astype(bf16))
                values = jnp.concatenate([head_values(k[0], h) for k in keys], axis=1)
                sums = dot(values, jnp.concatenate(weights, axis=0))
                if held:
                    sums = sums + before[0][i, h * tall : (h + 1) * tall, :]
                if not last:
                    refs[0][i, h * tall : (h + 1) * tall, :] = sums
                    refs[1][i, h : h + 1, :] = top
                    continue
                total = sums[HEAD_DIM : HEAD_DIM + 1, :]
                worst = jnp.maximum(worst, jnp.where(total < SAFE_TOTAL, 0.0, 1.0))
                parts.append(sums[:HEAD_DIM, :] * (1.0 / total))
            if last:
                outs[i][...] = jnp.transpose(jnp.concatenate(parts, axis=0)).astype(bf16)
        if not last:
            return
        work, work_stat = refs[-2:]

        @pl.when(jnp.max(worst) > 0.0)
        def _():
            for i, (view, sources) in enumerate(plan):
                exact_add(qs[i], kvs[view], work, work_stat, heads, True)
                every = [(kvs[t], s, o) for t, s, o in sources_of(view, local_views, window)]
                every += [(far_kvs[name], s, o) for name, s, o in sources]
                for kv, source, o in every:

                    @pl.when(inter_ref[o, global_view(source)] > 0)
                    def _(i=i, kv=kv):
                        exact_add(qs[i], kv, work, work_stat, heads, False)

                parts = []
                for h in range(heads):
                    total = work_stat[h, 1:2, :]
                    parts.append(work[h * HEAD_DIM : (h + 1) * HEAD_DIM, :] * (1.0 / total))
                outs[i][...] = jnp.transpose(jnp.concatenate(parts, axis=0)).astype(bf16)

    if last:
        out_shape = [jax.ShapeDtypeStruct((tokens, sub), bf16)] * count
        if merged:
            out_shape = [jax.ShapeDtypeStruct((count, tokens, sub), bf16)]
        scratch = [pltpu.VMEM((sub, tokens), f32), pltpu.VMEM((heads, 8, tokens), f32)]
    else:
        out_shape = [
            jax.ShapeDtypeStruct((count, heads * tall, tokens), f32),
            jax.ShapeDtypeStruct((count, heads, tokens), f32),
        ]
        scratch = []
    pairs = sum(len(s) for _, s in plan)
    if not held:
        pairs += sum(1 + len(sources_of(v, local_views, window)) for v, _ in plan)
    return pl.pallas_call(
        body,
        in_specs=[SMEM_SPEC, SMEM_SPEC]
        + many(VMEM_SPEC, held + count + local_views + len(names)),
        out_specs=many(VMEM_SPEC, len(out_shape)),
        out_shape=out_shape,
        scratch_shapes=scratch,
        name="attend" if last else "attend_local",
        compiler_params=grant(12),
        cost_estimate=attention_cost(tokens, sub, pairs),
    )(
        meta,
        inter,
        *(earlier or ()),
        *queries,
        *[blocks[v] for v in range(local_views)],
        *[remote[name] for name in names],
    )


def exact_add(q_ref, kv_ref, work, work_stat, heads, start):
    per = LANES // HEAD_DIM

    def one_head(h, _):
        base = pl.multiple_of((h // per) * LANES, LANES)
        queries = q_ref[pl.ds(base, LANES), :]
        owner = lax.broadcasted_iota(jnp.int32, queries.shape, 0) // HEAD_DIM
        queries = jnp.where(owner == h % per, queries.astype(f32), 0.0).astype(bf16)
        scores = dot(kv_ref[0, :, pl.ds(base, LANES)], queries)
        top = jnp.max(scores, axis=0, keepdims=True)
        rows = pl.ds(pl.multiple_of(h * HEAD_DIM, HEAD_DIM), HEAD_DIM)
        values = kv_ref[1, rows, :]
        if not start:
            old = work_stat[h, 0:1, :]
            top = jnp.maximum(old, top)
        weights = jnp.exp(scores - top)
        total = jnp.sum(weights, axis=0, keepdims=True)
        sums = dot(values, weights.astype(bf16))
        if not start:
            fade = jnp.exp(old - top)
            total = total + work_stat[h, 1:2, :] * fade
            sums = sums + work[rows, :] * fade
        work_stat[h, 0:1, :] = top
        work_stat[h, 1:2, :] = total
        work[rows, :] = sums
        return 0

    lax.fori_loop(0, heads, one_head, 0)


def partial_out(meta, attended, near, w_own, w_near, halves, place):
    tokens, sub = attended.shape
    width = w_own.shape[1]
    half = width // 2

    def body(meta_ref, att, near_ref, own_ref, near_w_ref, halves_ref, keep, send):
        side = meta_ref[1] // 2
        here = pl.ds(pl.multiple_of(side * half, half), half)
        away = pl.ds(pl.multiple_of((1 - side) * half, half), half)
        rows = jnp.concatenate([att[...], near_ref[...]], axis=1)
        send[...] = dot(
            rows, jnp.concatenate([own_ref[:, away], near_w_ref[:, away]], axis=0)
        ).astype(bf16)
        total = dot(rows, jnp.concatenate([own_ref[:, here], near_w_ref[:, here]], axis=0))
        keep[...] = halves_ref[place].astype(f32) + total

    return pl.pallas_call(
        body,
        in_specs=[SMEM_SPEC] + many(VMEM_SPEC, 5),
        out_specs=many(VMEM_SPEC, 2),
        out_shape=[
            jax.ShapeDtypeStruct((tokens, half), f32),
            jax.ShapeDtypeStruct((tokens, half), bf16),
        ],
        name="partial_out",
        compiler_params=grant(12),
        cost_estimate=cost(4 * tokens * sub * width, 4 * sub * width + tokens * width * 6),
    )(meta, attended, near, w_own, w_near, halves)


def merge_out(meta, keep, got):
    tokens, half = keep.shape
    sub = half // 2

    def body(meta_ref, keep_ref, got_ref, own, other):
        layer = (keep_ref[...] + got_ref[...].astype(f32)).astype(bf16)
        low, high = layer[:, :sub], layer[:, sub:]
        odd = meta_ref[1] % 2 == 1
        own[...] = jnp.where(odd, high, low)
        other[...] = jnp.where(odd, low, high)

    return pl.pallas_call(
        body,
        in_specs=[SMEM_SPEC] + many(VMEM_SPEC, 2),
        out_specs=many(VMEM_SPEC, 2),
        out_shape=[jax.ShapeDtypeStruct((tokens, sub), bf16)] * 2,
        name="merge_out",
        compiler_params=grant(8),
        cost_estimate=cost(tokens * half * 2, tokens * half * 8),
    )(meta, keep, got)


def prepare_requests(block_rows, token_rows, peers, capacity):
    strips, lanes = block_rows.shape

    def body(block_ref, token_ref, wanted_ref, code_ref):
        before = (
            lax.broadcasted_iota(jnp.int32, (lanes, lanes), 0)
            < lax.broadcasted_iota(jnp.int32, (lanes, lanes), 1)
        ).astype(bf16)
        peer_ids = lax.broadcasted_iota(jnp.int32, (peers, lanes), 0)
        carry = jnp.zeros((peers, 1), f32)
        slots, lefts = [], []
        for i in range(strips):
            block = block_ref[i : i + 1, :]
            hit = (peer_ids == block).astype(f32)
            rank = dot(hit.astype(bf16), before) + carry
            carry = carry + jnp.sum(hit, axis=1, keepdims=True)
            slot = jnp.sum(rank * hit, axis=0, keepdims=True)
            slots.append(slot)
            code_ref[i : i + 1, :] = block * capacity + slot.astype(jnp.int32)
            token = token_ref[i : i + 1, :]
            coarse = (token // 32).astype(f32)
            fine = (token % 32).astype(f32)
            lefts.append(jnp.concatenate([hit * coarse, hit * fine], axis=0).astype(bf16))
        columns = jnp.transpose(jnp.concatenate(slots, axis=0))
        place = lax.broadcasted_iota(jnp.int32, (lanes, capacity), 1).astype(f32)
        total = jnp.zeros((2 * peers, capacity), f32)
        for i in range(strips):
            spot = (columns[:, i : i + 1] == place).astype(bf16)
            total = total + dot(lefts[i], spot)
        wanted_ref[...] = (total[:peers] * 32.0 + total[peers:]).astype(jnp.int32)

    return pl.pallas_call(
        body,
        in_specs=[VMEM_SPEC, VMEM_SPEC],
        out_specs=[VMEM_SPEC, VMEM_SPEC],
        out_shape=[
            jax.ShapeDtypeStruct((peers, capacity), jnp.int32),
            jax.ShapeDtypeStruct((strips, lanes), jnp.int32),
        ],
        name="prepare_requests",
        compiler_params=grant(8),
        cost_estimate=cost(2 * strips * lanes * lanes * capacity, 3 * strips * lanes * 4),
    )(block_rows, token_rows)


def picks(offsets, width):
    clamped = jnp.minimum(jnp.maximum(offsets, -1.0), float(width)).astype(bf16)
    place = lax.broadcasted_iota(jnp.int32, (offsets.shape[0], width), 1).astype(f32).astype(bf16)
    spread = jnp.broadcast_to(clamped, place.shape)
    return jnp.where(spread == place, jnp.ones_like(place), jnp.zeros_like(place))


def gather_rows(meta, wanted, pieces):
    peers, capacity = wanted.shape
    tokens, sub = pieces[0][0].shape
    local_views = len(pieces)
    rows = local_views * tokens
    flat = [p for pair in pieces for p in pair]

    def body(meta_ref, wanted_ref, *refs):
        ins = refs[: len(flat)]
        layer, outs = refs[len(flat)], refs[len(flat) + 1 :]
        end = jnp.logical_or(meta_ref[1] == 0, meta_ref[1] == meta_ref[2] - 1)
        for v in range(local_views):
            layer[v * tokens : (v + 1) * tokens, :] = jnp.where(
                end, ins[2 * v + 1][...], ins[2 * v][...]
            )
        lines = [wanted_ref[pl.ds(lax.bitwise_xor(meta_ref[0], m), 1), :] for m in range(peers)]
        columns = jnp.transpose(jnp.concatenate(lines, axis=0).astype(f32))
        for mask in range(peers):
            column = columns[:, mask : mask + 1]
            pick = jnp.concatenate(
                [picks(column - float(v * tokens), tokens) for v in range(local_views)], axis=1
            )
            outs[mask][...] = dot(pick, layer[...]).astype(bf16)

    return pl.pallas_call(
        body,
        in_specs=[SMEM_SPEC] + many(VMEM_SPEC, 1 + len(flat)),
        out_specs=many(VMEM_SPEC, 1 + peers),
        out_shape=[jax.ShapeDtypeStruct((rows, sub), bf16)]
        + [jax.ShapeDtypeStruct((capacity, sub), bf16)] * peers,
        name="gather_rows",
        compiler_params=grant(12),
        cost_estimate=cost(2 * peers * capacity * rows * sub, 2 * (rows + peers * capacity) * sub * 2),
    )(meta, wanted, *flat)


def finish_rows(meta, code, confidence, layer, replies, tokens):
    rows, sub = layer.shape
    peers = len(replies)
    capacity = replies[0].shape[0]
    _, lanes = code.shape
    blocks = rows // tokens
    per = tokens // lanes

    def body(meta_ref, code_ref, conf_ref, layer_ref, *refs):
        reps, (out_hbm, buffer, sems) = refs[:peers], refs[peers:]
        codes = jnp.transpose(code_ref[...].astype(f32))
        confs = jnp.transpose(conf_ref[...]) * coupling
        copies = []
        for g in range(blocks):

            def column(turned):
                return jnp.concatenate(
                    [turned[:, g * per + j : g * per + j + 1] for j in range(per)], axis=0
                )

            code_column = column(codes)
            pick = jnp.concatenate(
                [
                    picks(
                        code_column
                        - (lax.bitwise_xor(meta_ref[0], mask) * capacity).astype(f32),
                        capacity,
                    )
                    for mask in range(peers)
                ],
                axis=1,
            )
            fetched = dot(pick, jnp.concatenate([r[...] for r in reps], axis=0))
            wide = layer_ref[g * tokens : (g + 1) * tokens, :].astype(f32)
            buffer[g] = wide + column(confs) * (fetched - wide)
            copies.append(
                pltpu.make_async_copy(
                    buffer.at[g], out_hbm.at[pl.ds(g * tokens, tokens), :], sems.at[g]
                )
            )
            copies[-1].start()
        for copy in copies:
            copy.wait()

    return pl.pallas_call(
        body,
        in_specs=[SMEM_SPEC] + many(VMEM_SPEC, 3 + peers),
        out_specs=ANY_SPEC,
        out_shape=jax.ShapeDtypeStruct((rows, sub), f32),
        scratch_shapes=[
            pltpu.VMEM((blocks, tokens, sub), f32),
            pltpu.SemaphoreType.DMA((blocks,)),
        ],
        name="finish_rows",
        compiler_params=grant(12),
        cost_estimate=cost(2 * peers * capacity * rows * sub, rows * sub * 6 + peers * capacity * sub * 2),
    )(meta, code, confidence, layer, *replies)


def per_device(latents, norm_gain, w_qkv, w_out, intersection, match_block, match_row, confidence):
    local_views, tokens, width = latents.shape
    window = intersection.shape[1]
    sub = w_qkv.shape[2]
    peers = lax.axis_size("views")
    ends = lax.axis_size("heads")
    rows = local_views * tokens
    capacity = 2 * rows // peers
    assert local_views == 4 and window == 2 and ends == 4 and tokens == sub
    view_at, head_at = lax.axis_index("views"), lax.axis_index("heads")
    spot = jnp.arange(4, dtype=jnp.int32)
    meta = jnp.where(spot == 0, view_at, jnp.where(spot == 1, head_at, ends)).astype(jnp.int32)

    def along(x, by):
        return lax.ppermute(x, "views", [(i, (i + by) % peers) for i in range(peers)])

    def partner(x, mask):
        return lax.ppermute(x, "views", [(i, i ^ mask) for i in range(peers)])

    def across(x, pairs):
        return lax.ppermute(x, "heads", pairs)

    def after(x, done):
        return lax.optimization_barrier((x, done))[0]

    beside, middle, back = [(0, 1), (3, 2)], [(1, 2), (2, 1)], [(1, 0), (2, 3)]
    gain = norm_gain.reshape(1, width)
    inter = intersection.T
    loaded = (0, local_views - 1, 1, 2)
    projected, halves = project_views(meta, latents, gain, w_qkv, loaded)
    queries = {v: projected[v][0] for v in range(local_views)}
    blocks = {v: projected[v][1] for v in range(local_views)}
    next_first = along(blocks[0], -1)
    prev_last = along(blocks[3], 1)
    w_near = across(after(w_out, queries[1]), beside)

    inner_plan = [(1, [("prev_last", -1, 1)]), (2, [("next_first", 2, 1)])]
    inner_queries = [queries[1], queries[2]]
    local = attend(
        meta, inter, inner_queries, blocks, {}, [(v, []) for v, _ in inner_plan], window, last=False
    )
    next_second = along(after(blocks[1], local[0]), -1)
    prev_second = along(after(blocks[2], local[0]), 1)
    remote = dict(prev_last=prev_last, next_first=next_first)
    inner = attend(
        meta, inter, inner_queries, blocks, remote, inner_plan, window, earlier=tuple(local)
    )
    remote.update(prev_second=prev_second, next_second=next_second)
    outer_plan = [
        (0, [("prev_last", -1, 0), ("prev_second", -2, 1)]),
        (3, [("next_first", 3, 0), ("next_second", 3, 1)]),
    ]
    outer_queries = [after(queries[0], inner[0]), queries[3]]
    outer = attend(meta, inter, outer_queries, blocks, remote, outer_plan, window)
    attended = {1: inner[0], 2: inner[1], 0: outer[0], 3: outer[1]}
    strips = rows // LANES
    wanted, code = prepare_requests(
        after(match_block.reshape(strips, LANES), outer[0]),
        match_row.reshape(strips, LANES),
        peers,
        capacity,
    )
    keep, got, formed = {}, {}, {}
    for n, v in enumerate(VIEW_ORDER):
        near = across(attended[v], beside)
        if n == 2:
            wanted = lax.all_to_all(
                after(wanted, send), "views", split_axis=0, concat_axis=0, tiled=True
            )
            near = after(near, wanted)
        keep[v], send = partial_out(meta, attended[v], near, w_out, w_near, halves, loaded.index(v))
        got[v] = across(send, middle)
    for v in VIEW_ORDER:
        own, other = merge_out(meta, keep[v], got[v])
        formed[v] = (own, across(other, back))

    pieces = [formed[v] for v in range(local_views)]
    layer, *outgoing = gather_rows(meta, wanted, pieces)
    replies = [outgoing[0]]
    for mask in range(1, peers):
        replies.append(partner(outgoing[mask], mask))
    refined = finish_rows(
        meta, code, confidence.reshape(strips, LANES), layer, replies, tokens
    )
    return refined.reshape(local_views, tokens, sub)


def solution(mesh):
    in_specs = (
        P("views", None, None),
        P(),
        P(None, None, "heads"),
        P("heads", None),
        P(),
        P("views", None),
        P("views"),
        P("views"),
    )
    out_specs = P("views", None, "heads")
    return jax.shard_map(
        per_device, mesh=mesh, in_specs=in_specs, out_specs=out_specs, check_vma=False
    )
```

```python
import jax
import jax.numpy as jnp
from jax import lax
from jax.experimental import pallas as pl
from jax.experimental.pallas import tpu as pltpu
from jax.sharding import PartitionSpec as P


HEAD_DIM = 64
LANES = 128
VIEW_ORDER = (1, 2, 0, 3)

coupling = 0.5
epsilon = 1e-06

bf16 = jnp.bfloat16
f32 = jnp.float32


def cost(flops, bytes_accessed, transcendentals=0):
    return pl.CostEstimate(
        flops=int(flops), bytes_accessed=int(bytes_accessed), transcendentals=int(transcendentals)
    )


def dot(a, b):
    return jnp.dot(a, b, preferred_element_type=f32)


VMEM_SPEC = pl.BlockSpec(memory_space=pltpu.VMEM)
SMEM_SPEC = pl.BlockSpec(memory_space=pltpu.SMEM)
ANY_SPEC = pl.BlockSpec(memory_space=pl.ANY)


def grant(mib):
    return pltpu.CompilerParams(vmem_limit_bytes=mib << 20)


def many(spec, count):
    return [spec] * count


def project_views(meta, latents, gain, w_qkv, w_out, which):
    _, tokens, width = latents.shape
    sub = w_qkv.shape[2]
    count = len(which)
    scale = HEAD_DIM ** (-0.5)
    order = (2, 0, 1)

    strip = sub // 2

    def body(meta_ref, lat_hbm, gain_hbm, w_hbm, w_out_hbm, *refs):
        outs, (halves, w_half, buffer, gains, ws, sems) = refs[: 2 * count], refs[2 * count :]
        mine = pl.ds(pl.multiple_of((meta_ref[0] % 2) * strip, strip), strip)
        w_copy = pltpu.make_async_copy(w_out_hbm.at[mine], w_half, sems.at[2 * count + 4])
        here = pl.ds(pl.multiple_of((meta_ref[1] // 2) * (width // 2), width // 2), width // 2)
        kept = [
            pltpu.make_async_copy(buffer.at[i, :, here], halves.at[i], sems.at[count + 4 + i])
            for i in range(count)
        ]
        copies = [
            pltpu.make_async_copy(lat_hbm.at[v], buffer.at[i], sems.at[i])
            for i, v in enumerate(which)
        ]
        gain_copy = pltpu.make_async_copy(gain_hbm, gains, sems.at[count])
        w_copies = {
            part: pltpu.make_async_copy(w_hbm.at[part], ws.at[part], sems.at[count + 1 + part])
            for part in order
        }
        for copy in copies[:2] + [gain_copy] + [w_copies[p] for p in order] + copies[2:] + [w_copy]:
            copy.start()
        for i in range(0, count, 2):
            normed = []
            for j in (i, i + 1):
                copies[j].wait()
                kept[j].start()
                if j == 0:
                    gain_copy.wait()
                wide = buffer[j].astype(f32)
                mean_square = jnp.mean(wide * wide, axis=-1, keepdims=True)
                normed.append((wide * lax.rsqrt(mean_square + epsilon) * gains[...]).astype(bf16))
            normed = jnp.concatenate(normed, axis=0)
            if i == 0:
                w_copies[2].wait()
            values = dot(normed, ws[2])
            if i == 0:
                w_copies[0].wait()
            queries = dot(normed, ws[0])
            if i == 0:
                w_copies[1].wait()
            keys = dot(normed, ws[1]).astype(bf16)
            for j in (i, i + 1):
                at = slice((j - i) * tokens, (j - i + 1) * tokens)
                outs[2 * j + 1][1] = jnp.transpose(values[at]).astype(bf16)
                outs[2 * j][...] = jnp.transpose(queries[at]).astype(bf16) * jnp.asarray(scale, bf16)
                outs[2 * j + 1][0] = keys[at]
        w_copy.wait()
        for copy in kept:
            copy.wait()

    out_shape = []
    for _ in which:
        out_shape += [
            jax.ShapeDtypeStruct((sub, tokens), bf16),
            jax.ShapeDtypeStruct((2, tokens, sub), bf16),
        ]
    out_shape.append(jax.ShapeDtypeStruct((count, tokens, width // 2), bf16))
    out_shape.append(jax.ShapeDtypeStruct((strip, w_out.shape[1]), bf16))
    outs = pl.pallas_call(
        body,
        in_specs=[SMEM_SPEC] + many(ANY_SPEC, 4),
        out_specs=many(VMEM_SPEC, len(out_shape)),
        out_shape=out_shape,
        scratch_shapes=[
            pltpu.VMEM((count, tokens, width), bf16),
            pltpu.VMEM((1, width), f32),
            pltpu.VMEM((3, width, sub), bf16),
            pltpu.SemaphoreType.DMA((2 * count + 5,)),
        ],
        name="project_views",
        compiler_params=grant(52),
        cost_estimate=cost(
            count * 6 * tokens * width * sub, count * tokens * (width + 3 * sub) * 2 + 6 * width * sub
        ),
    )(meta, latents, gain, w_qkv, w_out)
    return {v: (outs[2 * i], outs[2 * i + 1]) for i, v in enumerate(which)}, outs[-2], outs[-1]


ONES = 16
SAFE_TOTAL = 1e30
FAR = 1e30


def head_scores(q_ref, kv_ref, h):
    per = LANES // HEAD_DIM
    j, slot = h // per, h % per
    own = q_ref[h * HEAD_DIM : (h + 1) * HEAD_DIM, :]
    zero = jnp.zeros_like(own)
    padded = jnp.concatenate([own if s == slot else zero for s in range(per)], axis=0)
    return dot(kv_ref[0, :, j * LANES : (j + 1) * LANES], padded)


def head_values(kv_ref, h):
    rows = kv_ref[1, h * HEAD_DIM : (h + 1) * HEAD_DIM, :]
    return jnp.concatenate([rows, jnp.ones((ONES, rows.shape[1]), bf16)], axis=0)


def attention_cost(tokens, sub, pairs):
    heads = sub // HEAD_DIM
    return cost(
        pairs * heads * tokens * tokens * 4 * LANES,
        pairs * tokens * sub * 8,
        pairs * heads * tokens * tokens,
    )


def far_if_absent(inter_ref, at, offset):
    return jnp.where(inter_ref[offset, at] > 0, 0.0, FAR).astype(f32)


def sources_of(view, local_views, window):
    found = []
    for o in range(window):
        if view + o + 1 < local_views:
            found.append((view + o + 1, view, o))
        if view - o - 1 >= 0:
            found.append((view - o - 1, view - o - 1, o))
    return found


def attend(
    meta, inter, queries, blocks, remote, plan, window, earlier=None, last=True, merged=False
):
    local_views = len(blocks)
    sub, tokens = queries[0].shape
    heads = sub // HEAD_DIM
    tall = HEAD_DIM + ONES
    views_total = inter.shape[1]
    names = sorted(remote)
    count = len(plan)
    held = 0 if earlier is None else 2

    def body(meta_ref, inter_ref, *refs):
        before, refs = refs[:held], refs[held:]
        qs, refs = refs[:count], refs[count:]
        kvs, refs = refs[:local_views], refs[local_views:]
        far_kvs, refs = dict(zip(names, refs[: len(names)])), refs[len(names) :]
        first = meta_ref[0] * local_views

        def global_view(source):
            at = first + source
            return jnp.where(at < 0, at + views_total, at) if source < 0 else at

        def keys_of(i):
            view, sources = plan[i]
            keys = [] if held else [(kvs[view], None, None)]
            if not held:
                keys += [(kvs[t], source, o) for t, source, o in sources_of(view, local_views, window)]
            return keys + [(far_kvs[name], source, o) for name, source, o in sources]

        if last:
            outs = [refs[0].at[i] for i in range(count)] if merged else refs[:count]
        units = [(i, h, k) for i in range(count) for h in range(heads) for k in keys_of(i)]
        far = {}
        for _, _, (_, source, o) in units:
            if source is not None and (source, o) not in far:
                far[source, o] = far_if_absent(inter_ref, global_view(source), o)
        upcoming = head_scores(qs[units[0][0]], units[0][2][0], units[0][1])
        worst = jnp.zeros((1, tokens), f32)
        n = 0
        for i, (view, _) in enumerate(plan):
            parts = []
            for h in range(heads):
                keys = keys_of(i)
                weights = []
                top = before[1][i, h : h + 1, :] if held else None
                for _, source, o in keys:
                    scores = upcoming
                    n += 1
                    if n < len(units):
                        ni, nh, (nk, _, _) = units[n]
                        upcoming = head_scores(qs[ni], nk, nh)
                    if source is None:
                        top = jnp.max(scores, axis=0, keepdims=True)
                        shift = top
                    else:
                        shift = top + far[source, o]
                    weights.append(jnp.exp(scores - shift).astype(bf16))
                values = jnp.concatenate([head_values(k[0], h) for k in keys], axis=1)
                sums = dot(values, jnp.concatenate(weights, axis=0))
                if held:
                    sums = sums + before[0][i, h * tall : (h + 1) * tall, :]
                if not last:
                    refs[0][i, h * tall : (h + 1) * tall, :] = sums
                    refs[1][i, h : h + 1, :] = top
                    continue
                total = sums[HEAD_DIM : HEAD_DIM + 1, :]
                worst = jnp.maximum(worst, jnp.where(total < SAFE_TOTAL, 0.0, 1.0))
                parts.append(sums[:HEAD_DIM, :] * (1.0 / total))
            if last:
                outs[i][...] = jnp.transpose(jnp.concatenate(parts, axis=0)).astype(bf16)
        if not last:
            return
        work, work_stat = refs[-2:]

        @pl.when(jnp.max(worst) > 0.0)
        def _():
            for i, (view, sources) in enumerate(plan):
                exact_add(qs[i], kvs[view], work, work_stat, heads, True)
                every = [(kvs[t], s, o) for t, s, o in sources_of(view, local_views, window)]
                every += [(far_kvs[name], s, o) for name, s, o in sources]
                for kv, source, o in every:

                    @pl.when(inter_ref[o, global_view(source)] > 0)
                    def _(i=i, kv=kv):
                        exact_add(qs[i], kv, work, work_stat, heads, False)

                parts = []
                for h in range(heads):
                    total = work_stat[h, 1:2, :]
                    parts.append(work[h * HEAD_DIM : (h + 1) * HEAD_DIM, :] * (1.0 / total))
                outs[i][...] = jnp.transpose(jnp.concatenate(parts, axis=0)).astype(bf16)

    if last:
        out_shape = [jax.ShapeDtypeStruct((tokens, sub), bf16)] * count
        if merged:
            out_shape = [jax.ShapeDtypeStruct((count, tokens, sub), bf16)]
        scratch = [pltpu.VMEM((sub, tokens), f32), pltpu.VMEM((heads, 8, tokens), f32)]
    else:
        out_shape = [
            jax.ShapeDtypeStruct((count, heads * tall, tokens), f32),
            jax.ShapeDtypeStruct((count, heads, tokens), f32),
        ]
        scratch = []
    pairs = sum(len(s) for _, s in plan)
    if not held:
        pairs += sum(1 + len(sources_of(v, local_views, window)) for v, _ in plan)
    return pl.pallas_call(
        body,
        in_specs=[SMEM_SPEC, SMEM_SPEC]
        + many(VMEM_SPEC, held + count + local_views + len(names)),
        out_specs=many(VMEM_SPEC, len(out_shape)),
        out_shape=out_shape,
        scratch_shapes=scratch,
        name="attend" if last else "attend_local",
        compiler_params=grant(12),
        cost_estimate=attention_cost(tokens, sub, pairs),
    )(
        meta,
        inter,
        *(earlier or ()),
        *queries,
        *[blocks[v] for v in range(local_views)],
        *[remote[name] for name in names],
    )


def exact_add(q_ref, kv_ref, work, work_stat, heads, start):
    per = LANES // HEAD_DIM

    def one_head(h, _):
        base = pl.multiple_of((h // per) * LANES, LANES)
        queries = q_ref[pl.ds(base, LANES), :]
        owner = lax.broadcasted_iota(jnp.int32, queries.shape, 0) // HEAD_DIM
        queries = jnp.where(owner == h % per, queries.astype(f32), 0.0).astype(bf16)
        scores = dot(kv_ref[0, :, pl.ds(base, LANES)], queries)
        top = jnp.max(scores, axis=0, keepdims=True)
        rows = pl.ds(pl.multiple_of(h * HEAD_DIM, HEAD_DIM), HEAD_DIM)
        values = kv_ref[1, rows, :]
        if not start:
            old = work_stat[h, 0:1, :]
            top = jnp.maximum(old, top)
        weights = jnp.exp(scores - top)
        total = jnp.sum(weights, axis=0, keepdims=True)
        sums = dot(values, weights.astype(bf16))
        if not start:
            fade = jnp.exp(old - top)
            total = total + work_stat[h, 1:2, :] * fade
            sums = sums + work[rows, :] * fade
        work_stat[h, 0:1, :] = top
        work_stat[h, 1:2, :] = total
        work[rows, :] = sums
        return 0

    lax.fori_loop(0, heads, one_head, 0)


def partial_out(meta, attended, near, w_own, w_mine, w_theirs, halves, place):
    tokens, sub = attended.shape
    width = w_own.shape[1]
    half = width // 2

    def body(meta_ref, att, near_ref, own_ref, mine_ref, theirs_ref, halves_ref, keep, send):
        side = meta_ref[1] // 2
        here = pl.ds(pl.multiple_of(side * half, half), half)
        away = pl.ds(pl.multiple_of((1 - side) * half, half), half)
        second = meta_ref[0] % 2
        strip = sub // 2
        mine = near_ref[:, pl.ds(pl.multiple_of(second * strip, strip), strip)]
        theirs = near_ref[:, pl.ds(pl.multiple_of((1 - second) * strip, strip), strip)]
        rows = jnp.concatenate([att[...], mine, theirs], axis=1)

        def columns(at):
            return jnp.concatenate([own_ref[:, at], mine_ref[:, at], theirs_ref[:, at]], axis=0)

        send[...] = dot(rows, columns(away)).astype(bf16)
        total = dot(rows, columns(here))
        keep[...] = halves_ref[place].astype(f32) + total

    return pl.pallas_call(
        body,
        in_specs=[SMEM_SPEC] + many(VMEM_SPEC, 6),
        out_specs=many(VMEM_SPEC, 2),
        out_shape=[
            jax.ShapeDtypeStruct((tokens, half), f32),
            jax.ShapeDtypeStruct((tokens, half), bf16),
        ],
        name="partial_out",
        compiler_params=grant(12),
        cost_estimate=cost(4 * tokens * sub * width, 4 * sub * width + tokens * width * 6),
    )(meta, attended, near, w_own, w_mine, w_theirs, halves)


def merge_out(meta, keep, got):
    tokens, half = keep.shape
    sub = half // 2

    def body(meta_ref, keep_ref, got_ref, own, other):
        layer = (keep_ref[...] + got_ref[...].astype(f32)).astype(bf16)
        low, high = layer[:, :sub], layer[:, sub:]
        odd = meta_ref[1] % 2 == 1
        own[...] = jnp.where(odd, high, low)
        other[...] = jnp.where(odd, low, high)

    return pl.pallas_call(
        body,
        in_specs=[SMEM_SPEC] + many(VMEM_SPEC, 2),
        out_specs=many(VMEM_SPEC, 2),
        out_shape=[jax.ShapeDtypeStruct((tokens, sub), bf16)] * 2,
        name="merge_out",
        compiler_params=grant(8),
        cost_estimate=cost(tokens * half * 2, tokens * half * 8),
    )(meta, keep, got)


def prepare_requests(block_rows, token_rows, peers, capacity):
    strips, lanes = block_rows.shape

    def body(block_ref, token_ref, wanted_ref, code_ref):
        before = (
            lax.broadcasted_iota(jnp.int32, (lanes, lanes), 0)
            < lax.broadcasted_iota(jnp.int32, (lanes, lanes), 1)
        ).astype(bf16)
        peer_ids = lax.broadcasted_iota(jnp.int32, (peers, lanes), 0)
        carry = jnp.zeros((peers, 1), f32)
        slots, lefts = [], []
        for i in range(strips):
            block = block_ref[i : i + 1, :]
            hit = (peer_ids == block).astype(f32)
            rank = dot(hit.astype(bf16), before) + carry
            carry = carry + jnp.sum(hit, axis=1, keepdims=True)
            slot = jnp.sum(rank * hit, axis=0, keepdims=True)
            slots.append(slot)
            code_ref[i : i + 1, :] = block * capacity + slot.astype(jnp.int32)
            token = token_ref[i : i + 1, :]
            coarse = (token // 32).astype(f32)
            fine = (token % 32).astype(f32)
            lefts.append(jnp.concatenate([hit * coarse, hit * fine], axis=0).astype(bf16))
        columns = jnp.transpose(jnp.concatenate(slots, axis=0))
        place = lax.broadcasted_iota(jnp.int32, (lanes, capacity), 1).astype(f32)
        total = jnp.zeros((2 * peers, capacity), f32)
        for i in range(strips):
            spot = (columns[:, i : i + 1] == place).astype(bf16)
            total = total + dot(lefts[i], spot)
        wanted_ref[...] = (total[:peers] * 32.0 + total[peers:]).astype(jnp.int32)

    return pl.pallas_call(
        body,
        in_specs=[VMEM_SPEC, VMEM_SPEC],
        out_specs=[VMEM_SPEC, VMEM_SPEC],
        out_shape=[
            jax.ShapeDtypeStruct((peers, capacity), jnp.int32),
            jax.ShapeDtypeStruct((strips, lanes), jnp.int32),
        ],
        name="prepare_requests",
        compiler_params=grant(8),
        cost_estimate=cost(2 * strips * lanes * lanes * capacity, 3 * strips * lanes * 4),
    )(block_rows, token_rows)


def picks(offsets, width):
    clamped = jnp.minimum(jnp.maximum(offsets, -1.0), float(width)).astype(bf16)
    place = lax.broadcasted_iota(jnp.int32, (offsets.shape[0], width), 1).astype(f32).astype(bf16)
    spread = jnp.broadcast_to(clamped, place.shape)
    return jnp.where(spread == place, jnp.ones_like(place), jnp.zeros_like(place))


def gather_rows(meta, wanted, pieces):
    peers, capacity = int(round(wanted.shape[0] ** 0.5)), wanted.shape[1]
    tokens, sub = pieces[0][0].shape
    local_views = len(pieces)
    rows = local_views * tokens
    flat = [p for pair in pieces for p in pair]

    def body(meta_ref, wanted_ref, *refs):
        ins = refs[: len(flat)]
        layer, outs = refs[len(flat)], refs[len(flat) + 1 :]
        end = jnp.logical_or(meta_ref[1] == 0, meta_ref[1] == meta_ref[2] - 1)
        for v in range(local_views):
            layer[v * tokens : (v + 1) * tokens, :] = jnp.where(
                end, ins[2 * v + 1][...], ins[2 * v][...]
            )
        lines = [wanted_ref[pl.ds(m * peers + meta_ref[0], 1), :] for m in range(peers)]
        columns = jnp.transpose(jnp.concatenate(lines, axis=0).astype(f32))
        for mask in range(peers):
            column = columns[:, mask : mask + 1]
            pick = jnp.concatenate(
                [picks(column - float(v * tokens), tokens) for v in range(local_views)], axis=1
            )
            outs[mask][...] = dot(pick, layer[...]).astype(bf16)

    return pl.pallas_call(
        body,
        in_specs=[SMEM_SPEC] + many(VMEM_SPEC, 1 + len(flat)),
        out_specs=many(VMEM_SPEC, 1 + peers),
        out_shape=[jax.ShapeDtypeStruct((rows, sub), bf16)]
        + [jax.ShapeDtypeStruct((capacity, sub), bf16)] * peers,
        name="gather_rows",
        compiler_params=grant(12),
        cost_estimate=cost(2 * peers * capacity * rows * sub, 2 * (rows + peers * capacity) * sub * 2),
    )(meta, wanted, *flat)


def finish_rows(meta, code, confidence, layer, replies, tokens):
    rows, sub = layer.shape
    peers = len(replies)
    capacity = replies[0].shape[0]
    _, lanes = code.shape
    blocks = rows // tokens
    per = tokens // lanes

    def body(meta_ref, code_ref, conf_ref, layer_ref, *refs):
        reps, (out_hbm, buffer, sems) = refs[:peers], refs[peers:]
        codes = jnp.transpose(code_ref[...].astype(f32))
        confs = jnp.transpose(conf_ref[...]) * coupling
        copies = []
        for g in range(blocks):

            def column(turned):
                return jnp.concatenate(
                    [turned[:, g * per + j : g * per + j + 1] for j in range(per)], axis=0
                )

            code_column = column(codes)
            pick = jnp.concatenate(
                [
                    picks(
                        code_column
                        - (lax.bitwise_xor(meta_ref[0], mask) * capacity).astype(f32),
                        capacity,
                    )
                    for mask in range(peers)
                ],
                axis=1,
            )
            fetched = dot(pick, jnp.concatenate([r[...] for r in reps], axis=0))
            wide = layer_ref[g * tokens : (g + 1) * tokens, :].astype(f32)
            buffer[g] = wide + column(confs) * (fetched - wide)
            copies.append(
                pltpu.make_async_copy(
                    buffer.at[g], out_hbm.at[pl.ds(g * tokens, tokens), :], sems.at[g]
                )
            )
            copies[-1].start()
        for copy in copies:
            copy.wait()

    return pl.pallas_call(
        body,
        in_specs=[SMEM_SPEC] + many(VMEM_SPEC, 3 + peers),
        out_specs=ANY_SPEC,
        out_shape=jax.ShapeDtypeStruct((rows, sub), f32),
        scratch_shapes=[
            pltpu.VMEM((blocks, tokens, sub), f32),
            pltpu.SemaphoreType.DMA((blocks,)),
        ],
        name="finish_rows",
        compiler_params=grant(12),
        cost_estimate=cost(2 * peers * capacity * rows * sub, rows * sub * 6 + peers * capacity * sub * 2),
    )(meta, code, confidence, layer, *replies)


def per_device(latents, norm_gain, w_qkv, w_out, intersection, match_block, match_row, confidence):
    local_views, tokens, width = latents.shape
    window = intersection.shape[1]
    sub = w_qkv.shape[2]
    peers = lax.axis_size("views")
    ends = lax.axis_size("heads")
    rows = local_views * tokens
    capacity = 2 * rows // peers
    assert local_views == 4 and window == 2 and ends == 4 and tokens == sub
    view_at, head_at = lax.axis_index("views"), lax.axis_index("heads")
    spot = jnp.arange(4, dtype=jnp.int32)
    meta = jnp.where(spot == 0, view_at, jnp.where(spot == 1, head_at, ends)).astype(jnp.int32)

    def along(x, by):
        return lax.ppermute(x, "views", [(i, (i + by) % peers) for i in range(peers)])

    def partner(x, mask):
        return lax.ppermute(x, "views", [(i, i ^ mask) for i in range(peers)])

    def across(x, pairs):
        return lax.ppermute(x, "heads", pairs)

    def after(x, done):
        return lax.optimization_barrier((x, done))[0]

    beside, middle, back = [(0, 1), (3, 2)], [(1, 2), (2, 1)], [(1, 0), (2, 3)]
    gain = norm_gain.reshape(1, width)
    inter = intersection.T
    loaded = (0, local_views - 1, 1, 2)
    projected, halves, w_half = project_views(meta, latents, gain, w_qkv, w_out, loaded)
    queries = {v: projected[v][0] for v in range(local_views)}
    blocks = {v: projected[v][1] for v in range(local_views)}
    next_first = along(blocks[0], -1)
    prev_last = along(blocks[3], 1)
    w_mine = across(w_half, beside)

    inner_plan = [(1, [("prev_last", -1, 1)]), (2, [("next_first", 2, 1)])]
    inner_queries = [queries[1], queries[2]]
    local = attend(
        meta, inter, inner_queries, blocks, {}, [(v, []) for v, _ in inner_plan], window, last=False
    )
    next_second = along(after(blocks[1], local[0]), -1)
    prev_second = along(after(blocks[2], local[0]), 1)
    remote = dict(prev_last=prev_last, next_first=next_first)
    inner = attend(
        meta, inter, inner_queries, blocks, remote, inner_plan, window, earlier=tuple(local)
    )
    remote.update(prev_second=prev_second, next_second=next_second)
    outer_plan = [
        (0, [("prev_last", -1, 0), ("prev_second", -2, 1)]),
        (3, [("next_first", 3, 0), ("next_second", 3, 1)]),
    ]
    outer_queries = [after(queries[0], inner[0]), queries[3]]
    outer = attend(meta, inter, outer_queries, blocks, remote, outer_plan, window)
    attended = {1: inner[0], 2: inner[1], 0: outer[0], 3: outer[1]}
    w_theirs = partner(after(w_mine, inner[0]), 1)
    keep, got, formed = {}, {}, {}
    for v in VIEW_ORDER:
        near = across(attended[v], beside)
        keep[v], send = partial_out(
            meta, attended[v], near, w_out, w_mine, w_theirs, halves, loaded.index(v)
        )
        got[v] = across(send, middle)
    strips = rows // LANES
    wanted, code = prepare_requests(
        after(match_block.reshape(strips, LANES), send),
        match_row.reshape(strips, LANES),
        peers,
        capacity,
    )
    mask = 1
    while mask < peers:
        wanted = jnp.concatenate([wanted, partner(wanted, mask)], axis=0)
        mask *= 2
    for v in VIEW_ORDER:
        own, other = merge_out(meta, keep[v], got[v])
        formed[v] = (own, across(other, back))

    pieces = [formed[v] for v in range(local_views)]
    layer, *outgoing = gather_rows(meta, wanted, pieces)
    replies = [outgoing[0]]
    for mask in range(1, peers):
        replies.append(partner(outgoing[mask], mask))
    refined = finish_rows(
        meta, code, confidence.reshape(strips, LANES), layer, replies, tokens
    )
    return refined.reshape(local_views, tokens, sub)


def solution(mesh):
    in_specs = (
        P("views", None, None),
        P(),
        P(None, None, "heads"),
        P("heads", None),
        P(),
        P("views", None),
        P("views"),
        P("views"),
    )
    out_specs = P("views", None, "heads")
    return jax.shard_map(
        per_device, mesh=mesh, in_specs=in_specs, out_specs=out_specs, check_vma=False
    )
```

```python
import jax
import jax.numpy as jnp
from jax import lax
from jax.experimental import pallas as pl
from jax.experimental.pallas import tpu as pltpu
from jax.sharding import PartitionSpec as P


HEAD_DIM = 64
LANES = 128
VIEW_ORDER = (1, 2, 0, 3)

coupling = 0.5
epsilon = 1e-06

bf16 = jnp.bfloat16
f32 = jnp.float32


def cost(flops, bytes_accessed, transcendentals=0):
    return pl.CostEstimate(
        flops=int(flops), bytes_accessed=int(bytes_accessed), transcendentals=int(transcendentals)
    )


def dot(a, b):
    return jnp.dot(a, b, preferred_element_type=f32)


VMEM_SPEC = pl.BlockSpec(memory_space=pltpu.VMEM)
SMEM_SPEC = pl.BlockSpec(memory_space=pltpu.SMEM)
ANY_SPEC = pl.BlockSpec(memory_space=pl.ANY)


def grant(mib):
    return pltpu.CompilerParams(vmem_limit_bytes=mib << 20)


def many(spec, count):
    return [spec] * count


def project_views(meta, latents, gain, w_qkv, w_out, which):
    _, tokens, width = latents.shape
    sub = w_qkv.shape[2]
    count = len(which)
    scale = HEAD_DIM ** (-0.5)
    order = (2, 0, 1)

    strip = sub // 2

    def body(meta_ref, lat_hbm, gain_hbm, w_hbm, w_out_hbm, *refs):
        outs, (halves, w_half, buffer, gains, ws, sems) = refs[: 2 * count], refs[2 * count :]
        mine = pl.ds(pl.multiple_of((meta_ref[0] % 2) * strip, strip), strip)
        w_copy = pltpu.make_async_copy(w_out_hbm.at[mine], w_half, sems.at[2 * count + 4])
        here = pl.ds(pl.multiple_of((meta_ref[1] // 2) * (width // 2), width // 2), width // 2)
        kept = [
            pltpu.make_async_copy(buffer.at[i, :, here], halves.at[i], sems.at[count + 4 + i])
            for i in range(count)
        ]
        copies = [
            pltpu.make_async_copy(lat_hbm.at[v], buffer.at[i], sems.at[i])
            for i, v in enumerate(which)
        ]
        gain_copy = pltpu.make_async_copy(gain_hbm, gains, sems.at[count])
        w_copies = {
            part: pltpu.make_async_copy(w_hbm.at[part], ws.at[part], sems.at[count + 1 + part])
            for part in order
        }
        for copy in [gain_copy, copies[0]] + [w_copies[p] for p in order] + copies[1:] + [w_copy]:
            copy.start()

        def load_norm(i):
            copies[i].wait()
            kept[i].start()
            wide = buffer[i].astype(f32)
            mean_square = jnp.mean(wide * wide, axis=-1, keepdims=True)
            return (wide * lax.rsqrt(mean_square + epsilon) * gains[...]).astype(bf16)

        gain_copy.wait()
        following = load_norm(0)
        for part in order:
            w_copies[part].wait()
        for i in range(count):
            normed = following
            if i + 1 < count:
                following = load_norm(i + 1)
            values = dot(normed, ws[2])
            queries = dot(normed, ws[0])
            outs[2 * i + 1][0] = dot(normed, ws[1]).astype(bf16)
            outs[2 * i + 1][1] = jnp.transpose(values).astype(bf16)
            outs[2 * i][...] = jnp.transpose(queries).astype(bf16) * jnp.asarray(scale, bf16)
        w_copy.wait()
        for copy in kept:
            copy.wait()

    out_shape = []
    for _ in which:
        out_shape += [
            jax.ShapeDtypeStruct((sub, tokens), bf16),
            jax.ShapeDtypeStruct((2, tokens, sub), bf16),
        ]
    out_shape.append(jax.ShapeDtypeStruct((count, tokens, width // 2), bf16))
    out_shape.append(jax.ShapeDtypeStruct((strip, w_out.shape[1]), bf16))
    outs = pl.pallas_call(
        body,
        in_specs=[SMEM_SPEC] + many(ANY_SPEC, 4),
        out_specs=many(VMEM_SPEC, len(out_shape)),
        out_shape=out_shape,
        scratch_shapes=[
            pltpu.VMEM((count, tokens, width), bf16),
            pltpu.VMEM((1, width), f32),
            pltpu.VMEM((3, width, sub), bf16),
            pltpu.SemaphoreType.DMA((2 * count + 5,)),
        ],
        name="project_views",
        compiler_params=grant(52),
        cost_estimate=cost(
            count * 6 * tokens * width * sub, count * tokens * (width + 3 * sub) * 2 + 6 * width * sub
        ),
    )(meta, latents, gain, w_qkv, w_out)
    return {v: (outs[2 * i], outs[2 * i + 1]) for i, v in enumerate(which)}, outs[-2], outs[-1]


ONES = 16
SAFE_TOTAL = 1e30
FAR = 1e30


def head_scores(q_ref, kv_ref, h):
    per = LANES // HEAD_DIM
    j, slot = h // per, h % per
    own = q_ref[h * HEAD_DIM : (h + 1) * HEAD_DIM, :]
    zero = jnp.zeros_like(own)
    padded = jnp.concatenate([own if s == slot else zero for s in range(per)], axis=0)
    return dot(kv_ref[0, :, j * LANES : (j + 1) * LANES], padded)


def head_values(kv_ref, h):
    rows = kv_ref[1, h * HEAD_DIM : (h + 1) * HEAD_DIM, :]
    return jnp.concatenate([rows, jnp.ones((ONES, rows.shape[1]), bf16)], axis=0)


def attention_cost(tokens, sub, pairs):
    heads = sub // HEAD_DIM
    return cost(
        pairs * heads * tokens * tokens * 4 * LANES,
        pairs * tokens * sub * 8,
        pairs * heads * tokens * tokens,
    )


def far_if_absent(inter_ref, at, offset):
    return jnp.where(inter_ref[offset, at] > 0, 0.0, FAR).astype(f32)


def sources_of(view, local_views, window):
    found = []
    for o in range(window):
        if view + o + 1 < local_views:
            found.append((view + o + 1, view, o))
        if view - o - 1 >= 0:
            found.append((view - o - 1, view - o - 1, o))
    return found


def attend(
    meta, inter, queries, blocks, remote, plan, window, earlier=None, last=True, merged=False
):
    local_views = len(blocks)
    sub, tokens = queries[0].shape
    heads = sub // HEAD_DIM
    tall = HEAD_DIM + ONES
    views_total = inter.shape[1]
    names = sorted(remote)
    count = len(plan)
    held = 0 if earlier is None else 2

    def body(meta_ref, inter_ref, *refs):
        before, refs = refs[:held], refs[held:]
        qs, refs = refs[:count], refs[count:]
        kvs, refs = refs[:local_views], refs[local_views:]
        far_kvs, refs = dict(zip(names, refs[: len(names)])), refs[len(names) :]
        first = meta_ref[0] * local_views

        def global_view(source):
            at = first + source
            return jnp.where(at < 0, at + views_total, at) if source < 0 else at

        def keys_of(i):
            view, sources = plan[i]
            keys = [] if held else [(kvs[view], None, None)]
            if not held:
                keys += [(kvs[t], source, o) for t, source, o in sources_of(view, local_views, window)]
            return keys + [(far_kvs[name], source, o) for name, source, o in sources]

        if last:
            outs = [refs[0].at[i] for i in range(count)] if merged else refs[:count]
        units = [(i, h, k) for i in range(count) for h in range(heads) for k in keys_of(i)]
        far = {}
        for _, _, (_, source, o) in units:
            if source is not None and (source, o) not in far:
                far[source, o] = far_if_absent(inter_ref, global_view(source), o)
        upcoming = head_scores(qs[units[0][0]], units[0][2][0], units[0][1])
        worst = jnp.zeros((1, tokens), f32)
        n = 0
        for i, (view, _) in enumerate(plan):
            parts = []
            for h in range(heads):
                keys = keys_of(i)
                weights = []
                top = before[1][i, h : h + 1, :] if held else None
                for _, source, o in keys:
                    scores = upcoming
                    n += 1
                    if n < len(units):
                        ni, nh, (nk, _, _) = units[n]
                        upcoming = head_scores(qs[ni], nk, nh)
                    if source is None:
                        top = jnp.max(scores, axis=0, keepdims=True)
                        shift = top
                    else:
                        shift = top + far[source, o]
                    weights.append(jnp.exp(scores - shift).astype(bf16))
                values = jnp.concatenate([head_values(k[0], h) for k in keys], axis=1)
                sums = dot(values, jnp.concatenate(weights, axis=0))
                if held:
                    sums = sums + before[0][i, h * tall : (h + 1) * tall, :]
                if not last:
                    refs[0][i, h * tall : (h + 1) * tall, :] = sums
                    refs[1][i, h : h + 1, :] = top
                    continue
                total = sums[HEAD_DIM : HEAD_DIM + 1, :]
                worst = jnp.maximum(worst, jnp.where(total < SAFE_TOTAL, 0.0, 1.0))
                parts.append(sums[:HEAD_DIM, :] * (1.0 / total))
            if last:
                outs[i][...] = jnp.transpose(jnp.concatenate(parts, axis=0)).astype(bf16)
        if not last:
            return
        work, work_stat = refs[-2:]

        @pl.when(jnp.max(worst) > 0.0)
        def _():
            for i, (view, sources) in enumerate(plan):
                exact_add(qs[i], kvs[view], work, work_stat, heads, True)
                every = [(kvs[t], s, o) for t, s, o in sources_of(view, local_views, window)]
                every += [(far_kvs[name], s, o) for name, s, o in sources]
                for kv, source, o in every:

                    @pl.when(inter_ref[o, global_view(source)] > 0)
                    def _(i=i, kv=kv):
                        exact_add(qs[i], kv, work, work_stat, heads, False)

                parts = []
                for h in range(heads):
                    total = work_stat[h, 1:2, :]
                    parts.append(work[h * HEAD_DIM : (h + 1) * HEAD_DIM, :] * (1.0 / total))
                outs[i][...] = jnp.transpose(jnp.concatenate(parts, axis=0)).astype(bf16)

    if last:
        out_shape = [jax.ShapeDtypeStruct((tokens, sub), bf16)] * count
        if merged:
            out_shape = [jax.ShapeDtypeStruct((count, tokens, sub), bf16)]
        scratch = [pltpu.VMEM((sub, tokens), f32), pltpu.VMEM((heads, 8, tokens), f32)]
    else:
        out_shape = [
            jax.ShapeDtypeStruct((count, heads * tall, tokens), f32),
            jax.ShapeDtypeStruct((count, heads, tokens), f32),
        ]
        scratch = []
    pairs = sum(len(s) for _, s in plan)
    if not held:
        pairs += sum(1 + len(sources_of(v, local_views, window)) for v, _ in plan)
    return pl.pallas_call(
        body,
        in_specs=[SMEM_SPEC, SMEM_SPEC]
        + many(VMEM_SPEC, held + count + local_views + len(names)),
        out_specs=many(VMEM_SPEC, len(out_shape)),
        out_shape=out_shape,
        scratch_shapes=scratch,
        name="attend" if last else "attend_local",
        compiler_params=grant(12),
        cost_estimate=attention_cost(tokens, sub, pairs),
    )(
        meta,
        inter,
        *(earlier or ()),
        *queries,
        *[blocks[v] for v in range(local_views)],
        *[remote[name] for name in names],
    )


def exact_add(q_ref, kv_ref, work, work_stat, heads, start):
    per = LANES // HEAD_DIM

    def one_head(h, _):
        base = pl.multiple_of((h // per) * LANES, LANES)
        queries = q_ref[pl.ds(base, LANES), :]
        owner = lax.broadcasted_iota(jnp.int32, queries.shape, 0) // HEAD_DIM
        queries = jnp.where(owner == h % per, queries.astype(f32), 0.0).astype(bf16)
        scores = dot(kv_ref[0, :, pl.ds(base, LANES)], queries)
        top = jnp.max(scores, axis=0, keepdims=True)
        rows = pl.ds(pl.multiple_of(h * HEAD_DIM, HEAD_DIM), HEAD_DIM)
        values = kv_ref[1, rows, :]
        if not start:
            old = work_stat[h, 0:1, :]
            top = jnp.maximum(old, top)
        weights = jnp.exp(scores - top)
        total = jnp.sum(weights, axis=0, keepdims=True)
        sums = dot(values, weights.astype(bf16))
        if not start:
            fade = jnp.exp(old - top)
            total = total + work_stat[h, 1:2, :] * fade
            sums = sums + work[rows, :] * fade
        work_stat[h, 0:1, :] = top
        work_stat[h, 1:2, :] = total
        work[rows, :] = sums
        return 0

    lax.fori_loop(0, heads, one_head, 0)


def partial_out(meta, attended, near, w_own, w_mine, w_theirs, halves, place):
    tokens, sub = attended.shape
    width = w_own.shape[1]
    half = width // 2

    def body(meta_ref, att, near_ref, own_ref, mine_ref, theirs_ref, halves_ref, keep, send):
        side = meta_ref[1] // 2
        here = pl.ds(pl.multiple_of(side * half, half), half)
        away = pl.ds(pl.multiple_of((1 - side) * half, half), half)
        second = meta_ref[0] % 2
        strip = sub // 2
        mine = near_ref[:, pl.ds(pl.multiple_of(second * strip, strip), strip)]
        theirs = near_ref[:, pl.ds(pl.multiple_of((1 - second) * strip, strip), strip)]
        rows = jnp.concatenate([att[...], mine, theirs], axis=1)

        def columns(at):
            return jnp.concatenate([own_ref[:, at], mine_ref[:, at], theirs_ref[:, at]], axis=0)

        send[...] = dot(rows, columns(away)).astype(bf16)
        total = dot(rows, columns(here))
        keep[...] = halves_ref[place].astype(f32) + total

    return pl.pallas_call(
        body,
        in_specs=[SMEM_SPEC] + many(VMEM_SPEC, 6),
        out_specs=many(VMEM_SPEC, 2),
        out_shape=[
            jax.ShapeDtypeStruct((tokens, half), f32),
            jax.ShapeDtypeStruct((tokens, half), bf16),
        ],
        name="partial_out",
        compiler_params=grant(12),
        cost_estimate=cost(4 * tokens * sub * width, 4 * sub * width + tokens * width * 6),
    )(meta, attended, near, w_own, w_mine, w_theirs, halves)


def merge_out(meta, keep, got):
    tokens, half = keep.shape
    sub = half // 2

    def body(meta_ref, keep_ref, got_ref, own, other):
        layer = (keep_ref[...] + got_ref[...].astype(f32)).astype(bf16)
        low, high = layer[:, :sub], layer[:, sub:]
        odd = meta_ref[1] % 2 == 1
        own[...] = jnp.where(odd, high, low)
        other[...] = jnp.where(odd, low, high)

    return pl.pallas_call(
        body,
        in_specs=[SMEM_SPEC] + many(VMEM_SPEC, 2),
        out_specs=many(VMEM_SPEC, 2),
        out_shape=[jax.ShapeDtypeStruct((tokens, sub), bf16)] * 2,
        name="merge_out",
        compiler_params=grant(8),
        cost_estimate=cost(tokens * half * 2, tokens * half * 8),
    )(meta, keep, got)


def prepare_requests(block_rows, token_rows, peers, capacity):
    strips, lanes = block_rows.shape

    def body(block_ref, token_ref, wanted_ref, code_ref):
        before = (
            lax.broadcasted_iota(jnp.int32, (lanes, lanes), 0)
            < lax.broadcasted_iota(jnp.int32, (lanes, lanes), 1)
        ).astype(bf16)
        peer_ids = lax.broadcasted_iota(jnp.int32, (peers, lanes), 0)
        carry = jnp.zeros((peers, 1), f32)
        slots, lefts = [], []
        for i in range(strips):
            block = block_ref[i : i + 1, :]
            hit = (peer_ids == block).astype(f32)
            rank = dot(hit.astype(bf16), before) + carry
            carry = carry + jnp.sum(hit, axis=1, keepdims=True)
            slot = jnp.sum(rank * hit, axis=0, keepdims=True)
            slots.append(slot)
            code_ref[i : i + 1, :] = block * capacity + slot.astype(jnp.int32)
            token = token_ref[i : i + 1, :]
            coarse = (token // 32).astype(f32)
            fine = (token % 32).astype(f32)
            lefts.append(jnp.concatenate([hit * coarse, hit * fine], axis=0).astype(bf16))
        columns = jnp.transpose(jnp.concatenate(slots, axis=0))
        place = lax.broadcasted_iota(jnp.int32, (lanes, capacity), 1).astype(f32)
        total = jnp.zeros((2 * peers, capacity), f32)
        for i in range(strips):
            spot = (columns[:, i : i + 1] == place).astype(bf16)
            total = total + dot(lefts[i], spot)
        wanted_ref[...] = (total[:peers] * 32.0 + total[peers:]).astype(jnp.int32)

    return pl.pallas_call(
        body,
        in_specs=[VMEM_SPEC, VMEM_SPEC],
        out_specs=[VMEM_SPEC, VMEM_SPEC],
        out_shape=[
            jax.ShapeDtypeStruct((peers, capacity), jnp.int32),
            jax.ShapeDtypeStruct((strips, lanes), jnp.int32),
        ],
        name="prepare_requests",
        compiler_params=grant(8),
        cost_estimate=cost(2 * strips * lanes * lanes * capacity, 3 * strips * lanes * 4),
    )(block_rows, token_rows)


def spread_picks(spread, shift, width):
    clamped = jnp.minimum(jnp.maximum(spread - shift, -1.0), float(width)).astype(bf16)
    wide = jnp.concatenate([clamped] * (width // LANES), axis=1) if width > LANES else clamped[:, :width]
    place = lax.broadcasted_iota(jnp.int32, wide.shape, 1).astype(f32).astype(bf16)
    return jnp.where(wide == place, jnp.ones_like(place), jnp.zeros_like(place))


def gather_rows(meta, wanted, pieces, masks, tokens):
    peers, capacity = int(round(wanted.shape[0] ** 0.5)), wanted.shape[1]
    whole = not isinstance(pieces, list)
    flat = [pieces] if whole else [p for pair in pieces for p in pair]
    sub = flat[0].shape[1]
    rows = flat[0].shape[0] if whole else len(pieces) * tokens
    local_views = rows // tokens

    def body(meta_ref, wanted_ref, *refs):
        ins, outs = refs[: len(flat)], refs[len(flat) :]
        if whole:
            layer = ins[0]
        else:
            layer, outs = outs[0], outs[1:]
            end = jnp.logical_or(meta_ref[1] == 0, meta_ref[1] == meta_ref[2] - 1)
            for v in range(local_views):
                layer[v * tokens : (v + 1) * tokens, :] = jnp.where(
                    end, ins[2 * v + 1][...], ins[2 * v][...]
                )
        lines = [wanted_ref[pl.ds(m * peers + meta_ref[0], 1), :] for m in masks]
        lines += [lines[0]] * (-len(lines) % 8)
        columns = jnp.transpose(jnp.concatenate(lines, axis=0).astype(f32))
        for n in range(len(masks)):
            spread = jnp.broadcast_to(columns[:, n : n + 1], (capacity, LANES))
            pick = jnp.concatenate(
                [spread_picks(spread, float(v * tokens), tokens) for v in range(local_views)], axis=1
            )
            outs[n][...] = dot(pick, layer[...]).astype(bf16)

    out_shape = [jax.ShapeDtypeStruct((capacity, sub), bf16)] * len(masks)
    if not whole:
        out_shape = [jax.ShapeDtypeStruct((rows, sub), bf16)] + out_shape
    return pl.pallas_call(
        body,
        in_specs=[SMEM_SPEC] + many(VMEM_SPEC, 1 + len(flat)),
        out_specs=many(VMEM_SPEC, len(out_shape)),
        out_shape=out_shape,
        name="gather_rows",
        compiler_params=grant(12),
        cost_estimate=cost(
            2 * len(masks) * capacity * rows * sub, 2 * (rows + len(masks) * capacity) * sub * 2
        ),
    )(meta, wanted, *flat)


def fetched_part(meta_ref, code_spread, masks, reps, capacity):
    pick = jnp.concatenate(
        [
            spread_picks(
                code_spread, (lax.bitwise_xor(meta_ref[0], mask) * capacity).astype(f32), capacity
            )
            for mask in masks
        ],
        axis=1,
    )
    return dot(pick, jnp.concatenate([r[...] for r in reps], axis=0))


def spread_column(turned, g, per, lanes):
    return jnp.concatenate(
        [
            jnp.broadcast_to(turned[:, g * per + j : g * per + j + 1], (lanes, LANES))
            for j in range(per)
        ],
        axis=0,
    )


def first_replies(meta, code, replies, tokens):
    masks = sorted(replies)
    capacity, sub = replies[masks[0]].shape
    strips, lanes = code.shape
    rows = strips * lanes
    per = tokens // lanes

    def body(meta_ref, code_ref, *refs):
        codes = jnp.transpose(code_ref[...].astype(f32))
        for g in range(rows // tokens):
            refs[-1][g * tokens : (g + 1) * tokens, :] = fetched_part(
                meta_ref, spread_column(codes, g, per, lanes), masks, refs[:-1], capacity
            ).astype(bf16)

    return pl.pallas_call(
        body,
        in_specs=[SMEM_SPEC] + many(VMEM_SPEC, 1 + len(masks)),
        out_specs=VMEM_SPEC,
        out_shape=jax.ShapeDtypeStruct((rows, sub), bf16),
        name="first_replies",
        compiler_params=grant(12),
        cost_estimate=cost(2 * len(masks) * capacity * rows * sub, rows * sub * 4),
    )(meta, code, *[replies[m] for m in masks])


def finish_rows(meta, code, confidence, layer, early, replies, tokens):
    rows, sub = layer.shape
    masks = sorted(replies)
    capacity = replies[masks[0]].shape[0]
    _, lanes = code.shape
    blocks = rows // tokens
    per = tokens // lanes

    def body(meta_ref, code_ref, conf_ref, layer_ref, early_ref, *refs):
        reps, (out_hbm, buffer, sems) = refs[: len(masks)], refs[len(masks) :]
        codes = jnp.transpose(code_ref[...].astype(f32))
        confs = jnp.transpose(conf_ref[...]) * coupling
        copies = []
        for g in range(blocks):
            at = slice(g * tokens, (g + 1) * tokens)
            fetched = early_ref[at, :].astype(f32) + fetched_part(
                meta_ref, spread_column(codes, g, per, lanes), masks, reps, capacity
            )
            wide = layer_ref[at, :].astype(f32)
            weight = jnp.concatenate([spread_column(confs, g, per, lanes)] * (sub // LANES), axis=1)
            buffer[g] = wide + weight * (fetched - wide)
            copies.append(
                pltpu.make_async_copy(
                    buffer.at[g], out_hbm.at[pl.ds(g * tokens, tokens), :], sems.at[g]
                )
            )
            copies[-1].start()
        for copy in copies:
            copy.wait()

    return pl.pallas_call(
        body,
        in_specs=[SMEM_SPEC] + many(VMEM_SPEC, 4 + len(masks)),
        out_specs=ANY_SPEC,
        out_shape=jax.ShapeDtypeStruct((rows, sub), f32),
        scratch_shapes=[
            pltpu.VMEM((blocks, tokens, sub), f32),
            pltpu.SemaphoreType.DMA((blocks,)),
        ],
        name="finish_rows",
        compiler_params=grant(12),
        cost_estimate=cost(2 * len(masks) * capacity * rows * sub, rows * sub * 8),
    )(meta, code, confidence, layer, early, *[replies[m] for m in masks])


def per_device(latents, norm_gain, w_qkv, w_out, intersection, match_block, match_row, confidence):
    local_views, tokens, width = latents.shape
    window = intersection.shape[1]
    sub = w_qkv.shape[2]
    peers = lax.axis_size("views")
    ends = lax.axis_size("heads")
    rows = local_views * tokens
    capacity = 2 * rows // peers
    assert local_views == 4 and window == 2 and ends == 4 and tokens == sub
    view_at, head_at = lax.axis_index("views"), lax.axis_index("heads")
    spot = jnp.arange(4, dtype=jnp.int32)
    meta = jnp.where(spot == 0, view_at, jnp.where(spot == 1, head_at, ends)).astype(jnp.int32)

    def along(x, by):
        return lax.ppermute(x, "views", [(i, (i + by) % peers) for i in range(peers)])

    def partner(x, mask):
        return lax.ppermute(x, "views", [(i, i ^ mask) for i in range(peers)])

    def across(x, pairs):
        return lax.ppermute(x, "heads", pairs)

    def after(x, done):
        return lax.optimization_barrier((x, done))[0]

    beside, middle, back = [(0, 1), (3, 2)], [(1, 2), (2, 1)], [(1, 0), (2, 3)]
    gain = norm_gain.reshape(1, width)
    inter = intersection.T
    loaded = (0, local_views - 1, 1, 2)
    projected, halves, w_half = project_views(meta, latents, gain, w_qkv, w_out, loaded)
    queries = {v: projected[v][0] for v in range(local_views)}
    blocks = {v: projected[v][1] for v in range(local_views)}
    next_first = along(blocks[0], -1)
    prev_last = along(blocks[3], 1)
    w_mine = across(w_half, beside)

    inner_plan = [(1, [("prev_last", -1, 1)]), (2, [("next_first", 2, 1)])]
    inner_queries = [queries[1], queries[2]]
    local = attend(
        meta, inter, inner_queries, blocks, {}, [(v, []) for v, _ in inner_plan], window, last=False
    )
    next_second = along(after(blocks[1], local[0]), -1)
    prev_second = along(after(blocks[2], local[0]), 1)
    remote = dict(prev_last=prev_last, next_first=next_first)
    inner = attend(
        meta, inter, inner_queries, blocks, remote, inner_plan, window, earlier=tuple(local)
    )
    w_theirs = partner(after(w_mine, inner[0]), 1)
    sent = {}

    def attend_outer(view, sources, done):
        (result,) = attend(
            meta,
            inter,
            [after(queries[view], done)],
            blocks,
            {k: x for k, x in halo.items() if k in [s[0] for s in sources]},
            [(view, sources)],
            window,
        )
        return result

    halo = dict(remote, prev_second=prev_second, next_second=next_second)
    attended = {1: inner[0], 2: inner[1]}
    attended[0] = attend_outer(0, [("prev_last", -1, 0), ("prev_second", -2, 1)], inner[0])
    keep, got, formed = {}, {}, {}

    def pass_on(v):
        near = across(attended[v], beside)
        keep[v], sent[v] = partial_out(
            meta, attended[v], near, w_out, w_mine, w_theirs, halves, loaded.index(v)
        )
        got[v] = across(sent[v], middle)

    pass_on(1)
    pass_on(2)
    attended[3] = attend_outer(3, [("next_first", 3, 0), ("next_second", 3, 1)], sent[2])
    pass_on(0)
    pass_on(3)
    strips = rows // LANES
    wanted, code = prepare_requests(
        after(match_block.reshape(strips, LANES), sent[3]),
        match_row.reshape(strips, LANES),
        peers,
        capacity,
    )
    mask = 1
    while mask < peers:
        wanted = jnp.concatenate([wanted, partner(wanted, mask)], axis=0)
        mask *= 2
    for v in VIEW_ORDER:
        own, other = merge_out(meta, keep[v], got[v])
        formed[v] = (own, across(other, back))

    pieces = [formed[v] for v in range(local_views)]
    first_masks, last_masks = reply_order(peers)
    replies = {}

    def reply(masks, outgoing):
        for mask, rows_out in zip(masks, outgoing):
            replies[mask] = partner(rows_out, mask)

    layer, *outgoing = gather_rows(meta, wanted, pieces, first_masks, tokens)
    reply(first_masks, outgoing)
    *outgoing, own_rows = gather_rows(meta, wanted, layer, last_masks + [0], tokens)
    reply(last_masks, outgoing)
    late = [m for m in last_masks if m > 1]
    early = first_replies(
        meta, code, {0: own_rows, **{m: r for m, r in replies.items() if m not in late}}, tokens
    )
    refined = finish_rows(
        meta,
        code,
        confidence.reshape(strips, LANES),
        layer,
        early,
        {m: replies[m] for m in late},
        tokens,
    )
    return refined.reshape(local_views, tokens, sub)


def reply_order(peers):
    far_half = list(range(peers // 2, peers))
    far_half = far_half[len(far_half) // 2 :] + far_half[: len(far_half) // 2]
    pairs = zip(far_half[: len(far_half) // 2], far_half[len(far_half) // 2 :])
    return [m for pair in pairs for m in pair], list(range(2, peers // 2)) + [1]


def solution(mesh):
    in_specs = (
        P("views", None, None),
        P(),
        P(None, None, "heads"),
        P("heads", None),
        P(),
        P("views", None),
        P("views"),
        P("views"),
    )
    out_specs = P("views", None, "heads")
    return jax.shard_map(
        per_device, mesh=mesh, in_specs=in_specs, out_specs=out_specs, check_vma=False
    )
```

```python
import jax
import jax.numpy as jnp
from jax import lax
from jax.experimental import pallas as pl
from jax.experimental.pallas import tpu as pltpu
from jax.sharding import PartitionSpec as P


VIEWS, HEADS = "views", "heads"
HEAD_DIM = 64
LANES = 128
CHUNKS = dict(a=(1, 2), b=(0,), c=(3,))

coupling = 0.5
epsilon = 1e-06

bf16 = jnp.bfloat16
f32 = jnp.float32


def cost(flops, bytes_accessed, transcendentals=0):
    return pl.CostEstimate(
        flops=int(flops), bytes_accessed=int(bytes_accessed), transcendentals=int(transcendentals)
    )


def dot(a, b):
    return jnp.dot(a, b, preferred_element_type=f32)


VMEM_SPEC = pl.BlockSpec(memory_space=pltpu.VMEM)
SMEM_SPEC = pl.BlockSpec(memory_space=pltpu.SMEM)
ANY_SPEC = pl.BlockSpec(memory_space=pl.ANY)


def grant(mib):
    return pltpu.CompilerParams(vmem_limit_bytes=mib << 20)


def many(spec, count):
    return [spec] * count


def project_views(meta, latents, gain, w_qkv, w_out, which):
    _, tokens, width = latents.shape
    sub = w_qkv.shape[2]
    count = len(which)
    scale = HEAD_DIM ** (-0.5)
    order = (2, 0, 1)

    strip = sub // 2

    def body(meta_ref, lat_hbm, gain_hbm, w_hbm, w_out_hbm, *refs):
        outs, (halves, w_half, buffer, gains, ws, sems) = refs[: 2 * count], refs[2 * count :]
        mine = pl.ds(pl.multiple_of((meta_ref[0] % 2) * strip, strip), strip)
        w_copy = pltpu.make_async_copy(w_out_hbm.at[mine], w_half, sems.at[2 * count + 4])
        here = pl.ds(pl.multiple_of((meta_ref[1] // 2) * (width // 2), width // 2), width // 2)
        kept = [
            pltpu.make_async_copy(buffer.at[i, :, here], halves.at[i], sems.at[count + 4 + i])
            for i in range(count)
        ]
        copies = [
            pltpu.make_async_copy(lat_hbm.at[v], buffer.at[i], sems.at[i])
            for i, v in enumerate(which)
        ]
        gain_copy = pltpu.make_async_copy(gain_hbm, gains, sems.at[count])
        w_copies = {
            part: pltpu.make_async_copy(w_hbm.at[part], ws.at[part], sems.at[count + 1 + part])
            for part in order
        }
        for copy in [gain_copy, copies[0]] + [w_copies[p] for p in order] + copies[1:] + [w_copy]:
            copy.start()

        def load_norm(i):
            copies[i].wait()
            kept[i].start()
            wide = buffer[i].astype(f32)
            mean_square = jnp.mean(wide * wide, axis=-1, keepdims=True)
            return (wide * lax.rsqrt(mean_square + epsilon) * gains[...]).astype(bf16)

        gain_copy.wait()
        following = load_norm(0)
        for i in range(count):
            normed = following
            if i == 0:
                w_copies[2].wait()
            elif i + 1 < count:
                following = load_norm(i + 1)
            values = dot(normed, ws[2])
            if i == 0:
                w_copies[0].wait()
            queries = dot(normed, ws[0])
            if i == 0:
                w_copies[1].wait()
                following = load_norm(i + 1)
            outs[2 * i + 1][0] = dot(normed, ws[1]).astype(bf16)
            outs[2 * i + 1][1] = jnp.transpose(values).astype(bf16)
            outs[2 * i][...] = jnp.transpose(queries).astype(bf16) * jnp.asarray(scale, bf16)
        w_copy.wait()
        for copy in kept:
            copy.wait()

    out_shape = []
    for _ in which:
        out_shape += [
            jax.ShapeDtypeStruct((sub, tokens), bf16),
            jax.ShapeDtypeStruct((2, tokens, sub), bf16),
        ]
    out_shape.append(jax.ShapeDtypeStruct((count, tokens, width // 2), bf16))
    out_shape.append(jax.ShapeDtypeStruct((strip, w_out.shape[1]), bf16))
    outs = pl.pallas_call(
        body,
        in_specs=[SMEM_SPEC] + many(ANY_SPEC, 4),
        out_specs=many(VMEM_SPEC, len(out_shape)),
        out_shape=out_shape,
        scratch_shapes=[
            pltpu.VMEM((count, tokens, width), bf16),
            pltpu.VMEM((1, width), f32),
            pltpu.VMEM((3, width, sub), bf16),
            pltpu.SemaphoreType.DMA((2 * count + 5,)),
        ],
        name="proj",
        compiler_params=grant(52),
        cost_estimate=cost(
            count * 6 * tokens * width * sub, count * tokens * (width + 3 * sub) * 2 + 6 * width * sub
        ),
    )(meta, latents, gain, w_qkv, w_out)
    return {v: (outs[2 * i], outs[2 * i + 1]) for i, v in enumerate(which)}, outs[-2], outs[-1]


ONES = 16
SAFE_TOTAL = 1e30
FAR = 1e30


def head_scores(q_ref, kv_ref, h):
    per = LANES // HEAD_DIM
    j, slot = h // per, h % per
    own = q_ref[h * HEAD_DIM : (h + 1) * HEAD_DIM, :]
    zero = jnp.zeros_like(own)
    padded = jnp.concatenate([own if s == slot else zero for s in range(per)], axis=0)
    return dot(kv_ref[0, :, j * LANES : (j + 1) * LANES], padded)


def head_values(kv_ref, h):
    rows = kv_ref[1, h * HEAD_DIM : (h + 1) * HEAD_DIM, :]
    return jnp.concatenate([rows, jnp.ones((ONES, rows.shape[1]), bf16)], axis=0)


def attention_cost(tokens, sub, pairs):
    heads = sub // HEAD_DIM
    return cost(
        pairs * heads * tokens * tokens * 4 * LANES,
        pairs * tokens * sub * 8,
        pairs * heads * tokens * tokens,
    )


def far_if_absent(inter_ref, at, offset):
    return jnp.where(inter_ref[offset, at] > 0, 0.0, FAR).astype(f32)


def sources_of(view, local_views, window):
    found = []
    for o in range(window):
        if view + o + 1 < local_views:
            found.append((view + o + 1, view, o))
        if view - o - 1 >= 0:
            found.append((view - o - 1, view - o - 1, o))
    return found


def attend(
    meta, inter, queries, blocks, remote, plan, window, earlier=None, last=True, merged=False
):
    local_views = len(blocks)
    sub, tokens = queries[0].shape
    heads = sub // HEAD_DIM
    tall = HEAD_DIM + ONES
    views_total = inter.shape[1]
    names = sorted(remote)
    count = len(plan)
    held = 0 if earlier is None else 2

    def body(meta_ref, inter_ref, *refs):
        before, refs = refs[:held], refs[held:]
        qs, refs = refs[:count], refs[count:]
        kvs, refs = refs[:local_views], refs[local_views:]
        far_kvs, refs = dict(zip(names, refs[: len(names)])), refs[len(names) :]
        first = meta_ref[0] * local_views

        def global_view(source):
            at = first + source
            return jnp.where(at < 0, at + views_total, at) if source < 0 else at

        def keys_of(i):
            view, sources = plan[i]
            keys = [] if held else [(kvs[view], None, None)]
            if not held:
                keys += [(kvs[t], source, o) for t, source, o in sources_of(view, local_views, window)]
            return keys + [(far_kvs[name], source, o) for name, source, o in sources]

        if last:
            outs = [refs[0].at[i] for i in range(count)] if merged else refs[:count]
        units = [(i, h, k) for i in range(count) for h in range(heads) for k in keys_of(i)]
        far = {}
        for _, _, (_, source, o) in units:
            if source is not None and (source, o) not in far:
                far[source, o] = far_if_absent(inter_ref, global_view(source), o)
        upcoming = head_scores(qs[units[0][0]], units[0][2][0], units[0][1])
        worst = jnp.zeros((1, tokens), f32)
        n = 0
        for i, (view, _) in enumerate(plan):
            parts = []
            for h in range(heads):
                keys = keys_of(i)
                weights = []
                top = before[1][i, h : h + 1, :] if held else None
                for _, source, o in keys:
                    scores = upcoming
                    n += 1
                    if n < len(units):
                        ni, nh, (nk, _, _) = units[n]
                        upcoming = head_scores(qs[ni], nk, nh)
                    if source is None:
                        top = jnp.max(scores, axis=0, keepdims=True)
                        shift = top
                    else:
                        shift = top + far[source, o]
                    weights.append(jnp.exp(scores - shift).astype(bf16))
                values = jnp.concatenate([head_values(k[0], h) for k in keys], axis=1)
                sums = dot(values, jnp.concatenate(weights, axis=0))
                if held:
                    sums = sums + before[0][i, h * tall : (h + 1) * tall, :]
                if not last:
                    refs[0][i, h * tall : (h + 1) * tall, :] = sums
                    refs[1][i, h : h + 1, :] = top
                    continue
                total = sums[HEAD_DIM : HEAD_DIM + 1, :]
                worst = jnp.maximum(worst, jnp.where(total < SAFE_TOTAL, 0.0, 1.0))
                parts.append(sums[:HEAD_DIM, :] * (1.0 / total))
            if last:
                outs[i][...] = jnp.transpose(jnp.concatenate(parts, axis=0)).astype(bf16)
        if not last:
            return
        work, work_stat = refs[-2:]

        @pl.when(jnp.max(worst) > 0.0)
        def _():
            for i, (view, sources) in enumerate(plan):
                exact_add(qs[i], kvs[view], work, work_stat, heads, True)
                every = [(kvs[t], s, o) for t, s, o in sources_of(view, local_views, window)]
                every += [(far_kvs[name], s, o) for name, s, o in sources]
                for kv, source, o in every:

                    @pl.when(inter_ref[o, global_view(source)] > 0)
                    def _(i=i, kv=kv):
                        exact_add(qs[i], kv, work, work_stat, heads, False)

                parts = []
                for h in range(heads):
                    total = work_stat[h, 1:2, :]
                    parts.append(work[h * HEAD_DIM : (h + 1) * HEAD_DIM, :] * (1.0 / total))
                outs[i][...] = jnp.transpose(jnp.concatenate(parts, axis=0)).astype(bf16)

    if last:
        out_shape = [jax.ShapeDtypeStruct((tokens, sub), bf16)] * count
        if merged:
            out_shape = [jax.ShapeDtypeStruct((count, tokens, sub), bf16)]
        scratch = [pltpu.VMEM((sub, tokens), f32), pltpu.VMEM((heads, 8, tokens), f32)]
    else:
        out_shape = [
            jax.ShapeDtypeStruct((count, heads * tall, tokens), f32),
            jax.ShapeDtypeStruct((count, heads, tokens), f32),
        ]
        scratch = []
    pairs = sum(len(s) for _, s in plan)
    if not held:
        pairs += sum(1 + len(sources_of(v, local_views, window)) for v, _ in plan)
    return pl.pallas_call(
        body,
        in_specs=[SMEM_SPEC, SMEM_SPEC]
        + many(VMEM_SPEC, held + count + local_views + len(names)),
        out_specs=many(VMEM_SPEC, len(out_shape)),
        out_shape=out_shape,
        scratch_shapes=scratch,
        name="att",
        compiler_params=grant(12),
        cost_estimate=attention_cost(tokens, sub, pairs),
    )(
        meta,
        inter,
        *(earlier or ()),
        *queries,
        *[blocks[v] for v in range(local_views)],
        *[remote[name] for name in names],
    )


def exact_add(q_ref, kv_ref, work, work_stat, heads, start):
    per = LANES // HEAD_DIM

    def one_head(h, _):
        base = pl.multiple_of((h // per) * LANES, LANES)
        queries = q_ref[pl.ds(base, LANES), :]
        owner = lax.broadcasted_iota(jnp.int32, queries.shape, 0) // HEAD_DIM
        queries = jnp.where(owner == h % per, queries.astype(f32), 0.0).astype(bf16)
        scores = dot(kv_ref[0, :, pl.ds(base, LANES)], queries)
        top = jnp.max(scores, axis=0, keepdims=True)
        rows = pl.ds(pl.multiple_of(h * HEAD_DIM, HEAD_DIM), HEAD_DIM)
        values = kv_ref[1, rows, :]
        if not start:
            old = work_stat[h, 0:1, :]
            top = jnp.maximum(old, top)
        weights = jnp.exp(scores - top)
        total = jnp.sum(weights, axis=0, keepdims=True)
        sums = dot(values, weights.astype(bf16))
        if not start:
            fade = jnp.exp(old - top)
            total = total + work_stat[h, 1:2, :] * fade
            sums = sums + work[rows, :] * fade
        work_stat[h, 0:1, :] = top
        work_stat[h, 1:2, :] = total
        work[rows, :] = sums
        return 0

    lax.fori_loop(0, heads, one_head, 0)


def partial_out(meta, attended, near, w_own, w_mine, w_theirs, halves, places):
    sub = attended.shape[-1]
    rows_all = attended.size // sub
    width = w_own.shape[1]
    half = width // 2

    def body(meta_ref, att, near_ref, own_ref, mine_ref, theirs_ref, halves_ref, keep, send):
        side = meta_ref[1] // 2
        here = pl.ds(pl.multiple_of(side * half, half), half)
        away = pl.ds(pl.multiple_of((1 - side) * half, half), half)
        second = meta_ref[0] % 2
        strip = sub // 2
        lead = (slice(None),) * (len(attended.shape) - 1)
        mine = near_ref[lead + (pl.ds(pl.multiple_of(second * strip, strip), strip),)]
        theirs = near_ref[lead + (pl.ds(pl.multiple_of((1 - second) * strip, strip), strip),)]
        rows = jnp.concatenate(
            [x.reshape(rows_all, x.shape[-1]) for x in (att[...], mine, theirs)], axis=1
        )

        def columns(at):
            return jnp.concatenate([own_ref[:, at], mine_ref[:, at], theirs_ref[:, at]], axis=0)

        send[...] = dot(rows, columns(away)).astype(bf16)
        total = dot(rows, columns(here))
        base = jnp.concatenate([halves_ref[p] for p in places], axis=0)
        keep[...] = base.astype(f32) + total

    return pl.pallas_call(
        body,
        in_specs=[SMEM_SPEC] + many(VMEM_SPEC, 6),
        out_specs=many(VMEM_SPEC, 2),
        out_shape=[
            jax.ShapeDtypeStruct((rows_all, half), f32),
            jax.ShapeDtypeStruct((rows_all, half), bf16),
        ],
        name="part",
        compiler_params=grant(12),
        cost_estimate=cost(4 * rows_all * sub * width, 4 * sub * width + rows_all * width * 6),
    )(meta, attended, near, w_own, w_mine, w_theirs, halves)


def merge_out(meta, keep, got):
    rows_all, half = keep.shape
    sub = half // 2

    def body(meta_ref, keep_ref, got_ref, own, other):
        layer = (keep_ref[...] + got_ref[...].astype(f32)).astype(bf16)
        low, high = layer[:, :sub], layer[:, sub:]
        odd = meta_ref[1] % 2 == 1
        own[...] = jnp.where(odd, high, low)
        other[...] = jnp.where(odd, low, high)

    return pl.pallas_call(
        body,
        in_specs=[SMEM_SPEC] + many(VMEM_SPEC, 2),
        out_specs=many(VMEM_SPEC, 2),
        out_shape=[jax.ShapeDtypeStruct((rows_all, sub), bf16)] * 2,
        name="merge",
        compiler_params=grant(8),
        cost_estimate=cost(rows_all * half * 2, rows_all * half * 8),
    )(meta, keep, got)


def prepare_requests(block_rows, token_rows, peers, capacity):
    strips, lanes = block_rows.shape

    def body(block_ref, token_ref, wanted_ref, code_ref):
        before = (
            lax.broadcasted_iota(jnp.int32, (lanes, lanes), 0)
            < lax.broadcasted_iota(jnp.int32, (lanes, lanes), 1)
        ).astype(bf16)
        peer_ids = lax.broadcasted_iota(jnp.int32, (peers, lanes), 0)
        carry = jnp.zeros((peers, 1), f32)
        slots, lefts = [], []
        for i in range(strips):
            block = block_ref[i : i + 1, :]
            hit = (peer_ids == block).astype(f32)
            rank = dot(hit.astype(bf16), before) + carry
            carry = carry + jnp.sum(hit, axis=1, keepdims=True)
            slot = jnp.sum(rank * hit, axis=0, keepdims=True)
            slots.append(slot)
            code_ref[i : i + 1, :] = block * capacity + slot.astype(jnp.int32)
            token = token_ref[i : i + 1, :]
            coarse = (token // 32).astype(f32)
            fine = (token % 32).astype(f32)
            lefts.append(jnp.concatenate([hit * coarse, hit * fine], axis=0).astype(bf16))
        columns = jnp.transpose(jnp.concatenate(slots, axis=0))
        place = lax.broadcasted_iota(jnp.int32, (lanes, capacity), 1).astype(f32)
        total = jnp.zeros((2 * peers, capacity), f32)
        for i in range(strips):
            spot = (columns[:, i : i + 1] == place).astype(bf16)
            total = total + dot(lefts[i], spot)
        wanted_ref[...] = (total[:peers] * 32.0 + total[peers:]).astype(jnp.int32)

    return pl.pallas_call(
        body,
        in_specs=[VMEM_SPEC, VMEM_SPEC],
        out_specs=[VMEM_SPEC, VMEM_SPEC],
        out_shape=[
            jax.ShapeDtypeStruct((peers, capacity), jnp.int32),
            jax.ShapeDtypeStruct((strips, lanes), jnp.int32),
        ],
        name="prep",
        compiler_params=grant(8),
        cost_estimate=cost(2 * strips * lanes * lanes * capacity, 3 * strips * lanes * 4),
    )(block_rows, token_rows)


def spread_picks(spread, shift, width):
    clamped = jnp.minimum(jnp.maximum(spread - shift, -1.0), float(width)).astype(bf16)
    wide = jnp.concatenate([clamped] * (width // LANES), axis=1) if width > LANES else clamped[:, :width]
    place = lax.broadcasted_iota(jnp.int32, wide.shape, 1).astype(f32).astype(bf16)
    return jnp.where(wide == place, jnp.ones_like(place), jnp.zeros_like(place))


def gather_rows(meta, wanted, pieces, masks, tokens):
    peers, capacity = int(round(wanted.shape[0] ** 0.5)), wanted.shape[1]
    whole = not isinstance(pieces, list)
    flat = [pieces] if whole else [p for _, *pair in pieces for p in pair]
    sub = flat[0].shape[1]
    rows = flat[0].shape[0] if whole else sum(p.shape[0] for p in flat[::2])
    local_views = rows // tokens

    def body(meta_ref, wanted_ref, *refs):
        ins, outs = refs[: len(flat)], refs[len(flat) :]
        if whole:
            layer = ins[0]
        else:
            layer, outs = outs[0], outs[1:]
            end = jnp.logical_or(meta_ref[1] == 0, meta_ref[1] == meta_ref[2] - 1)
            for c, (views, _, _) in enumerate(pieces):
                for i, v in enumerate(views):
                    at = slice(i * tokens, (i + 1) * tokens)
                    layer[v * tokens : (v + 1) * tokens, :] = jnp.where(
                        end, ins[2 * c + 1][at, :], ins[2 * c][at, :]
                    )
        lines = [wanted_ref[pl.ds(m * peers + meta_ref[0], 1), :] for m in masks]
        lines += [lines[0]] * (-len(lines) % 8)
        columns = jnp.transpose(jnp.concatenate(lines, axis=0).astype(f32))
        for n in range(len(masks)):
            spread = jnp.broadcast_to(columns[:, n : n + 1], (capacity, LANES))
            pick = jnp.concatenate(
                [spread_picks(spread, float(v * tokens), tokens) for v in range(local_views)], axis=1
            )
            outs[n][...] = dot(pick, layer[...]).astype(bf16)

    out_shape = [jax.ShapeDtypeStruct((capacity, sub), bf16)] * len(masks)
    if not whole:
        out_shape = [jax.ShapeDtypeStruct((rows, sub), bf16)] + out_shape
    return pl.pallas_call(
        body,
        in_specs=[SMEM_SPEC] + many(VMEM_SPEC, 1 + len(flat)),
        out_specs=many(VMEM_SPEC, len(out_shape)),
        out_shape=out_shape,
        name="gath",
        compiler_params=grant(12),
        cost_estimate=cost(
            2 * len(masks) * capacity * rows * sub, 2 * (rows + len(masks) * capacity) * sub * 2
        ),
    )(meta, wanted, *flat)


def fetched_part(meta_ref, code_spread, masks, reps, capacity):
    pick = jnp.concatenate(
        [
            spread_picks(
                code_spread, (lax.bitwise_xor(meta_ref[0], mask) * capacity).astype(f32), capacity
            )
            for mask in masks
        ],
        axis=1,
    )
    return dot(pick, jnp.concatenate([r[...] for r in reps], axis=0))


def spread_column(turned, g, per, lanes):
    return jnp.concatenate(
        [
            jnp.broadcast_to(turned[:, g * per + j : g * per + j + 1], (lanes, LANES))
            for j in range(per)
        ],
        axis=0,
    )


def first_replies(meta, code, replies, tokens):
    masks = sorted(replies)
    capacity, sub = replies[masks[0]].shape
    strips, lanes = code.shape
    rows = strips * lanes
    per = tokens // lanes

    def body(meta_ref, code_ref, *refs):
        codes = jnp.transpose(code_ref[...].astype(f32))
        for g in range(rows // tokens):
            refs[-1][g * tokens : (g + 1) * tokens, :] = fetched_part(
                meta_ref, spread_column(codes, g, per, lanes), masks, refs[:-1], capacity
            ).astype(bf16)

    return pl.pallas_call(
        body,
        in_specs=[SMEM_SPEC] + many(VMEM_SPEC, 1 + len(masks)),
        out_specs=VMEM_SPEC,
        out_shape=jax.ShapeDtypeStruct((rows, sub), bf16),
        name="first",
        compiler_params=grant(12),
        cost_estimate=cost(2 * len(masks) * capacity * rows * sub, rows * sub * 4),
    )(meta, code, *[replies[m] for m in masks])


def finish_rows(meta, code, confidence, layer, early, replies, tokens):
    rows, sub = layer.shape
    masks = sorted(replies)
    capacity = replies[masks[0]].shape[0]
    _, lanes = code.shape
    blocks = rows // tokens
    per = tokens // lanes

    def body(meta_ref, code_ref, conf_ref, layer_ref, early_ref, *refs):
        reps, (out_hbm, buffer, sems) = refs[: len(masks)], refs[len(masks) :]
        codes = jnp.transpose(code_ref[...].astype(f32))
        confs = jnp.transpose(conf_ref[...]) * coupling
        copies = []
        for g in range(blocks):
            at = slice(g * tokens, (g + 1) * tokens)
            fetched = early_ref[at, :].astype(f32) + fetched_part(
                meta_ref, spread_column(codes, g, per, lanes), masks, reps, capacity
            )
            wide = layer_ref[at, :].astype(f32)
            weight = jnp.concatenate([spread_column(confs, g, per, lanes)] * (sub // LANES), axis=1)
            buffer[g] = wide + weight * (fetched - wide)
            copies.append(
                pltpu.make_async_copy(
                    buffer.at[g], out_hbm.at[pl.ds(g * tokens, tokens), :], sems.at[g]
                )
            )
            copies[-1].start()
        for copy in copies:
            copy.wait()

    return pl.pallas_call(
        body,
        in_specs=[SMEM_SPEC] + many(VMEM_SPEC, 4 + len(masks)),
        out_specs=ANY_SPEC,
        out_shape=jax.ShapeDtypeStruct((rows, sub), f32),
        scratch_shapes=[
            pltpu.VMEM((blocks, tokens, sub), f32),
            pltpu.SemaphoreType.DMA((blocks,)),
        ],
        name="fin",
        compiler_params=grant(12),
        cost_estimate=cost(2 * len(masks) * capacity * rows * sub, rows * sub * 8),
    )(meta, code, confidence, layer, early, *[replies[m] for m in masks])


def per_device(latents, norm_gain, w_qkv, w_out, intersection, match_block, match_row, confidence):
    local_views, tokens, width = latents.shape
    window = intersection.shape[1]
    sub = w_qkv.shape[2]
    peers = lax.axis_size(VIEWS)
    ends = lax.axis_size(HEADS)
    rows = local_views * tokens
    capacity = 2 * rows // peers
    assert local_views == 4 and window == 2 and ends == 4 and tokens == sub
    view_at, head_at = lax.axis_index(VIEWS), lax.axis_index(HEADS)
    spot = jnp.arange(4, dtype=jnp.int32)
    meta = jnp.where(spot == 0, view_at, jnp.where(spot == 1, head_at, ends)).astype(jnp.int32)

    def along(x, by):
        return lax.ppermute(x, VIEWS, [(i, (i + by) % peers) for i in range(peers)])

    def partner(x, mask):
        return lax.ppermute(x, VIEWS, [(i, i ^ mask) for i in range(peers)])

    def across(x, pairs):
        return lax.ppermute(x, HEADS, pairs)

    def after(x, done):
        return lax.optimization_barrier((x, done))[0]

    beside, middle, back = [(0, 1), (3, 2)], [(1, 2), (2, 1)], [(1, 0), (2, 3)]
    gain = norm_gain.reshape(1, width)
    inter = intersection.T
    loaded = (0, 3, 1, 2)
    projected, halves, w_half = project_views(meta, latents, gain, w_qkv, w_out, loaded)
    queries = {v: projected[v][0] for v in range(local_views)}
    blocks = {v: projected[v][1] for v in range(local_views)}
    far = {}
    far["n1"] = along(blocks[0], -1)
    far["p1"] = along(blocks[3], 1)
    w_mine = across(w_half, beside)

    inner_plan = [(1, [("p1", -1, 1)]), (2, [("n1", 2, 1)])]
    inner_queries = [queries[1], queries[2]]
    local = attend(
        meta, inter, inner_queries, blocks, {}, [(v, []) for v, _ in inner_plan], window, last=False
    )
    inner_far = dict(far)
    far["n2"] = along(after(blocks[1], local[0]), -1)
    far["p2"] = along(after(blocks[2], local[0]), 1)
    attended = {}
    (attended["a"],) = attend(
        meta,
        inter,
        inner_queries,
        blocks,
        inner_far,
        inner_plan,
        window,
        earlier=tuple(local),
        merged=True,
    )
    w_theirs = partner(after(w_mine, attended["a"]), 1)

    def attend_outer(view, sources, done):
        (result,) = attend(
            meta,
            inter,
            [after(queries[view], done)],
            blocks,
            {s[0]: far[s[0]] for s in sources},
            [(view, sources)],
            window,
        )
        return result

    keep, sent, got = {}, {}, {}

    def pass_on(c):
        near = across(attended[c], beside)
        keep[c], sent[c] = partial_out(
            meta,
            attended[c],
            near,
            w_out,
            w_mine,
            w_theirs,
            halves,
            [loaded.index(v) for v in CHUNKS[c]],
        )
        got[c] = across(sent[c], middle)

    attended["b"] = attend_outer(0, [("p1", -1, 0), ("p2", -2, 1)], attended["a"])
    pass_on("a")
    attended["c"] = attend_outer(3, [("n1", 3, 0), ("n2", 3, 1)], sent["a"])
    pass_on("b")
    pass_on("c")
    strips = rows // LANES
    wanted, code = prepare_requests(
        after(match_block.reshape(strips, LANES), sent["c"]),
        match_row.reshape(strips, LANES),
        peers,
        capacity,
    )
    mask = 1
    while mask < peers:
        wanted = jnp.concatenate([wanted, partner(wanted, mask)], axis=0)
        mask *= 2
    pieces = []
    for c in CHUNKS:
        own, other = merge_out(meta, keep[c], got[c])
        pieces.append((CHUNKS[c], own, across(other, back)))

    first_masks, last_masks = reply_order(peers)
    replies = {}

    def reply(masks, outgoing):
        for mask, rows_out in zip(masks, outgoing):
            replies[mask] = partner(rows_out, mask)

    layer, *outgoing = gather_rows(meta, wanted, pieces, first_masks, tokens)
    reply(first_masks, outgoing)
    *outgoing, own_rows = gather_rows(meta, wanted, layer, last_masks + [0], tokens)
    reply(last_masks, outgoing)
    late = [m for m in last_masks if m > 1]
    early = first_replies(
        meta, code, {0: own_rows, **{m: r for m, r in replies.items() if m not in late}}, tokens
    )
    refined = finish_rows(
        meta,
        code,
        confidence.reshape(strips, LANES),
        layer,
        early,
        {m: replies[m] for m in late},
        tokens,
    )
    return refined.reshape(local_views, tokens, sub)


def reply_order(peers):
    far_half = list(range(peers // 2, peers))
    far_half = far_half[len(far_half) // 2 :] + far_half[: len(far_half) // 2]
    pairs = zip(far_half[: len(far_half) // 2], far_half[len(far_half) // 2 :])
    return [m for pair in pairs for m in pair], list(range(2, peers // 2)) + [1]


def solution(mesh):
    in_specs = (
        P(VIEWS, None, None),
        P(),
        P(None, None, HEADS),
        P(HEADS, None),
        P(),
        P(VIEWS, None),
        P(VIEWS),
        P(VIEWS),
    )
    out_specs = P(VIEWS, None, HEADS)
    return jax.shard_map(
        per_device, mesh=mesh, in_specs=in_specs, out_specs=out_specs, check_vma=False
    )
```

```python
import jax
import jax.numpy as jnp
from jax import lax
from jax.experimental import pallas as pl
from jax.experimental.pallas import tpu as pltpu
from jax.sharding import PartitionSpec as P


VIEWS, HEADS = "views", "heads"
HEAD_DIM = 64
LANES = 128
CHUNKS = dict(a=(1,), b=(2, 0), c=(3,))

coupling = 0.5
epsilon = 1e-06

bf16 = jnp.bfloat16
f32 = jnp.float32


def cost(flops, bytes_accessed, transcendentals=0):
    return pl.CostEstimate(
        flops=int(flops), bytes_accessed=int(bytes_accessed), transcendentals=int(transcendentals)
    )


def dot(a, b):
    return jnp.dot(a, b, preferred_element_type=f32)


VMEM_SPEC = pl.BlockSpec(memory_space=pltpu.VMEM)
SMEM_SPEC = pl.BlockSpec(memory_space=pltpu.SMEM)
ANY_SPEC = pl.BlockSpec(memory_space=pl.ANY)


def grant(mib):
    return pltpu.CompilerParams(vmem_limit_bytes=mib << 20)


def many(spec, count):
    return [spec] * count


def project_views(meta, latents, gain, w_qkv, w_out, which):
    _, tokens, width = latents.shape
    sub = w_qkv.shape[2]
    count = len(which)
    scale = HEAD_DIM ** (-0.5)
    order = (2, 0, 1)

    strip = sub // 2

    def body(meta_ref, lat_hbm, gain_hbm, w_hbm, w_out_hbm, *refs):
        outs, (halves, w_half, buffer, gains, ws, sems) = refs[: 2 * count], refs[2 * count :]
        mine = pl.ds(pl.multiple_of((meta_ref[0] % 2) * strip, strip), strip)
        w_copy = pltpu.make_async_copy(w_out_hbm.at[mine], w_half, sems.at[2 * count + 4])
        here = pl.ds(pl.multiple_of((meta_ref[1] // 2) * (width // 2), width // 2), width // 2)
        kept = [
            pltpu.make_async_copy(buffer.at[i, :, here], halves.at[i], sems.at[count + 4 + i])
            for i in range(count)
        ]
        copies = [
            pltpu.make_async_copy(lat_hbm.at[v], buffer.at[i], sems.at[i])
            for i, v in enumerate(which)
        ]
        gain_copy = pltpu.make_async_copy(gain_hbm, gains, sems.at[count])
        w_copies = {
            part: pltpu.make_async_copy(w_hbm.at[part], ws.at[part], sems.at[count + 1 + part])
            for part in order
        }
        for copy in [gain_copy, copies[0]] + [w_copies[p] for p in order] + copies[1:] + [w_copy]:
            copy.start()

        def load_norm(i):
            copies[i].wait()
            kept[i].start()
            wide = buffer[i].astype(f32)
            mean_square = jnp.mean(wide * wide, axis=-1, keepdims=True)
            return (wide * lax.rsqrt(mean_square + epsilon) * gains[...]).astype(bf16)

        gain_copy.wait()
        following = load_norm(0)
        for i in range(count):
            normed = following
            if i == 0:
                w_copies[2].wait()
            elif i + 1 < count:
                following = load_norm(i + 1)
            values = dot(normed, ws[2])
            if i == 0:
                w_copies[0].wait()
            queries = dot(normed, ws[0])
            if i == 0:
                w_copies[1].wait()
                following = load_norm(i + 1)
            outs[2 * i + 1][0] = dot(normed, ws[1]).astype(bf16)
            outs[2 * i + 1][1] = jnp.transpose(values).astype(bf16)
            outs[2 * i][...] = jnp.transpose(queries).astype(bf16) * jnp.asarray(scale, bf16)
        w_copy.wait()
        for copy in kept:
            copy.wait()

    out_shape = []
    for _ in which:
        out_shape += [
            jax.ShapeDtypeStruct((sub, tokens), bf16),
            jax.ShapeDtypeStruct((2, tokens, sub), bf16),
        ]
    out_shape.append(jax.ShapeDtypeStruct((count, tokens, width // 2), bf16))
    out_shape.append(jax.ShapeDtypeStruct((strip, w_out.shape[1]), bf16))
    outs = pl.pallas_call(
        body,
        in_specs=[SMEM_SPEC] + many(ANY_SPEC, 4),
        out_specs=many(VMEM_SPEC, len(out_shape)),
        out_shape=out_shape,
        scratch_shapes=[
            pltpu.VMEM((count, tokens, width), bf16),
            pltpu.VMEM((1, width), f32),
            pltpu.VMEM((3, width, sub), bf16),
            pltpu.SemaphoreType.DMA((2 * count + 5,)),
        ],
        name="proj",
        compiler_params=grant(52),
        cost_estimate=cost(
            count * 6 * tokens * width * sub, count * tokens * (width + 3 * sub) * 2 + 6 * width * sub
        ),
    )(meta, latents, gain, w_qkv, w_out)
    return {v: (outs[2 * i], outs[2 * i + 1]) for i, v in enumerate(which)}, outs[-2], outs[-1]


ONES = 16
SAFE_TOTAL = 1e30
FAR = 1e30


def head_scores(q_ref, kv_ref, h):
    per = LANES // HEAD_DIM
    j, slot = h // per, h % per
    own = q_ref[h * HEAD_DIM : (h + 1) * HEAD_DIM, :]
    zero = jnp.zeros_like(own)
    padded = jnp.concatenate([own if s == slot else zero for s in range(per)], axis=0)
    return dot(kv_ref[0, :, j * LANES : (j + 1) * LANES], padded)


def head_values(kv_ref, h):
    rows = kv_ref[1, h * HEAD_DIM : (h + 1) * HEAD_DIM, :]
    return jnp.concatenate([rows, jnp.ones((ONES, rows.shape[1]), bf16)], axis=0)


def attention_cost(tokens, sub, pairs):
    heads = sub // HEAD_DIM
    return cost(
        pairs * heads * tokens * tokens * 4 * LANES,
        pairs * tokens * sub * 8,
        pairs * heads * tokens * tokens,
    )


def far_if_absent(inter_ref, at, offset):
    return jnp.where(inter_ref[offset, at] > 0, 0.0, FAR).astype(f32)


def sources_of(view, local_views, window):
    found = []
    for o in range(window):
        if view + o + 1 < local_views:
            found.append((view + o + 1, view, o))
        if view - o - 1 >= 0:
            found.append((view - o - 1, view - o - 1, o))
    return found


def attend(
    meta, inter, queries, blocks, remote, plan, window, earlier=None, last=True, carry=None
):
    local_views = len(blocks)
    sub, tokens = queries[0].shape
    heads = sub // HEAD_DIM
    tall = HEAD_DIM + ONES
    views_total = inter.shape[1]
    names = sorted(remote)
    count = len(plan)
    held = 0 if earlier is None else 2

    def body(meta_ref, inter_ref, *refs):
        before, refs = refs[:held], refs[held:]
        qs, refs = refs[:count], refs[count:]
        kvs, refs = refs[:local_views], refs[local_views:]
        far_kvs, refs = dict(zip(names, refs[: len(names)])), refs[len(names) :]
        first = meta_ref[0] * local_views

        def global_view(source):
            at = first + source
            return jnp.where(at < 0, at + views_total, at) if source < 0 else at

        def keys_of(i):
            view, sources = plan[i]
            keys = [] if held else [(kvs[view], None, None)]
            if not held:
                keys += [(kvs[t], source, o) for t, source, o in sources_of(view, local_views, window)]
            return keys + [(far_kvs[name], source, o) for name, source, o in sources]

        if last and carry is not None:
            refs[1][0] = refs[0][...]
            outs, refs = [refs[1].at[1 + i] for i in range(count)], refs[1:]
        elif last:
            outs = refs[:count]
        units = [(i, h, k) for i in range(count) for h in range(heads) for k in keys_of(i)]
        far = {}
        for _, _, (_, source, o) in units:
            if source is not None and (source, o) not in far:
                far[source, o] = far_if_absent(inter_ref, global_view(source), o)
        upcoming = head_scores(qs[units[0][0]], units[0][2][0], units[0][1])
        worst = jnp.zeros((1, tokens), f32)
        n = 0
        for i, (view, _) in enumerate(plan):
            parts = []
            for h in range(heads):
                keys = keys_of(i)
                weights = []
                top = before[1][i, h : h + 1, :] if held else None
                for _, source, o in keys:
                    scores = upcoming
                    n += 1
                    if n < len(units):
                        ni, nh, (nk, _, _) = units[n]
                        upcoming = head_scores(qs[ni], nk, nh)
                    if source is None:
                        top = jnp.max(scores, axis=0, keepdims=True)
                        shift = top
                    else:
                        shift = top + far[source, o]
                    weights.append(jnp.exp(scores - shift).astype(bf16))
                values = jnp.concatenate([head_values(k[0], h) for k in keys], axis=1)
                sums = dot(values, jnp.concatenate(weights, axis=0))
                if held:
                    sums = sums + before[0][i, h * tall : (h + 1) * tall, :]
                if not last:
                    refs[0][i, h * tall : (h + 1) * tall, :] = sums
                    refs[1][i, h : h + 1, :] = top
                    continue
                total = sums[HEAD_DIM : HEAD_DIM + 1, :]
                worst = jnp.maximum(worst, jnp.where(total < SAFE_TOTAL, 0.0, 1.0))
                parts.append(sums[:HEAD_DIM, :] * (1.0 / total))
            if last:
                outs[i][...] = jnp.transpose(jnp.concatenate(parts, axis=0)).astype(bf16)
        if not last:
            return
        work, work_stat = refs[-2:]

        @pl.when(jnp.max(worst) > 0.0)
        def _():
            for i, (view, sources) in enumerate(plan):
                exact_add(qs[i], kvs[view], work, work_stat, heads, True)
                every = [(kvs[t], s, o) for t, s, o in sources_of(view, local_views, window)]
                every += [(far_kvs[name], s, o) for name, s, o in sources]
                for kv, source, o in every:

                    @pl.when(inter_ref[o, global_view(source)] > 0)
                    def _(i=i, kv=kv):
                        exact_add(qs[i], kv, work, work_stat, heads, False)

                parts = []
                for h in range(heads):
                    total = work_stat[h, 1:2, :]
                    parts.append(work[h * HEAD_DIM : (h + 1) * HEAD_DIM, :] * (1.0 / total))
                outs[i][...] = jnp.transpose(jnp.concatenate(parts, axis=0)).astype(bf16)

    if last:
        out_shape = [jax.ShapeDtypeStruct((tokens, sub), bf16)] * count
        if carry is not None:
            out_shape = [jax.ShapeDtypeStruct((1 + count, tokens, sub), bf16)]
        scratch = [pltpu.VMEM((sub, tokens), f32), pltpu.VMEM((heads, 8, tokens), f32)]
    else:
        out_shape = [
            jax.ShapeDtypeStruct((count, heads * tall, tokens), f32),
            jax.ShapeDtypeStruct((count, heads, tokens), f32),
        ]
        scratch = []
    pairs = sum(len(s) for _, s in plan)
    if not held:
        pairs += sum(1 + len(sources_of(v, local_views, window)) for v, _ in plan)
    return pl.pallas_call(
        body,
        in_specs=[SMEM_SPEC, SMEM_SPEC]
        + many(VMEM_SPEC, held + count + local_views + len(names) + (carry is not None)),
        out_specs=many(VMEM_SPEC, len(out_shape)),
        out_shape=out_shape,
        scratch_shapes=scratch,
        name="att",
        compiler_params=grant(12),
        cost_estimate=attention_cost(tokens, sub, pairs),
    )(
        meta,
        inter,
        *(earlier or ()),
        *queries,
        *[blocks[v] for v in range(local_views)],
        *[remote[name] for name in names],
        *(() if carry is None else (carry,)),
    )


def exact_add(q_ref, kv_ref, work, work_stat, heads, start):
    per = LANES // HEAD_DIM

    def one_head(h, _):
        base = pl.multiple_of((h // per) * LANES, LANES)
        queries = q_ref[pl.ds(base, LANES), :]
        owner = lax.broadcasted_iota(jnp.int32, queries.shape, 0) // HEAD_DIM
        queries = jnp.where(owner == h % per, queries.astype(f32), 0.0).astype(bf16)
        scores = dot(kv_ref[0, :, pl.ds(base, LANES)], queries)
        top = jnp.max(scores, axis=0, keepdims=True)
        rows = pl.ds(pl.multiple_of(h * HEAD_DIM, HEAD_DIM), HEAD_DIM)
        values = kv_ref[1, rows, :]
        if not start:
            old = work_stat[h, 0:1, :]
            top = jnp.maximum(old, top)
        weights = jnp.exp(scores - top)
        total = jnp.sum(weights, axis=0, keepdims=True)
        sums = dot(values, weights.astype(bf16))
        if not start:
            fade = jnp.exp(old - top)
            total = total + work_stat[h, 1:2, :] * fade
            sums = sums + work[rows, :] * fade
        work_stat[h, 0:1, :] = top
        work_stat[h, 1:2, :] = total
        work[rows, :] = sums
        return 0

    lax.fori_loop(0, heads, one_head, 0)


def partial_out(meta, attended, near, w_own, w_mine, w_theirs, halves, places):
    sub = attended.shape[-1]
    rows_all = attended.size // sub
    width = w_own.shape[1]
    half = width // 2

    def body(meta_ref, att, near_ref, own_ref, mine_ref, theirs_ref, halves_ref, keep, send):
        side = meta_ref[1] // 2
        here = pl.ds(pl.multiple_of(side * half, half), half)
        away = pl.ds(pl.multiple_of((1 - side) * half, half), half)
        second = meta_ref[0] % 2
        strip = sub // 2
        lead = (slice(None),) * (len(attended.shape) - 1)
        mine = near_ref[lead + (pl.ds(pl.multiple_of(second * strip, strip), strip),)]
        theirs = near_ref[lead + (pl.ds(pl.multiple_of((1 - second) * strip, strip), strip),)]
        rows = jnp.concatenate(
            [x.reshape(rows_all, x.shape[-1]) for x in (att[...], mine, theirs)], axis=1
        )

        def columns(at):
            return jnp.concatenate([own_ref[:, at], mine_ref[:, at], theirs_ref[:, at]], axis=0)

        send[...] = dot(rows, columns(away)).astype(bf16)
        total = dot(rows, columns(here))
        base = jnp.concatenate([halves_ref[p] for p in places], axis=0)
        keep[...] = base.astype(f32) + total

    return pl.pallas_call(
        body,
        in_specs=[SMEM_SPEC] + many(VMEM_SPEC, 6),
        out_specs=many(VMEM_SPEC, 2),
        out_shape=[
            jax.ShapeDtypeStruct((rows_all, half), f32),
            jax.ShapeDtypeStruct((rows_all, half), bf16),
        ],
        name="part",
        compiler_params=grant(12),
        cost_estimate=cost(4 * rows_all * sub * width, 4 * sub * width + rows_all * width * 6),
    )(meta, attended, near, w_own, w_mine, w_theirs, halves)


def merge_out(meta, keep, got):
    rows_all, half = keep.shape
    sub = half // 2

    def body(meta_ref, keep_ref, got_ref, own, other):
        layer = (keep_ref[...] + got_ref[...].astype(f32)).astype(bf16)
        low, high = layer[:, :sub], layer[:, sub:]
        odd = meta_ref[1] % 2 == 1
        own[...] = jnp.where(odd, high, low)
        other[...] = jnp.where(odd, low, high)

    return pl.pallas_call(
        body,
        in_specs=[SMEM_SPEC] + many(VMEM_SPEC, 2),
        out_specs=many(VMEM_SPEC, 2),
        out_shape=[jax.ShapeDtypeStruct((rows_all, sub), bf16)] * 2,
        name="merge",
        compiler_params=grant(8),
        cost_estimate=cost(rows_all * half * 2, rows_all * half * 8),
    )(meta, keep, got)


def prepare_requests(block_rows, token_rows, peers, capacity):
    strips, lanes = block_rows.shape

    def body(block_ref, token_ref, wanted_ref, code_ref):
        before = (
            lax.broadcasted_iota(jnp.int32, (lanes, lanes), 0)
            < lax.broadcasted_iota(jnp.int32, (lanes, lanes), 1)
        ).astype(bf16)
        peer_ids = lax.broadcasted_iota(jnp.int32, (peers, lanes), 0)
        carry = jnp.zeros((peers, 1), f32)
        slots, lefts = [], []
        for i in range(strips):
            block = block_ref[i : i + 1, :]
            hit = (peer_ids == block).astype(f32)
            rank = dot(hit.astype(bf16), before) + carry
            carry = carry + jnp.sum(hit, axis=1, keepdims=True)
            slot = jnp.sum(rank * hit, axis=0, keepdims=True)
            slots.append(slot)
            code_ref[i : i + 1, :] = block * capacity + slot.astype(jnp.int32)
            token = token_ref[i : i + 1, :]
            coarse = (token // 32).astype(f32)
            fine = (token % 32).astype(f32)
            lefts.append(jnp.concatenate([hit * coarse, hit * fine], axis=0).astype(bf16))
        columns = jnp.transpose(jnp.concatenate(slots, axis=0))
        place = lax.broadcasted_iota(jnp.int32, (lanes, capacity), 1).astype(f32)
        total = jnp.zeros((2 * peers, capacity), f32)
        for i in range(strips):
            spot = (columns[:, i : i + 1] == place).astype(bf16)
            total = total + dot(lefts[i], spot)
        wanted_ref[...] = (total[:peers] * 32.0 + total[peers:]).astype(jnp.int32)

    return pl.pallas_call(
        body,
        in_specs=[VMEM_SPEC, VMEM_SPEC],
        out_specs=[VMEM_SPEC, VMEM_SPEC],
        out_shape=[
            jax.ShapeDtypeStruct((peers, capacity), jnp.int32),
            jax.ShapeDtypeStruct((strips, lanes), jnp.int32),
        ],
        name="prep",
        compiler_params=grant(8),
        cost_estimate=cost(2 * strips * lanes * lanes * capacity, 3 * strips * lanes * 4),
    )(block_rows, token_rows)


def spread_picks(spread, shift, width):
    clamped = jnp.minimum(jnp.maximum(spread - shift, -1.0), float(width)).astype(bf16)
    wide = jnp.concatenate([clamped] * (width // LANES), axis=1) if width > LANES else clamped[:, :width]
    place = lax.broadcasted_iota(jnp.int32, wide.shape, 1).astype(f32).astype(bf16)
    return jnp.where(wide == place, jnp.ones_like(place), jnp.zeros_like(place))


def gather_rows(meta, wanted, pieces, masks, tokens):
    peers, capacity = int(round(wanted.shape[0] ** 0.5)), wanted.shape[1]
    whole = not isinstance(pieces, list)
    flat = [pieces] if whole else [p for _, *pair in pieces for p in pair]
    sub = flat[0].shape[1]
    rows = flat[0].shape[0] if whole else sum(p.shape[0] for p in flat[::2])
    local_views = rows // tokens

    def body(meta_ref, wanted_ref, *refs):
        ins, outs = refs[: len(flat)], refs[len(flat) :]
        if whole:
            layer = ins[0]
        else:
            layer, outs = outs[0], outs[1:]
            end = jnp.logical_or(meta_ref[1] == 0, meta_ref[1] == meta_ref[2] - 1)
            for c, (views, _, _) in enumerate(pieces):
                for i, v in enumerate(views):
                    at = slice(i * tokens, (i + 1) * tokens)
                    layer[v * tokens : (v + 1) * tokens, :] = jnp.where(
                        end, ins[2 * c + 1][at, :], ins[2 * c][at, :]
                    )
        lines = [wanted_ref[pl.ds(m * peers + meta_ref[0], 1), :] for m in masks]
        lines += [lines[0]] * (-len(lines) % 8)
        columns = jnp.transpose(jnp.concatenate(lines, axis=0).astype(f32))
        for n in range(len(masks)):
            spread = jnp.broadcast_to(columns[:, n : n + 1], (capacity, LANES))
            pick = jnp.concatenate(
                [spread_picks(spread, float(v * tokens), tokens) for v in range(local_views)], axis=1
            )
            outs[n][...] = dot(pick, layer[...]).astype(bf16)

    out_shape = [jax.ShapeDtypeStruct((capacity, sub), bf16)] * len(masks)
    if not whole:
        out_shape = [jax.ShapeDtypeStruct((rows, sub), bf16)] + out_shape
    return pl.pallas_call(
        body,
        in_specs=[SMEM_SPEC] + many(VMEM_SPEC, 1 + len(flat)),
        out_specs=many(VMEM_SPEC, len(out_shape)),
        out_shape=out_shape,
        name="gath",
        compiler_params=grant(12),
        cost_estimate=cost(
            2 * len(masks) * capacity * rows * sub, 2 * (rows + len(masks) * capacity) * sub * 2
        ),
    )(meta, wanted, *flat)


def fetched_part(meta_ref, code_spread, masks, reps, capacity):
    pick = jnp.concatenate(
        [
            spread_picks(
                code_spread, (lax.bitwise_xor(meta_ref[0], mask) * capacity).astype(f32), capacity
            )
            for mask in masks
        ],
        axis=1,
    )
    return dot(pick, jnp.concatenate([r[...] for r in reps], axis=0))


def spread_column(turned, g, per, lanes):
    return jnp.concatenate(
        [
            jnp.broadcast_to(turned[:, g * per + j : g * per + j + 1], (lanes, LANES))
            for j in range(per)
        ],
        axis=0,
    )


def first_replies(meta, code, replies, tokens):
    masks = sorted(replies)
    capacity, sub = replies[masks[0]].shape
    strips, lanes = code.shape
    rows = strips * lanes
    per = tokens // lanes

    def body(meta_ref, code_ref, *refs):
        codes = jnp.transpose(code_ref[...].astype(f32))
        for g in range(rows // tokens):
            refs[-1][g * tokens : (g + 1) * tokens, :] = fetched_part(
                meta_ref, spread_column(codes, g, per, lanes), masks, refs[:-1], capacity
            ).astype(bf16)

    return pl.pallas_call(
        body,
        in_specs=[SMEM_SPEC] + many(VMEM_SPEC, 1 + len(masks)),
        out_specs=VMEM_SPEC,
        out_shape=jax.ShapeDtypeStruct((rows, sub), bf16),
        name="first",
        compiler_params=grant(12),
        cost_estimate=cost(2 * len(masks) * capacity * rows * sub, rows * sub * 4),
    )(meta, code, *[replies[m] for m in masks])


def finish_rows(meta, code, confidence, layer, early, replies, tokens):
    rows, sub = layer.shape
    masks = sorted(replies)
    capacity = replies[masks[0]].shape[0]
    _, lanes = code.shape
    blocks = rows // tokens
    per = tokens // lanes

    def body(meta_ref, code_ref, conf_ref, layer_ref, early_ref, *refs):
        reps, (out_hbm, buffer, sems) = refs[: len(masks)], refs[len(masks) :]
        codes = jnp.transpose(code_ref[...].astype(f32))
        confs = jnp.transpose(conf_ref[...]) * coupling
        copies = []
        for g in range(blocks):
            at = slice(g * tokens, (g + 1) * tokens)
            fetched = early_ref[at, :].astype(f32) + fetched_part(
                meta_ref, spread_column(codes, g, per, lanes), masks, reps, capacity
            )
            wide = layer_ref[at, :].astype(f32)
            weight = jnp.concatenate([spread_column(confs, g, per, lanes)] * (sub // LANES), axis=1)
            buffer[g] = wide + weight * (fetched - wide)
            copies.append(
                pltpu.make_async_copy(
                    buffer.at[g], out_hbm.at[pl.ds(g * tokens, tokens), :], sems.at[g]
                )
            )
            copies[-1].start()
        for copy in copies:
            copy.wait()

    return pl.pallas_call(
        body,
        in_specs=[SMEM_SPEC] + many(VMEM_SPEC, 4 + len(masks)),
        out_specs=ANY_SPEC,
        out_shape=jax.ShapeDtypeStruct((rows, sub), f32),
        scratch_shapes=[
            pltpu.VMEM((blocks, tokens, sub), f32),
            pltpu.SemaphoreType.DMA((blocks,)),
        ],
        name="fin",
        compiler_params=grant(12),
        cost_estimate=cost(2 * len(masks) * capacity * rows * sub, rows * sub * 8),
    )(meta, code, confidence, layer, early, *[replies[m] for m in masks])


def per_device(latents, norm_gain, w_qkv, w_out, intersection, match_block, match_row, confidence):
    local_views, tokens, width = latents.shape
    window = intersection.shape[1]
    sub = w_qkv.shape[2]
    peers = lax.axis_size(VIEWS)
    ends = lax.axis_size(HEADS)
    rows = local_views * tokens
    capacity = 2 * rows // peers
    assert local_views == 4 and window == 2 and ends == 4 and tokens == sub
    view_at, head_at = lax.axis_index(VIEWS), lax.axis_index(HEADS)
    spot = jnp.arange(4, dtype=jnp.int32)
    meta = jnp.where(spot == 0, view_at, jnp.where(spot == 1, head_at, ends)).astype(jnp.int32)

    def along(x, by):
        return lax.ppermute(x, VIEWS, [(i, (i + by) % peers) for i in range(peers)])

    def partner(x, mask):
        return lax.ppermute(x, VIEWS, [(i, i ^ mask) for i in range(peers)])

    def across(x, pairs):
        return lax.ppermute(x, HEADS, pairs)

    def after(x, done):
        return lax.optimization_barrier((x, done))[0]

    beside, middle, back = [(0, 1), (3, 2)], [(1, 2), (2, 1)], [(1, 0), (2, 3)]
    gain = norm_gain.reshape(1, width)
    inter = intersection.T
    loaded = (0, 3, 1, 2)
    projected, halves, w_half = project_views(meta, latents, gain, w_qkv, w_out, loaded)
    queries = {v: projected[v][0] for v in range(local_views)}
    blocks = {v: projected[v][1] for v in range(local_views)}
    far = {}
    far["n1"] = along(blocks[0], -1)
    far["p1"] = along(blocks[3], 1)
    w_mine = across(w_half, beside)

    inner_plan = [(1, [("p1", -1, 1)]), (2, [("n1", 2, 1)])]
    inner_queries = [queries[1], queries[2]]
    local = attend(
        meta, inter, inner_queries, blocks, {}, [(v, []) for v, _ in inner_plan], window, last=False
    )
    inner_far = dict(far)
    far["n2"] = along(after(blocks[1], local[0]), -1)
    far["p2"] = along(after(blocks[2], local[0]), 1)
    attended = {}
    attended["a"], second = attend(
        meta, inter, inner_queries, blocks, inner_far, inner_plan, window, earlier=tuple(local)
    )
    w_theirs = partner(after(w_mine, attended["a"]), 1)

    def attend_outer(view, sources, done, carry=None):
        (result,) = attend(
            meta,
            inter,
            [after(queries[view], done)],
            blocks,
            {s[0]: far[s[0]] for s in sources},
            [(view, sources)],
            window,
            carry=carry,
        )
        return result

    keep, sent, got = {}, {}, {}

    def pass_on(c):
        near = across(attended[c], beside)
        keep[c], sent[c] = partial_out(
            meta,
            attended[c],
            near,
            w_out,
            w_mine,
            w_theirs,
            halves,
            [loaded.index(v) for v in CHUNKS[c]],
        )
        got[c] = across(sent[c], middle)

    attended["b"] = attend_outer(0, [("p1", -1, 0), ("p2", -2, 1)], attended["a"], second)
    pass_on("a")
    attended["c"] = attend_outer(3, [("n1", 3, 0), ("n2", 3, 1)], sent["a"])
    pass_on("b")
    pass_on("c")
    strips = rows // LANES
    wanted, code = prepare_requests(
        after(match_block.reshape(strips, LANES), sent["c"]),
        match_row.reshape(strips, LANES),
        peers,
        capacity,
    )
    mask = 1
    while mask < peers:
        wanted = jnp.concatenate([wanted, partner(wanted, mask)], axis=0)
        mask *= 2
    pieces = []
    for c in CHUNKS:
        own, other = merge_out(meta, keep[c], got[c])
        pieces.append((CHUNKS[c], own, across(other, back)))

    first_masks, last_masks = reply_order(peers)
    replies = {}

    def reply(masks, outgoing):
        for mask, rows_out in zip(masks, outgoing):
            replies[mask] = partner(rows_out, mask)

    layer, *outgoing = gather_rows(meta, wanted, pieces, first_masks, tokens)
    reply(first_masks, outgoing)
    *outgoing, own_rows = gather_rows(meta, wanted, layer, last_masks + [0], tokens)
    reply(last_masks, outgoing)
    late = [m for m in last_masks if m > 1]
    early = first_replies(
        meta, code, {0: own_rows, **{m: r for m, r in replies.items() if m not in late}}, tokens
    )
    refined = finish_rows(
        meta,
        code,
        confidence.reshape(strips, LANES),
        layer,
        early,
        {m: replies[m] for m in late},
        tokens,
    )
    return refined.reshape(local_views, tokens, sub)


def reply_order(peers):
    far_half = list(range(peers // 2, peers))
    far_half = far_half[len(far_half) // 2 :] + far_half[: len(far_half) // 2]
    pairs = zip(far_half[: len(far_half) // 2], far_half[len(far_half) // 2 :])
    return [m for pair in pairs for m in pair], list(range(2, peers // 2)) + [1]


def solution(mesh):
    in_specs = (
        P(VIEWS, None, None),
        P(),
        P(None, None, HEADS),
        P(HEADS, None),
        P(),
        P(VIEWS, None),
        P(VIEWS),
        P(VIEWS),
    )
    out_specs = P(VIEWS, None, HEADS)
    return jax.shard_map(
        per_device, mesh=mesh, in_specs=in_specs, out_specs=out_specs, check_vma=False
    )
```

```python
import jax
import jax.numpy as jnp
from jax import lax
from jax.experimental import pallas as pl
from jax.experimental.pallas import tpu as pltpu
from jax.sharding import PartitionSpec as P


VIEWS, HEADS = "views", "heads"
HEAD_DIM = 64
LANES = 128
STAGED = 4
CHUNKS = dict(a=(1,), b=(2, 0), c=(3,))

coupling = 0.5
epsilon = 1e-06

bf16 = jnp.bfloat16
f32 = jnp.float32


def cost(flops, bytes_accessed, transcendentals=0):
    return pl.CostEstimate(
        flops=int(flops), bytes_accessed=int(bytes_accessed), transcendentals=int(transcendentals)
    )


def dot(a, b):
    return jnp.dot(a, b, preferred_element_type=f32)


VMEM_SPEC = pl.BlockSpec(memory_space=pltpu.VMEM)
SMEM_SPEC = pl.BlockSpec(memory_space=pltpu.SMEM)
ANY_SPEC = pl.BlockSpec(memory_space=pl.ANY)


def grant(mib):
    return pltpu.CompilerParams(vmem_limit_bytes=mib << 20)


def many(spec, count):
    return [spec] * count


def project_views(meta, latents, gain, w_qkv, which):
    _, tokens, width = latents.shape
    sub = w_qkv.shape[2]
    count = len(which)
    scale = HEAD_DIM ** (-0.5)
    order = (2, 0, 1)

    def body(meta_ref, lat_hbm, gain_hbm, w_hbm, *refs):
        outs, (halves, buffer, gains, ws, sems) = refs[: 2 * count], refs[2 * count :]
        here = pl.ds(pl.multiple_of((meta_ref[1] // 2) * (width // 2), width // 2), width // 2)
        kept = [
            pltpu.make_async_copy(buffer.at[i, :, here], halves.at[i], sems.at[count + 4 + i])
            for i in range(count)
        ]
        copies = [
            pltpu.make_async_copy(lat_hbm.at[v], buffer.at[i], sems.at[i])
            for i, v in enumerate(which)
        ]
        gain_copy = pltpu.make_async_copy(gain_hbm, gains, sems.at[count])
        w_copies = {
            part: pltpu.make_async_copy(w_hbm.at[part], ws.at[part], sems.at[count + 1 + part])
            for part in order
        }
        queue = [copies[0], gain_copy, w_copies[2], w_copies[0], w_copies[1]] + copies[1:]
        for copy in queue[:STAGED]:
            copy.start()
        waiting = queue[STAGED:]

        def arrive(copy):
            copy.wait()
            if waiting:
                waiting.pop(0).start()

        def load_norm(i):
            arrive(copies[i])
            kept[i].start()
            if i == 0:
                arrive(gain_copy)
            wide = buffer[i].astype(f32)
            mean_square = jnp.mean(wide * wide, axis=-1, keepdims=True)
            return (wide * lax.rsqrt(mean_square + epsilon) * gains[...]).astype(bf16)

        following = load_norm(0)
        for i in range(count):
            normed = following
            if i == 0:
                arrive(w_copies[2])
            elif i + 1 < count:
                following = load_norm(i + 1)
            values = dot(normed, ws[2])
            if i == 0:
                arrive(w_copies[0])
            queries = dot(normed, ws[0])
            if i == 0:
                arrive(w_copies[1])
                following = load_norm(i + 1)
            outs[2 * i + 1][0] = dot(normed, ws[1]).astype(bf16)
            outs[2 * i + 1][1] = jnp.transpose(values).astype(bf16)
            outs[2 * i][...] = jnp.transpose(queries).astype(bf16) * jnp.asarray(scale, bf16)
        for copy in kept:
            copy.wait()

    out_shape = []
    for _ in which:
        out_shape += [
            jax.ShapeDtypeStruct((sub, tokens), bf16),
            jax.ShapeDtypeStruct((2, tokens, sub), bf16),
        ]
    out_shape.append(jax.ShapeDtypeStruct((count, tokens, width // 2), bf16))
    outs = pl.pallas_call(
        body,
        in_specs=[SMEM_SPEC] + many(ANY_SPEC, 3),
        out_specs=many(VMEM_SPEC, len(out_shape)),
        out_shape=out_shape,
        scratch_shapes=[
            pltpu.VMEM((count, tokens, width), bf16),
            pltpu.VMEM((1, width), f32),
            pltpu.VMEM((3, width, sub), bf16),
            pltpu.SemaphoreType.DMA((2 * count + 4,)),
        ],
        name="proj",
        compiler_params=grant(50),
        cost_estimate=cost(
            count * 6 * tokens * width * sub, count * tokens * (width + 3 * sub) * 2 + 6 * width * sub
        ),
    )(meta, latents, gain, w_qkv)
    return {v: (outs[2 * i], outs[2 * i + 1]) for i, v in enumerate(which)}, outs[-1]


ONES = 16
SAFE_TOTAL = 1e30
FAR = 1e30


def head_scores(q_ref, kv_ref, h):
    per = LANES // HEAD_DIM
    j, slot = h // per, h % per
    own = q_ref[h * HEAD_DIM : (h + 1) * HEAD_DIM, :]
    zero = jnp.zeros_like(own)
    padded = jnp.concatenate([own if s == slot else zero for s in range(per)], axis=0)
    return dot(kv_ref[0, :, j * LANES : (j + 1) * LANES], padded)


def head_values(kv_ref, h):
    rows = kv_ref[1, h * HEAD_DIM : (h + 1) * HEAD_DIM, :]
    return jnp.concatenate([rows, jnp.ones((ONES, rows.shape[1]), bf16)], axis=0)


def attention_cost(tokens, sub, pairs):
    heads = sub // HEAD_DIM
    return cost(
        pairs * heads * tokens * tokens * 4 * LANES,
        pairs * tokens * sub * 8,
        pairs * heads * tokens * tokens,
    )


def far_if_absent(inter_ref, at, offset):
    return jnp.where(inter_ref[offset, at] > 0, 0.0, FAR).astype(f32)


def sources_of(view, local_views, window):
    found = []
    for o in range(window):
        if view + o + 1 < local_views:
            found.append((view + o + 1, view, o))
        if view - o - 1 >= 0:
            found.append((view - o - 1, view - o - 1, o))
    return found


def attend(
    meta, inter, queries, blocks, remote, plan, window, earlier=None, last=True, carry=None
):
    local_views = len(blocks)
    sub, tokens = queries[0].shape
    heads = sub // HEAD_DIM
    tall = HEAD_DIM + ONES
    views_total = inter.shape[1]
    names = sorted(remote)
    count = len(plan)
    held = 0 if earlier is None else 2

    def body(meta_ref, inter_ref, *refs):
        before, refs = refs[:held], refs[held:]
        qs, refs = refs[:count], refs[count:]
        kvs, refs = refs[:local_views], refs[local_views:]
        far_kvs, refs = dict(zip(names, refs[: len(names)])), refs[len(names) :]
        first = meta_ref[0] * local_views

        def global_view(source):
            at = first + source
            return jnp.where(at < 0, at + views_total, at) if source < 0 else at

        def keys_of(i):
            view, sources = plan[i]
            keys = [] if held else [(kvs[view], None, None)]
            if not held:
                keys += [(kvs[t], source, o) for t, source, o in sources_of(view, local_views, window)]
            return keys + [(far_kvs[name], source, o) for name, source, o in sources]

        if last and carry is not None:
            refs[1][0] = refs[0][...]
            outs, refs = [refs[1].at[1 + i] for i in range(count)], refs[1:]
        elif last:
            outs = refs[:count]
        units = [(i, h, k) for i in range(count) for h in range(heads) for k in keys_of(i)]
        far = {}
        for _, _, (_, source, o) in units:
            if source is not None and (source, o) not in far:
                far[source, o] = far_if_absent(inter_ref, global_view(source), o)
        upcoming = head_scores(qs[units[0][0]], units[0][2][0], units[0][1])
        worst = jnp.zeros((1, tokens), f32)
        n = 0
        for i, (view, _) in enumerate(plan):
            parts = []
            for h in range(heads):
                keys = keys_of(i)
                weights = []
                top = before[1][i, h : h + 1, :] if held else None
                for _, source, o in keys:
                    scores = upcoming
                    n += 1
                    if n < len(units):
                        ni, nh, (nk, _, _) = units[n]
                        upcoming = head_scores(qs[ni], nk, nh)
                    if source is None:
                        top = jnp.max(scores, axis=0, keepdims=True)
                        shift = top
                    else:
                        shift = top + far[source, o]
                    weights.append(jnp.exp(scores - shift).astype(bf16))
                values = jnp.concatenate([head_values(k[0], h) for k in keys], axis=1)
                sums = dot(values, jnp.concatenate(weights, axis=0))
                if held:
                    sums = sums + before[0][i, h * tall : (h + 1) * tall, :]
                if not last:
                    refs[0][i, h * tall : (h + 1) * tall, :] = sums
                    refs[1][i, h : h + 1, :] = top
                    continue
                total = sums[HEAD_DIM : HEAD_DIM + 1, :]
                worst = jnp.maximum(worst, jnp.where(total < SAFE_TOTAL, 0.0, 1.0))
                parts.append(sums[:HEAD_DIM, :] * (1.0 / total))
            if last:
                outs[i][...] = jnp.transpose(jnp.concatenate(parts, axis=0)).astype(bf16)
        if not last:
            return
        work, work_stat = refs[-2:]

        @pl.when(jnp.max(worst) > 0.0)
        def _():
            for i, (view, sources) in enumerate(plan):
                exact_add(qs[i], kvs[view], work, work_stat, heads, True)
                every = [(kvs[t], s, o) for t, s, o in sources_of(view, local_views, window)]
                every += [(far_kvs[name], s, o) for name, s, o in sources]
                for kv, source, o in every:

                    @pl.when(inter_ref[o, global_view(source)] > 0)
                    def _(i=i, kv=kv):
                        exact_add(qs[i], kv, work, work_stat, heads, False)

                parts = []
                for h in range(heads):
                    total = work_stat[h, 1:2, :]
                    parts.append(work[h * HEAD_DIM : (h + 1) * HEAD_DIM, :] * (1.0 / total))
                outs[i][...] = jnp.transpose(jnp.concatenate(parts, axis=0)).astype(bf16)

    if last:
        out_shape = [jax.ShapeDtypeStruct((tokens, sub), bf16)] * count
        if carry is not None:
            out_shape = [jax.ShapeDtypeStruct((1 + count, tokens, sub), bf16)]
        scratch = [pltpu.VMEM((sub, tokens), f32), pltpu.VMEM((heads, 8, tokens), f32)]
    else:
        out_shape = [
            jax.ShapeDtypeStruct((count, heads * tall, tokens), f32),
            jax.ShapeDtypeStruct((count, heads, tokens), f32),
        ]
        scratch = []
    pairs = sum(len(s) for _, s in plan)
    if not held:
        pairs += sum(1 + len(sources_of(v, local_views, window)) for v, _ in plan)
    return pl.pallas_call(
        body,
        in_specs=[SMEM_SPEC, SMEM_SPEC]
        + many(VMEM_SPEC, held + count + local_views + len(names) + (carry is not None)),
        out_specs=many(VMEM_SPEC, len(out_shape)),
        out_shape=out_shape,
        scratch_shapes=scratch,
        name="att",
        compiler_params=grant(12),
        cost_estimate=attention_cost(tokens, sub, pairs),
    )(
        meta,
        inter,
        *(earlier or ()),
        *queries,
        *[blocks[v] for v in range(local_views)],
        *[remote[name] for name in names],
        *(() if carry is None else (carry,)),
    )


def exact_add(q_ref, kv_ref, work, work_stat, heads, start):
    per = LANES // HEAD_DIM

    def one_head(h, _):
        base = pl.multiple_of((h // per) * LANES, LANES)
        queries = q_ref[pl.ds(base, LANES), :]
        owner = lax.broadcasted_iota(jnp.int32, queries.shape, 0) // HEAD_DIM
        queries = jnp.where(owner == h % per, queries.astype(f32), 0.0).astype(bf16)
        scores = dot(kv_ref[0, :, pl.ds(base, LANES)], queries)
        top = jnp.max(scores, axis=0, keepdims=True)
        rows = pl.ds(pl.multiple_of(h * HEAD_DIM, HEAD_DIM), HEAD_DIM)
        values = kv_ref[1, rows, :]
        if not start:
            old = work_stat[h, 0:1, :]
            top = jnp.maximum(old, top)
        weights = jnp.exp(scores - top)
        total = jnp.sum(weights, axis=0, keepdims=True)
        sums = dot(values, weights.astype(bf16))
        if not start:
            fade = jnp.exp(old - top)
            total = total + work_stat[h, 1:2, :] * fade
            sums = sums + work[rows, :] * fade
        work_stat[h, 0:1, :] = top
        work_stat[h, 1:2, :] = total
        work[rows, :] = sums
        return 0

    lax.fori_loop(0, heads, one_head, 0)


def partial_out(meta, attended, near, w_own, w_near, halves, places):
    sub = attended.shape[-1]
    rows_all = attended.size // sub
    width = w_own.shape[1]
    half = width // 2

    def body(meta_ref, att, near_ref, own_ref, near_w_ref, halves_ref, keep, send):
        side = meta_ref[1] // 2
        here = pl.ds(pl.multiple_of(side * half, half), half)
        away = pl.ds(pl.multiple_of((1 - side) * half, half), half)
        rows = jnp.concatenate([x[...].reshape(rows_all, sub) for x in (att, near_ref)], axis=1)

        def columns(at):
            return jnp.concatenate([own_ref[:, at], near_w_ref[:, at]], axis=0)

        send[...] = dot(rows, columns(away)).astype(bf16)
        total = dot(rows, columns(here))
        base = jnp.concatenate([halves_ref[p] for p in places], axis=0)
        keep[...] = base.astype(f32) + total

    return pl.pallas_call(
        body,
        in_specs=[SMEM_SPEC] + many(VMEM_SPEC, 5),
        out_specs=many(VMEM_SPEC, 2),
        out_shape=[
            jax.ShapeDtypeStruct((rows_all, half), f32),
            jax.ShapeDtypeStruct((rows_all, half), bf16),
        ],
        name="part",
        compiler_params=grant(12),
        cost_estimate=cost(4 * rows_all * sub * width, 4 * sub * width + rows_all * width * 6),
    )(meta, attended, near, w_own, w_near, halves)


def merge_out(meta, keep, got):
    rows_all, half = keep.shape
    sub = half // 2

    def body(meta_ref, keep_ref, got_ref, own, other):
        layer = (keep_ref[...] + got_ref[...].astype(f32)).astype(bf16)
        low, high = layer[:, :sub], layer[:, sub:]
        odd = meta_ref[1] % 2 == 1
        own[...] = jnp.where(odd, high, low)
        other[...] = jnp.where(odd, low, high)

    return pl.pallas_call(
        body,
        in_specs=[SMEM_SPEC] + many(VMEM_SPEC, 2),
        out_specs=many(VMEM_SPEC, 2),
        out_shape=[jax.ShapeDtypeStruct((rows_all, sub), bf16)] * 2,
        name="merge",
        compiler_params=grant(8),
        cost_estimate=cost(rows_all * half * 2, rows_all * half * 8),
    )(meta, keep, got)


def prepare_requests(block_rows, token_rows, peers, capacity):
    strips, lanes = block_rows.shape

    def body(block_ref, token_ref, wanted_ref, code_ref):
        before = (
            lax.broadcasted_iota(jnp.int32, (lanes, lanes), 0)
            < lax.broadcasted_iota(jnp.int32, (lanes, lanes), 1)
        ).astype(bf16)
        peer_ids = lax.broadcasted_iota(jnp.int32, (peers, lanes), 0)
        carry = jnp.zeros((peers, 1), f32)
        slots, lefts = [], []
        for i in range(strips):
            block = block_ref[i : i + 1, :]
            hit = (peer_ids == block).astype(f32)
            rank = dot(hit.astype(bf16), before) + carry
            carry = carry + jnp.sum(hit, axis=1, keepdims=True)
            slot = jnp.sum(rank * hit, axis=0, keepdims=True)
            slots.append(slot)
            code_ref[i : i + 1, :] = block * capacity + slot.astype(jnp.int32)
            token = token_ref[i : i + 1, :]
            coarse = (token // 32).astype(f32)
            fine = (token % 32).astype(f32)
            lefts.append(jnp.concatenate([hit * coarse, hit * fine], axis=0).astype(bf16))
        columns = jnp.transpose(jnp.concatenate(slots, axis=0))
        place = lax.broadcasted_iota(jnp.int32, (lanes, capacity), 1).astype(f32)
        total = jnp.zeros((2 * peers, capacity), f32)
        for i in range(strips):
            spot = (columns[:, i : i + 1] == place).astype(bf16)
            total = total + dot(lefts[i], spot)
        wanted_ref[...] = (total[:peers] * 32.0 + total[peers:]).astype(jnp.int32)

    return pl.pallas_call(
        body,
        in_specs=[VMEM_SPEC, VMEM_SPEC],
        out_specs=[VMEM_SPEC, VMEM_SPEC],
        out_shape=[
            jax.ShapeDtypeStruct((peers, capacity), jnp.int32),
            jax.ShapeDtypeStruct((strips, lanes), jnp.int32),
        ],
        name="prep",
        compiler_params=grant(8),
        cost_estimate=cost(2 * strips * lanes * lanes * capacity, 3 * strips * lanes * 4),
    )(block_rows, token_rows)


def spread_picks(spread, shift, width):
    clamped = jnp.minimum(jnp.maximum(spread - shift, -1.0), float(width)).astype(bf16)
    wide = jnp.concatenate([clamped] * (width // LANES), axis=1) if width > LANES else clamped[:, :width]
    place = lax.broadcasted_iota(jnp.int32, wide.shape, 1).astype(f32).astype(bf16)
    return jnp.where(wide == place, jnp.ones_like(place), jnp.zeros_like(place))


def gather_rows(meta, wanted, pieces, masks, tokens):
    peers, capacity = int(round(wanted.shape[0] ** 0.5)), wanted.shape[1]
    whole = not isinstance(pieces, list)
    flat = [pieces] if whole else [p for _, *pair in pieces for p in pair]
    sub = flat[0].shape[1]
    rows = flat[0].shape[0] if whole else sum(p.shape[0] for p in flat[::2])
    local_views = rows // tokens

    def body(meta_ref, wanted_ref, *refs):
        ins, outs = refs[: len(flat)], refs[len(flat) :]
        if whole:
            layer = ins[0]
        else:
            layer, outs = outs[0], outs[1:]
            end = jnp.logical_or(meta_ref[1] == 0, meta_ref[1] == meta_ref[2] - 1)
            for c, (views, _, _) in enumerate(pieces):
                for i, v in enumerate(views):
                    at = slice(i * tokens, (i + 1) * tokens)
                    layer[v * tokens : (v + 1) * tokens, :] = jnp.where(
                        end, ins[2 * c + 1][at, :], ins[2 * c][at, :]
                    )
        lines = [wanted_ref[pl.ds(m * peers + meta_ref[0], 1), :] for m in masks]
        lines += [lines[0]] * (-len(lines) % 8)
        columns = jnp.transpose(jnp.concatenate(lines, axis=0).astype(f32))
        for n in range(len(masks)):
            spread = jnp.broadcast_to(columns[:, n : n + 1], (capacity, LANES))
            pick = jnp.concatenate(
                [spread_picks(spread, float(v * tokens), tokens) for v in range(local_views)], axis=1
            )
            outs[n][...] = dot(pick, layer[...]).astype(bf16)

    out_shape = [jax.ShapeDtypeStruct((capacity, sub), bf16)] * len(masks)
    if not whole:
        out_shape = [jax.ShapeDtypeStruct((rows, sub), bf16)] + out_shape
    return pl.pallas_call(
        body,
        in_specs=[SMEM_SPEC] + many(VMEM_SPEC, 1 + len(flat)),
        out_specs=many(VMEM_SPEC, len(out_shape)),
        out_shape=out_shape,
        name="gath",
        compiler_params=grant(12),
        cost_estimate=cost(
            2 * len(masks) * capacity * rows * sub, 2 * (rows + len(masks) * capacity) * sub * 2
        ),
    )(meta, wanted, *flat)


def fetched_part(meta_ref, code_spread, masks, reps, capacity):
    pick = jnp.concatenate(
        [
            spread_picks(
                code_spread, (lax.bitwise_xor(meta_ref[0], mask) * capacity).astype(f32), capacity
            )
            for mask in masks
        ],
        axis=1,
    )
    return dot(pick, jnp.concatenate([r[...] for r in reps], axis=0))


def spread_column(turned, g, per, lanes):
    return jnp.concatenate(
        [
            jnp.broadcast_to(turned[:, g * per + j : g * per + j + 1], (lanes, LANES))
            for j in range(per)
        ],
        axis=0,
    )


def first_replies(meta, code, replies, tokens):
    masks = sorted(replies)
    capacity, sub = replies[masks[0]].shape
    strips, lanes = code.shape
    rows = strips * lanes
    per = tokens // lanes

    def body(meta_ref, code_ref, *refs):
        codes = jnp.transpose(code_ref[...].astype(f32))
        for g in range(rows // tokens):
            refs[-1][g * tokens : (g + 1) * tokens, :] = fetched_part(
                meta_ref, spread_column(codes, g, per, lanes), masks, refs[:-1], capacity
            ).astype(bf16)

    return pl.pallas_call(
        body,
        in_specs=[SMEM_SPEC] + many(VMEM_SPEC, 1 + len(masks)),
        out_specs=VMEM_SPEC,
        out_shape=jax.ShapeDtypeStruct((rows, sub), bf16),
        name="first",
        compiler_params=grant(12),
        cost_estimate=cost(2 * len(masks) * capacity * rows * sub, rows * sub * 4),
    )(meta, code, *[replies[m] for m in masks])


def finish_rows(meta, code, confidence, layer, early, replies, tokens):
    rows, sub = layer.shape
    masks = sorted(replies)
    capacity = replies[masks[0]].shape[0]
    _, lanes = code.shape
    blocks = rows // tokens
    per = tokens // lanes

    def body(meta_ref, code_ref, conf_ref, layer_ref, early_ref, *refs):
        reps, (out_hbm, buffer, sems) = refs[: len(masks)], refs[len(masks) :]
        codes = jnp.transpose(code_ref[...].astype(f32))
        confs = jnp.transpose(conf_ref[...]) * coupling
        copies = []
        for g in range(blocks):
            at = slice(g * tokens, (g + 1) * tokens)
            fetched = early_ref[at, :].astype(f32) + fetched_part(
                meta_ref, spread_column(codes, g, per, lanes), masks, reps, capacity
            )
            wide = layer_ref[at, :].astype(f32)
            weight = jnp.concatenate([spread_column(confs, g, per, lanes)] * (sub // LANES), axis=1)
            buffer[g] = wide + weight * (fetched - wide)
            copies.append(
                pltpu.make_async_copy(
                    buffer.at[g], out_hbm.at[pl.ds(g * tokens, tokens), :], sems.at[g]
                )
            )
            copies[-1].start()
        for copy in copies:
            copy.wait()

    return pl.pallas_call(
        body,
        in_specs=[SMEM_SPEC] + many(VMEM_SPEC, 4 + len(masks)),
        out_specs=ANY_SPEC,
        out_shape=jax.ShapeDtypeStruct((rows, sub), f32),
        scratch_shapes=[
            pltpu.VMEM((blocks, tokens, sub), f32),
            pltpu.SemaphoreType.DMA((blocks,)),
        ],
        name="fin",
        compiler_params=grant(12),
        cost_estimate=cost(2 * len(masks) * capacity * rows * sub, rows * sub * 8),
    )(meta, code, confidence, layer, early, *[replies[m] for m in masks])


def per_device(latents, norm_gain, w_qkv, w_out, intersection, match_block, match_row, confidence):
    local_views, tokens, width = latents.shape
    window = intersection.shape[1]
    sub = w_qkv.shape[2]
    peers = lax.axis_size(VIEWS)
    ends = lax.axis_size(HEADS)
    rows = local_views * tokens
    capacity = 2 * rows // peers
    assert local_views == 4 and window == 2 and ends == 4 and tokens == sub
    view_at, head_at = lax.axis_index(VIEWS), lax.axis_index(HEADS)
    spot = jnp.arange(4, dtype=jnp.int32)
    meta = jnp.where(spot == 0, view_at, jnp.where(spot == 1, head_at, ends)).astype(jnp.int32)

    def along(x, by):
        return lax.ppermute(x, VIEWS, [(i, (i + by) % peers) for i in range(peers)])

    def partner(x, mask):
        return lax.ppermute(x, VIEWS, [(i, i ^ mask) for i in range(peers)])

    def across(x, pairs):
        return lax.ppermute(x, HEADS, pairs)

    def after(x, done):
        return lax.optimization_barrier((x, done))[0]

    beside, middle, back = [(0, 1), (3, 2)], [(1, 2), (2, 1)], [(1, 0), (2, 3)]
    gain = norm_gain.reshape(1, width)
    inter = intersection.T
    loaded = (0, 3, 1, 2)
    w_near = across(w_out, beside)
    projected, halves = project_views(meta, latents, gain, w_qkv, loaded)
    queries = {v: projected[v][0] for v in range(local_views)}
    blocks = {v: projected[v][1] for v in range(local_views)}
    far = {}
    far["n1"] = along(blocks[0], -1)
    far["p1"] = along(blocks[3], 1)

    inner_plan = [(1, [("p1", -1, 1)]), (2, [("n1", 2, 1)])]
    inner_queries = [queries[1], queries[2]]
    local = attend(
        meta, inter, inner_queries, blocks, {}, [(v, []) for v, _ in inner_plan], window, last=False
    )
    inner_far = dict(far)
    far["n2"] = along(after(blocks[1], local[0]), -1)
    far["p2"] = along(after(blocks[2], local[0]), 1)
    attended = {}
    attended["a"], second = attend(
        meta, inter, inner_queries, blocks, inner_far, inner_plan, window, earlier=tuple(local)
    )

    def attend_outer(view, sources, done, carry=None):
        (result,) = attend(
            meta,
            inter,
            [after(queries[view], done)],
            blocks,
            {s[0]: far[s[0]] for s in sources},
            [(view, sources)],
            window,
            carry=carry,
        )
        return result

    keep, sent, got = {}, {}, {}

    def pass_on(c):
        near = across(attended[c], beside)
        keep[c], sent[c] = partial_out(
            meta,
            attended[c],
            near,
            w_out,
            w_near,
            halves,
            [loaded.index(v) for v in CHUNKS[c]],
        )
        got[c] = across(sent[c], middle)

    attended["b"] = attend_outer(0, [("p1", -1, 0), ("p2", -2, 1)], attended["a"], second)
    pass_on("a")
    attended["c"] = attend_outer(3, [("n1", 3, 0), ("n2", 3, 1)], sent["a"])
    pass_on("b")
    pass_on("c")
    strips = rows // LANES
    wanted, code = prepare_requests(
        after(match_block.reshape(strips, LANES), sent["c"]),
        match_row.reshape(strips, LANES),
        peers,
        capacity,
    )
    mask = 1
    while mask < peers:
        wanted = jnp.concatenate([wanted, partner(wanted, mask)], axis=0)
        mask *= 2
    pieces = []
    for c in CHUNKS:
        own, other = merge_out(meta, keep[c], got[c])
        pieces.append((CHUNKS[c], own, across(other, back)))

    first_masks, last_masks = reply_order(peers)
    replies = {}

    def reply(masks, outgoing):
        for mask, rows_out in zip(masks, outgoing):
            replies[mask] = partner(rows_out, mask)

    layer, *outgoing = gather_rows(meta, wanted, pieces, first_masks, tokens)
    reply(first_masks, outgoing)
    *outgoing, own_rows = gather_rows(meta, wanted, layer, last_masks + [0], tokens)
    reply(last_masks, outgoing)
    late = [m for m in last_masks if m > 1]
    early = first_replies(
        meta, code, {0: own_rows, **{m: r for m, r in replies.items() if m not in late}}, tokens
    )
    refined = finish_rows(
        meta,
        code,
        confidence.reshape(strips, LANES),
        layer,
        early,
        {m: replies[m] for m in late},
        tokens,
    )
    return refined.reshape(local_views, tokens, sub)


def reply_order(peers):
    far_half = list(range(peers // 2, peers))
    far_half = far_half[len(far_half) // 2 :] + far_half[: len(far_half) // 2]
    pairs = zip(far_half[: len(far_half) // 2], far_half[len(far_half) // 2 :])
    return [m for pair in pairs for m in pair], list(range(2, peers // 2)) + [1]


def solution(mesh):
    in_specs = (
        P(VIEWS, None, None),
        P(),
        P(None, None, HEADS),
        P(HEADS, None),
        P(),
        P(VIEWS, None),
        P(VIEWS),
        P(VIEWS),
    )
    out_specs = P(VIEWS, None, HEADS)
    return jax.shard_map(
        per_device, mesh=mesh, in_specs=in_specs, out_specs=out_specs, check_vma=False
    )
```

```python
import jax
import jax.numpy as jnp
from jax import lax
from jax.experimental import pallas as pl
from jax.experimental.pallas import tpu as pltpu
from jax.sharding import PartitionSpec as P


VIEWS, HEADS = "views", "heads"
HEAD_DIM = 64
LANES = 128
STAGED = 3
GRANT_A, GRANT_B = 50, 50
CHUNKS = dict(a=(1,), b=(2, 0), c=(3,))

coupling = 0.5
epsilon = 1e-06

bf16 = jnp.bfloat16
f32 = jnp.float32


def cost(flops, bytes_accessed, transcendentals=0):
    return pl.CostEstimate(
        flops=int(flops), bytes_accessed=int(bytes_accessed), transcendentals=int(transcendentals)
    )


def dot(a, b):
    return jnp.dot(a, b, preferred_element_type=f32)


VMEM_SPEC = pl.BlockSpec(memory_space=pltpu.VMEM)
SMEM_SPEC = pl.BlockSpec(memory_space=pltpu.SMEM)
ANY_SPEC = pl.BlockSpec(memory_space=pl.ANY)


def grant(mib):
    return pltpu.CompilerParams(vmem_limit_bytes=mib << 20)


def many(spec, count):
    return [spec] * count


def project_views(meta, latents, gain, w_qkv, which, loaded=False):
    _, tokens, width = latents.shape
    sub = w_qkv.shape[2]
    count = len(which)
    scale = HEAD_DIM ** (-0.5)

    def body(meta_ref, lat_hbm, gain_ref, w_ref, *refs):
        outs, refs = refs[: 2 * count], refs[2 * count :]
        halves, refs = refs[0], refs[1:]
        ws = w_ref if loaded else refs[0]
        buffer, sems = refs[-2:]
        here = pl.ds(pl.multiple_of((meta_ref[1] // 2) * (width // 2), width // 2), width // 2)
        kept = [
            pltpu.make_async_copy(buffer.at[i, :, here], halves.at[i], sems.at[i])
            for i in range(count)
        ]
        copies = [
            pltpu.make_async_copy(lat_hbm.at[v], buffer.at[i], sems.at[count + i])
            for i, v in enumerate(which)
        ]
        w_copies = []
        if not loaded:
            w_copies = [
                pltpu.make_async_copy(w_ref.at[p], ws.at[p], sems.at[2 * count + p]) for p in range(3)
            ]
        queue = copies[:1] + w_copies[::-1] + copies[1:]
        for copy in queue[:STAGED]:
            copy.start()
        waiting = queue[STAGED:]

        def arrive(copy):
            copy.wait()
            if waiting:
                waiting.pop(0).start()

        def load_norm(i):
            arrive(copies[i])
            kept[i].start()
            wide = buffer[i].astype(f32)
            mean_square = jnp.mean(wide * wide, axis=-1, keepdims=True)
            return (wide * lax.rsqrt(mean_square + epsilon) * gain_ref[...]).astype(bf16)

        following = load_norm(0)
        for i in range(count):
            normed = following
            staged = i == 0 and not loaded
            if staged:
                arrive(w_copies[2])
            elif i + 1 < count:
                following = load_norm(i + 1)
            values = dot(normed, ws[2])
            if staged:
                arrive(w_copies[1])
            outs[2 * i + 1][0] = dot(normed, ws[1]).astype(bf16)
            if staged:
                arrive(w_copies[0])
                following = load_norm(i + 1)
            queries = dot(normed, ws[0])
            outs[2 * i + 1][1] = jnp.transpose(values).astype(bf16)
            outs[2 * i][...] = jnp.transpose(queries).astype(bf16) * jnp.asarray(scale, bf16)
        for copy in kept:
            copy.wait()

    out_shape = []
    for _ in which:
        out_shape += [
            jax.ShapeDtypeStruct((sub, tokens), bf16),
            jax.ShapeDtypeStruct((2, tokens, sub), bf16),
        ]
    out_shape.append(jax.ShapeDtypeStruct((count, tokens, width // 2), bf16))
    if not loaded:
        out_shape.append(jax.ShapeDtypeStruct(w_qkv.shape, bf16))
    outs = pl.pallas_call(
        body,
        in_specs=[SMEM_SPEC, ANY_SPEC, VMEM_SPEC, VMEM_SPEC if loaded else ANY_SPEC],
        out_specs=many(VMEM_SPEC, len(out_shape)),
        out_shape=out_shape,
        scratch_shapes=[
            pltpu.VMEM((count, tokens, width), bf16),
            pltpu.SemaphoreType.DMA((2 * count + 3,)),
        ],
        name="proj",
        compiler_params=grant(GRANT_B if loaded else GRANT_A),
        cost_estimate=cost(
            count * 6 * tokens * width * sub, count * tokens * (width + 3 * sub) * 2 + 6 * width * sub
        ),
    )(meta, latents, gain, w_qkv)
    views = {v: (outs[2 * i], outs[2 * i + 1]) for i, v in enumerate(which)}
    return views, outs[2 * count], outs[-1]


ONES = 16
SAFE_TOTAL = 1e30
FAR = 1e30


def head_scores(q_ref, kv_ref, h):
    per = LANES // HEAD_DIM
    j, slot = h // per, h % per
    own = q_ref[h * HEAD_DIM : (h + 1) * HEAD_DIM, :]
    zero = jnp.zeros_like(own)
    padded = jnp.concatenate([own if s == slot else zero for s in range(per)], axis=0)
    return dot(kv_ref[0, :, j * LANES : (j + 1) * LANES], padded)


def head_values(kv_ref, h):
    rows = kv_ref[1, h * HEAD_DIM : (h + 1) * HEAD_DIM, :]
    return jnp.concatenate([rows, jnp.ones((ONES, rows.shape[1]), bf16)], axis=0)


def attention_cost(tokens, sub, pairs):
    heads = sub // HEAD_DIM
    return cost(
        pairs * heads * tokens * tokens * 4 * LANES,
        pairs * tokens * sub * 8,
        pairs * heads * tokens * tokens,
    )


def far_if_absent(inter_ref, at, offset):
    return jnp.where(inter_ref[offset, at] > 0, 0.0, FAR).astype(f32)


def sources_of(view, local_views, window):
    found = []
    for o in range(window):
        if view + o + 1 < local_views:
            found.append((view + o + 1, view, o))
        if view - o - 1 >= 0:
            found.append((view - o - 1, view - o - 1, o))
    return found


def attend(
    meta, inter, queries, blocks, remote, plan, window, earlier=None, last=True, carry=None
):
    local_views = len(blocks)
    sub, tokens = queries[0].shape
    heads = sub // HEAD_DIM
    tall = HEAD_DIM + ONES
    views_total = inter.shape[1]
    names = sorted(remote)
    count = len(plan)
    held = 0 if earlier is None else 2

    def body(meta_ref, inter_ref, *refs):
        before, refs = refs[:held], refs[held:]
        qs, refs = refs[:count], refs[count:]
        kvs, refs = refs[:local_views], refs[local_views:]
        far_kvs, refs = dict(zip(names, refs[: len(names)])), refs[len(names) :]
        first = meta_ref[0] * local_views

        def global_view(source):
            at = first + source
            return jnp.where(at < 0, at + views_total, at) if source < 0 else at

        def keys_of(i):
            view, sources = plan[i]
            keys = [] if held else [(kvs[view], None, None)]
            if not held:
                keys += [(kvs[t], source, o) for t, source, o in sources_of(view, local_views, window)]
            return keys + [(far_kvs[name], source, o) for name, source, o in sources]

        if last and carry is not None:
            refs[1][0] = refs[0][...]
            outs, refs = [refs[1].at[1 + i] for i in range(count)], refs[1:]
        elif last:
            outs = refs[:count]
        units = [(i, h, k) for i in range(count) for h in range(heads) for k in keys_of(i)]
        far = {}
        for _, _, (_, source, o) in units:
            if source is not None and (source, o) not in far:
                far[source, o] = far_if_absent(inter_ref, global_view(source), o)
        upcoming = head_scores(qs[units[0][0]], units[0][2][0], units[0][1])
        worst = jnp.zeros((1, tokens), f32)
        n = 0
        for i, (view, _) in enumerate(plan):
            parts = []
            for h in range(heads):
                keys = keys_of(i)
                weights = []
                top = before[1][i, h : h + 1, :] if held else None
                for _, source, o in keys:
                    scores = upcoming
                    n += 1
                    if n < len(units):
                        ni, nh, (nk, _, _) = units[n]
                        upcoming = head_scores(qs[ni], nk, nh)
                    if source is None:
                        top = jnp.max(scores, axis=0, keepdims=True)
                        shift = top
                    else:
                        shift = top + far[source, o]
                    weights.append(jnp.exp(scores - shift).astype(bf16))
                values = jnp.concatenate([head_values(k[0], h) for k in keys], axis=1)
                sums = dot(values, jnp.concatenate(weights, axis=0))
                if held:
                    sums = sums + before[0][i, h * tall : (h + 1) * tall, :]
                if not last:
                    refs[0][i, h * tall : (h + 1) * tall, :] = sums
                    refs[1][i, h : h + 1, :] = top
                    continue
                total = sums[HEAD_DIM : HEAD_DIM + 1, :]
                worst = jnp.maximum(worst, jnp.where(total < SAFE_TOTAL, 0.0, 1.0))
                parts.append(sums[:HEAD_DIM, :] * (1.0 / total))
            if last:
                outs[i][...] = jnp.transpose(jnp.concatenate(parts, axis=0)).astype(bf16)
        if not last:
            return
        work, work_stat = refs[-2:]

        @pl.when(jnp.max(worst) > 0.0)
        def _():
            for i, (view, sources) in enumerate(plan):
                exact_add(qs[i], kvs[view], work, work_stat, heads, True)
                every = [(kvs[t], s, o) for t, s, o in sources_of(view, local_views, window)]
                every += [(far_kvs[name], s, o) for name, s, o in sources]
                for kv, source, o in every:

                    @pl.when(inter_ref[o, global_view(source)] > 0)
                    def _(i=i, kv=kv):
                        exact_add(qs[i], kv, work, work_stat, heads, False)

                parts = []
                for h in range(heads):
                    total = work_stat[h, 1:2, :]
                    parts.append(work[h * HEAD_DIM : (h + 1) * HEAD_DIM, :] * (1.0 / total))
                outs[i][...] = jnp.transpose(jnp.concatenate(parts, axis=0)).astype(bf16)

    if last:
        out_shape = [jax.ShapeDtypeStruct((tokens, sub), bf16)] * count
        if carry is not None:
            out_shape = [jax.ShapeDtypeStruct((1 + count, tokens, sub), bf16)]
        scratch = [pltpu.VMEM((sub, tokens), f32), pltpu.VMEM((heads, 8, tokens), f32)]
    else:
        out_shape = [
            jax.ShapeDtypeStruct((count, heads * tall, tokens), f32),
            jax.ShapeDtypeStruct((count, heads, tokens), f32),
        ]
        scratch = []
    pairs = sum(len(s) for _, s in plan)
    if not held:
        pairs += sum(1 + len(sources_of(v, local_views, window)) for v, _ in plan)
    return pl.pallas_call(
        body,
        in_specs=[SMEM_SPEC, SMEM_SPEC]
        + many(VMEM_SPEC, held + count + local_views + len(names) + (carry is not None)),
        out_specs=many(VMEM_SPEC, len(out_shape)),
        out_shape=out_shape,
        scratch_shapes=scratch,
        name="att",
        compiler_params=grant(12),
        cost_estimate=attention_cost(tokens, sub, pairs),
    )(
        meta,
        inter,
        *(earlier or ()),
        *queries,
        *[blocks[v] for v in range(local_views)],
        *[remote[name] for name in names],
        *(() if carry is None else (carry,)),
    )


def exact_add(q_ref, kv_ref, work, work_stat, heads, start):
    per = LANES // HEAD_DIM

    def one_head(h, _):
        base = pl.multiple_of((h // per) * LANES, LANES)
        queries = q_ref[pl.ds(base, LANES), :]
        owner = lax.broadcasted_iota(jnp.int32, queries.shape, 0) // HEAD_DIM
        queries = jnp.where(owner == h % per, queries.astype(f32), 0.0).astype(bf16)
        scores = dot(kv_ref[0, :, pl.ds(base, LANES)], queries)
        top = jnp.max(scores, axis=0, keepdims=True)
        rows = pl.ds(pl.multiple_of(h * HEAD_DIM, HEAD_DIM), HEAD_DIM)
        values = kv_ref[1, rows, :]
        if not start:
            old = work_stat[h, 0:1, :]
            top = jnp.maximum(old, top)
        weights = jnp.exp(scores - top)
        total = jnp.sum(weights, axis=0, keepdims=True)
        sums = dot(values, weights.astype(bf16))
        if not start:
            fade = jnp.exp(old - top)
            total = total + work_stat[h, 1:2, :] * fade
            sums = sums + work[rows, :] * fade
        work_stat[h, 0:1, :] = top
        work_stat[h, 1:2, :] = total
        work[rows, :] = sums
        return 0

    lax.fori_loop(0, heads, one_head, 0)


def partial_out(meta, attended, near, w_own, w_near, base):
    sub = attended.shape[-1]
    rows_all = attended.size // sub
    width = w_own.shape[1]
    half = width // 2

    def body(meta_ref, att, near_ref, own_ref, near_w_ref, *refs):
        keep, send = refs[-2:]
        side = meta_ref[1] // 2
        here = pl.ds(pl.multiple_of(side * half, half), half)
        away = pl.ds(pl.multiple_of((1 - side) * half, half), half)
        rows = jnp.concatenate([x[...].reshape(rows_all, sub) for x in (att, near_ref)], axis=1)

        def columns(at):
            return jnp.concatenate([own_ref[:, at], near_w_ref[:, at]], axis=0)

        send[...] = dot(rows, columns(away)).astype(bf16)
        total = dot(rows, columns(here))
        start = jnp.concatenate([ref[place] for ref, (_, place) in zip(refs, base)], axis=0)
        keep[...] = start.astype(f32) + total

    return pl.pallas_call(
        body,
        in_specs=[SMEM_SPEC] + many(VMEM_SPEC, 4 + len(base)),
        out_specs=many(VMEM_SPEC, 2),
        out_shape=[
            jax.ShapeDtypeStruct((rows_all, half), f32),
            jax.ShapeDtypeStruct((rows_all, half), bf16),
        ],
        name="part",
        compiler_params=grant(12),
        cost_estimate=cost(4 * rows_all * sub * width, 4 * sub * width + rows_all * width * 6),
    )(meta, attended, near, w_own, w_near, *[array for array, _ in base])


def merge_out(meta, keep, got):
    rows_all, half = keep.shape
    sub = half // 2

    def body(meta_ref, keep_ref, got_ref, own, other):
        layer = (keep_ref[...] + got_ref[...].astype(f32)).astype(bf16)
        low, high = layer[:, :sub], layer[:, sub:]
        odd = meta_ref[1] % 2 == 1
        own[...] = jnp.where(odd, high, low)
        other[...] = jnp.where(odd, low, high)

    return pl.pallas_call(
        body,
        in_specs=[SMEM_SPEC] + many(VMEM_SPEC, 2),
        out_specs=many(VMEM_SPEC, 2),
        out_shape=[jax.ShapeDtypeStruct((rows_all, sub), bf16)] * 2,
        name="merge",
        compiler_params=grant(8),
        cost_estimate=cost(rows_all * half * 2, rows_all * half * 8),
    )(meta, keep, got)


def prepare_requests(block_rows, token_rows, peers, capacity):
    strips, lanes = block_rows.shape

    def body(block_ref, token_ref, wanted_ref, code_ref):
        before = (
            lax.broadcasted_iota(jnp.int32, (lanes, lanes), 0)
            < lax.broadcasted_iota(jnp.int32, (lanes, lanes), 1)
        ).astype(bf16)
        peer_ids = lax.broadcasted_iota(jnp.int32, (peers, lanes), 0)
        carry = jnp.zeros((peers, 1), f32)
        slots, lefts = [], []
        for i in range(strips):
            block = block_ref[i : i + 1, :]
            hit = (peer_ids == block).astype(f32)
            rank = dot(hit.astype(bf16), before) + carry
            carry = carry + jnp.sum(hit, axis=1, keepdims=True)
            slot = jnp.sum(rank * hit, axis=0, keepdims=True)
            slots.append(slot)
            code_ref[i : i + 1, :] = block * capacity + slot.astype(jnp.int32)
            token = token_ref[i : i + 1, :]
            coarse = (token // 32).astype(f32)
            fine = (token % 32).astype(f32)
            lefts.append(jnp.concatenate([hit * coarse, hit * fine], axis=0).astype(bf16))
        columns = jnp.transpose(jnp.concatenate(slots, axis=0))
        place = lax.broadcasted_iota(jnp.int32, (lanes, capacity), 1).astype(f32)
        total = jnp.zeros((2 * peers, capacity), f32)
        for i in range(strips):
            spot = (columns[:, i : i + 1] == place).astype(bf16)
            total = total + dot(lefts[i], spot)
        wanted_ref[...] = (total[:peers] * 32.0 + total[peers:]).astype(jnp.int32)

    return pl.pallas_call(
        body,
        in_specs=[VMEM_SPEC, VMEM_SPEC],
        out_specs=[VMEM_SPEC, VMEM_SPEC],
        out_shape=[
            jax.ShapeDtypeStruct((peers, capacity), jnp.int32),
            jax.ShapeDtypeStruct((strips, lanes), jnp.int32),
        ],
        name="prep",
        compiler_params=grant(8),
        cost_estimate=cost(2 * strips * lanes * lanes * capacity, 3 * strips * lanes * 4),
    )(block_rows, token_rows)


def spread_picks(spread, shift, width):
    clamped = jnp.minimum(jnp.maximum(spread - shift, -1.0), float(width)).astype(bf16)
    wide = jnp.concatenate([clamped] * (width // LANES), axis=1) if width > LANES else clamped[:, :width]
    place = lax.broadcasted_iota(jnp.int32, wide.shape, 1).astype(f32).astype(bf16)
    return jnp.where(wide == place, jnp.ones_like(place), jnp.zeros_like(place))


def gather_rows(meta, wanted, pieces, masks, tokens):
    peers, capacity = int(round(wanted.shape[0] ** 0.5)), wanted.shape[1]
    whole = not isinstance(pieces, list)
    flat = [pieces] if whole else [p for _, *pair in pieces for p in pair]
    sub = flat[0].shape[1]
    rows = flat[0].shape[0] if whole else sum(p.shape[0] for p in flat[::2])
    local_views = rows // tokens

    def body(meta_ref, wanted_ref, *refs):
        ins, outs = refs[: len(flat)], refs[len(flat) :]
        if whole:
            layer = ins[0]
        else:
            layer, outs = outs[0], outs[1:]
            end = jnp.logical_or(meta_ref[1] == 0, meta_ref[1] == meta_ref[2] - 1)
            for c, (views, _, _) in enumerate(pieces):
                for i, v in enumerate(views):
                    at = slice(i * tokens, (i + 1) * tokens)
                    layer[v * tokens : (v + 1) * tokens, :] = jnp.where(
                        end, ins[2 * c + 1][at, :], ins[2 * c][at, :]
                    )
        lines = [wanted_ref[pl.ds(m * peers + meta_ref[0], 1), :] for m in masks]
        lines += [lines[0]] * (-len(lines) % 8)
        columns = jnp.transpose(jnp.concatenate(lines, axis=0).astype(f32))
        for n in range(len(masks)):
            spread = jnp.broadcast_to(columns[:, n : n + 1], (capacity, LANES))
            pick = jnp.concatenate(
                [spread_picks(spread, float(v * tokens), tokens) for v in range(local_views)], axis=1
            )
            outs[n][...] = dot(pick, layer[...]).astype(bf16)

    out_shape = [jax.ShapeDtypeStruct((capacity, sub), bf16)] * len(masks)
    if not whole:
        out_shape = [jax.ShapeDtypeStruct((rows, sub), bf16)] + out_shape
    return pl.pallas_call(
        body,
        in_specs=[SMEM_SPEC] + many(VMEM_SPEC, 1 + len(flat)),
        out_specs=many(VMEM_SPEC, len(out_shape)),
        out_shape=out_shape,
        name="gath",
        compiler_params=grant(12),
        cost_estimate=cost(
            2 * len(masks) * capacity * rows * sub, 2 * (rows + len(masks) * capacity) * sub * 2
        ),
    )(meta, wanted, *flat)


def fetched_part(meta_ref, code_spread, masks, reps, capacity):
    pick = jnp.concatenate(
        [
            spread_picks(
                code_spread, (lax.bitwise_xor(meta_ref[0], mask) * capacity).astype(f32), capacity
            )
            for mask in masks
        ],
        axis=1,
    )
    return dot(pick, jnp.concatenate([r[...] for r in reps], axis=0))


def spread_column(turned, g, per, lanes):
    return jnp.concatenate(
        [
            jnp.broadcast_to(turned[:, g * per + j : g * per + j + 1], (lanes, LANES))
            for j in range(per)
        ],
        axis=0,
    )


def first_replies(meta, code, replies, tokens):
    masks = sorted(replies)
    capacity, sub = replies[masks[0]].shape
    strips, lanes = code.shape
    rows = strips * lanes
    per = tokens // lanes

    def body(meta_ref, code_ref, *refs):
        codes = jnp.transpose(code_ref[...].astype(f32))
        for g in range(rows // tokens):
            refs[-1][g * tokens : (g + 1) * tokens, :] = fetched_part(
                meta_ref, spread_column(codes, g, per, lanes), masks, refs[:-1], capacity
            ).astype(bf16)

    return pl.pallas_call(
        body,
        in_specs=[SMEM_SPEC] + many(VMEM_SPEC, 1 + len(masks)),
        out_specs=VMEM_SPEC,
        out_shape=jax.ShapeDtypeStruct((rows, sub), bf16),
        name="first",
        compiler_params=grant(12),
        cost_estimate=cost(2 * len(masks) * capacity * rows * sub, rows * sub * 4),
    )(meta, code, *[replies[m] for m in masks])


def finish_rows(meta, code, confidence, layer, early, replies, tokens):
    rows, sub = layer.shape
    masks = sorted(replies)
    capacity = replies[masks[0]].shape[0]
    _, lanes = code.shape
    blocks = rows // tokens
    per = tokens // lanes

    def body(meta_ref, code_ref, conf_ref, layer_ref, early_ref, *refs):
        reps, (out_hbm, buffer, sems) = refs[: len(masks)], refs[len(masks) :]
        codes = jnp.transpose(code_ref[...].astype(f32))
        confs = jnp.transpose(conf_ref[...]) * coupling
        copies = []
        for g in range(blocks):
            at = slice(g * tokens, (g + 1) * tokens)
            fetched = early_ref[at, :].astype(f32) + fetched_part(
                meta_ref, spread_column(codes, g, per, lanes), masks, reps, capacity
            )
            wide = layer_ref[at, :].astype(f32)
            weight = jnp.concatenate([spread_column(confs, g, per, lanes)] * (sub // LANES), axis=1)
            buffer[g] = wide + weight * (fetched - wide)
            copies.append(
                pltpu.make_async_copy(
                    buffer.at[g], out_hbm.at[pl.ds(g * tokens, tokens), :], sems.at[g]
                )
            )
            copies[-1].start()
        for copy in copies:
            copy.wait()

    return pl.pallas_call(
        body,
        in_specs=[SMEM_SPEC] + many(VMEM_SPEC, 4 + len(masks)),
        out_specs=ANY_SPEC,
        out_shape=jax.ShapeDtypeStruct((rows, sub), f32),
        scratch_shapes=[
            pltpu.VMEM((blocks, tokens, sub), f32),
            pltpu.SemaphoreType.DMA((blocks,)),
        ],
        name="fin",
        compiler_params=grant(12),
        cost_estimate=cost(2 * len(masks) * capacity * rows * sub, rows * sub * 8),
    )(meta, code, confidence, layer, early, *[replies[m] for m in masks])


def per_device(latents, norm_gain, w_qkv, w_out, intersection, match_block, match_row, confidence):
    local_views, tokens, width = latents.shape
    window = intersection.shape[1]
    sub = w_qkv.shape[2]
    peers = lax.axis_size(VIEWS)
    ends = lax.axis_size(HEADS)
    rows = local_views * tokens
    capacity = 2 * rows // peers
    assert local_views == 4 and window == 2 and ends == 4 and tokens == sub
    view_at, head_at = lax.axis_index(VIEWS), lax.axis_index(HEADS)
    spot = jnp.arange(4, dtype=jnp.int32)
    meta = jnp.where(spot == 0, view_at, jnp.where(spot == 1, head_at, ends)).astype(jnp.int32)

    def along(x, by):
        return lax.ppermute(x, VIEWS, [(i, (i + by) % peers) for i in range(peers)])

    def partner(x, mask):
        return lax.ppermute(x, VIEWS, [(i, i ^ mask) for i in range(peers)])

    def across(x, pairs):
        return lax.ppermute(x, HEADS, pairs)

    def after(x, done):
        return lax.optimization_barrier((x, done))[0]

    beside, middle, back = [(0, 1), (3, 2)], [(1, 2), (2, 1)], [(1, 0), (2, 3)]
    gain = norm_gain.reshape(1, width)
    inter = intersection.T
    w_near = across(w_out, beside)
    far = {}
    projected, edge_halves, weights = project_views(meta, latents, gain, w_qkv, (0, 3))
    far["n1"] = along(projected[0][1], -1)
    far["p1"] = along(projected[3][1], 1)
    more, inner_halves, _ = project_views(meta, latents, gain, weights, (1, 2), loaded=True)
    projected.update(more)
    queries = {v: projected[v][0] for v in range(local_views)}
    blocks = {v: projected[v][1] for v in range(local_views)}
    inner_far = dict(far)
    far["n2"] = along(blocks[1], -1)
    far["p2"] = along(blocks[2], 1)
    base = {0: (edge_halves, 0), 3: (edge_halves, 1), 1: (inner_halves, 0), 2: (inner_halves, 1)}

    inner_plan = [(1, [("p1", -1, 1)]), (2, [("n1", 2, 1)])]
    inner_queries = [queries[1], queries[2]]
    local = attend(
        meta, inter, inner_queries, blocks, {}, [(v, []) for v, _ in inner_plan], window, last=False
    )
    attended = {}
    attended["a"], second = attend(
        meta, inter, inner_queries, blocks, inner_far, inner_plan, window, earlier=tuple(local)
    )

    def attend_outer(view, sources, done, carry=None):
        (result,) = attend(
            meta,
            inter,
            [after(queries[view], done)],
            blocks,
            {s[0]: far[s[0]] for s in sources},
            [(view, sources)],
            window,
            carry=carry,
        )
        return result

    keep, sent, got = {}, {}, {}

    def pass_on(c):
        near = across(attended[c], beside)
        keep[c], sent[c] = partial_out(
            meta,
            attended[c],
            near,
            w_out,
            w_near,
            [base[v] for v in CHUNKS[c]],
        )
        got[c] = across(sent[c], middle)

    attended["b"] = attend_outer(0, [("p1", -1, 0), ("p2", -2, 1)], attended["a"], second)
    pass_on("a")
    attended["c"] = attend_outer(3, [("n1", 3, 0), ("n2", 3, 1)], sent["a"])
    pass_on("b")
    pass_on("c")
    strips = rows // LANES
    wanted, code = prepare_requests(
        after(match_block.reshape(strips, LANES), sent["c"]),
        match_row.reshape(strips, LANES),
        peers,
        capacity,
    )
    mask = 1
    while mask < peers:
        wanted = jnp.concatenate([wanted, partner(wanted, mask)], axis=0)
        mask *= 2
    pieces = []
    for c in CHUNKS:
        own, other = merge_out(meta, keep[c], got[c])
        pieces.append((CHUNKS[c], own, across(other, back)))

    first_masks, last_masks = reply_order(peers)
    replies = {}

    def reply(masks, outgoing):
        for mask, rows_out in zip(masks, outgoing):
            replies[mask] = partner(rows_out, mask)

    layer, *outgoing = gather_rows(meta, wanted, pieces, first_masks, tokens)
    reply(first_masks, outgoing)
    *outgoing, own_rows = gather_rows(meta, wanted, layer, last_masks + [0], tokens)
    reply(last_masks, outgoing)
    late = [m for m in last_masks if m > 1]
    early = first_replies(
        meta, code, {0: own_rows, **{m: r for m, r in replies.items() if m not in late}}, tokens
    )
    refined = finish_rows(
        meta,
        code,
        confidence.reshape(strips, LANES),
        layer,
        early,
        {m: replies[m] for m in late},
        tokens,
    )
    return refined.reshape(local_views, tokens, sub)


def reply_order(peers):
    far_half = list(range(peers // 2, peers))
    far_half = far_half[len(far_half) // 2 :] + far_half[: len(far_half) // 2]
    pairs = zip(far_half[: len(far_half) // 2], far_half[len(far_half) // 2 :])
    return [m for pair in pairs for m in pair], list(range(2, peers // 2)) + [1]


def solution(mesh):
    in_specs = (
        P(VIEWS, None, None),
        P(),
        P(None, None, HEADS),
        P(HEADS, None),
        P(),
        P(VIEWS, None),
        P(VIEWS),
        P(VIEWS),
    )
    out_specs = P(VIEWS, None, HEADS)
    return jax.shard_map(
        per_device, mesh=mesh, in_specs=in_specs, out_specs=out_specs, check_vma=False
    )
```

```python
import jax
import jax.numpy as jnp
from jax import lax
from jax.experimental import pallas as pl
from jax.experimental.pallas import tpu as pltpu
from jax.sharding import PartitionSpec as P


VIEWS, HEADS = "views", "heads"
HEAD_DIM = 64
LANES = 128
STAGED = 3
GRANT_A, GRANT_B = 50, 40
CHUNKS = dict(a=(1,), b=(2, 0), c=(3,))

coupling = 0.5
epsilon = 1e-06

bf16 = jnp.bfloat16
f32 = jnp.float32


def cost(flops, bytes_accessed, transcendentals=0):
    return pl.CostEstimate(
        flops=int(flops), bytes_accessed=int(bytes_accessed), transcendentals=int(transcendentals)
    )


def dot(a, b):
    return jnp.dot(a, b, preferred_element_type=f32)


VMEM_SPEC = pl.BlockSpec(memory_space=pltpu.VMEM)
SMEM_SPEC = pl.BlockSpec(memory_space=pltpu.SMEM)
ANY_SPEC = pl.BlockSpec(memory_space=pl.ANY)


def grant(mib):
    return pltpu.CompilerParams(vmem_limit_bytes=mib << 20)


def many(spec, count):
    return [spec] * count


def project_views(meta, latents, gain, w_qkv, which, following=()):
    tokens, width = latents.shape[1:]
    sub = w_qkv.shape[2]
    count, ahead = len(which), len(following)
    scale = HEAD_DIM ** (-0.5)

    def body(meta_ref, lat_ref, gain_ref, w_ref, *refs):
        outs, refs = refs[: 2 * count], refs[2 * count :]
        halves, refs = refs[0], refs[1:]
        ws, source = (refs[0], refs[2]) if ahead else (w_ref, lat_ref)
        sems = refs[-1]
        here = pl.ds(pl.multiple_of((meta_ref[1] // 2) * (width // 2), width // 2), width // 2)
        kept = [
            pltpu.make_async_copy(source.at[i, :, here], halves.at[i], sems.at[i])
            for i in range(count)
        ]
        queue, loads, parts = [], [], []
        if ahead:
            loads = [
                pltpu.make_async_copy(lat_ref.at[v], source.at[i], sems.at[count + i])
                for i, v in enumerate(which)
            ]
            parts = [
                pltpu.make_async_copy(w_ref.at[p], ws.at[p], sems.at[2 * count + p]) for p in range(3)
            ]
            later = [
                pltpu.make_async_copy(lat_ref.at[v], refs[1].at[i], sems.at[2 * count + 3 + i])
                for i, v in enumerate(following)
            ]
            queue = loads + [parts[2], parts[1], parts[0]] + later
        for copy in queue[:STAGED]:
            copy.start()
        waiting = queue[STAGED:]

        def arrive(copy):
            copy.wait()
            if waiting:
                waiting.pop(0).start()

        normed = []
        for i in range(count):
            if ahead:
                arrive(loads[i])
            kept[i].start()
            wide = source[i].astype(f32)
            mean_square = jnp.mean(wide * wide, axis=-1, keepdims=True)
            normed.append((wide * lax.rsqrt(mean_square + epsilon) * gain_ref[...]).astype(bf16))
        for part in (2, 1, 0):
            if ahead:
                arrive(parts[part])
            for i in range(count):
                product = dot(normed[i], ws[part])
                if part == 2:
                    outs[2 * i + 1][1] = jnp.transpose(product).astype(bf16)
                elif part == 1:
                    outs[2 * i + 1][0] = product.astype(bf16)
                else:
                    outs[2 * i][...] = jnp.transpose(product).astype(bf16) * jnp.asarray(scale, bf16)
        for copy in kept + (later if ahead else []):
            copy.wait()

    out_shape = []
    for _ in which:
        out_shape += [
            jax.ShapeDtypeStruct((sub, tokens), bf16),
            jax.ShapeDtypeStruct((2, tokens, sub), bf16),
        ]
    out_shape.append(jax.ShapeDtypeStruct((count, tokens, width // 2), bf16))
    scratch = [pltpu.SemaphoreType.DMA((2 * count + 3 + ahead,))]
    if ahead:
        out_shape.append(jax.ShapeDtypeStruct(w_qkv.shape, bf16))
        out_shape.append(jax.ShapeDtypeStruct((ahead, tokens, width), bf16))
        scratch = [pltpu.VMEM((count, tokens, width), bf16)] + scratch
    big = ANY_SPEC if ahead else VMEM_SPEC
    outs = pl.pallas_call(
        body,
        in_specs=[SMEM_SPEC, big, VMEM_SPEC, big],
        out_specs=many(VMEM_SPEC, len(out_shape)),
        out_shape=out_shape,
        scratch_shapes=scratch,
        name="proj",
        compiler_params=grant(GRANT_A if ahead else GRANT_B),
        cost_estimate=cost(
            count * 6 * tokens * width * sub, count * tokens * (width + 3 * sub) * 2 + 6 * width * sub
        ),
    )(meta, latents, gain, w_qkv)
    views = {v: (outs[2 * i], outs[2 * i + 1]) for i, v in enumerate(which)}
    return views, *outs[2 * count :]


ONES = 16
SAFE_TOTAL = 1e30
FAR = 1e30


def head_scores(q_ref, kv_ref, h):
    per = LANES // HEAD_DIM
    j, slot = h // per, h % per
    own = q_ref[h * HEAD_DIM : (h + 1) * HEAD_DIM, :]
    zero = jnp.zeros_like(own)
    padded = jnp.concatenate([own if s == slot else zero for s in range(per)], axis=0)
    return dot(kv_ref[0, :, j * LANES : (j + 1) * LANES], padded)


def head_values(kv_ref, h):
    rows = kv_ref[1, h * HEAD_DIM : (h + 1) * HEAD_DIM, :]
    return jnp.concatenate([rows, jnp.ones((ONES, rows.shape[1]), bf16)], axis=0)


def attention_cost(tokens, sub, pairs):
    heads = sub // HEAD_DIM
    return cost(
        pairs * heads * tokens * tokens * 4 * LANES,
        pairs * tokens * sub * 8,
        pairs * heads * tokens * tokens,
    )


def far_if_absent(inter_ref, at, offset):
    return jnp.where(inter_ref[offset, at] > 0, 0.0, FAR).astype(f32)


def sources_of(view, local_views, window):
    found = []
    for o in range(window):
        if view + o + 1 < local_views:
            found.append((view + o + 1, view, o))
        if view - o - 1 >= 0:
            found.append((view - o - 1, view - o - 1, o))
    return found


def attend(
    meta, inter, queries, blocks, remote, plan, window, earlier=None, last=True, carry=None, slot=0
):
    local_views = len(blocks)
    sub, tokens = queries[0].shape
    heads = sub // HEAD_DIM
    tall = HEAD_DIM + ONES
    views_total = inter.shape[1]
    names = sorted(remote)
    count = len(plan)
    held = 0 if earlier is None else 2

    def body(meta_ref, inter_ref, *refs):
        before, refs = refs[:held], refs[held:]
        qs, refs = refs[:count], refs[count:]
        kvs, refs = refs[:local_views], refs[local_views:]
        far_kvs, refs = dict(zip(names, refs[: len(names)])), refs[len(names) :]
        first = meta_ref[0] * local_views

        def global_view(source):
            at = first + source
            return jnp.where(at < 0, at + views_total, at) if source < 0 else at

        def keys_of(i):
            view, sources = plan[i]
            keys = [] if held else [(kvs[view], None, None)]
            if not held:
                keys += [(kvs[t], source, o) for t, source, o in sources_of(view, local_views, window)]
            return keys + [(far_kvs[name], source, o) for name, source, o in sources]

        if last and carry is not None:
            refs[1][0] = refs[0][...]
            outs, refs = [refs[1].at[1 + i] for i in range(count)], refs[1:]
        elif last:
            outs = refs[:count]
        units = [(i, h, k) for i in range(count) for h in range(heads) for k in keys_of(i)]
        far = {}
        for _, _, (_, source, o) in units:
            if source is not None and (source, o) not in far:
                far[source, o] = far_if_absent(inter_ref, global_view(source), o)
        upcoming = head_scores(qs[units[0][0]], units[0][2][0], units[0][1])
        worst = jnp.zeros((1, tokens), f32)
        n = 0
        for i, (view, _) in enumerate(plan):
            parts = []
            for h in range(heads):
                keys = keys_of(i)
                weights = []
                top = before[1][slot + i, h : h + 1, :] if held else None
                for _, source, o in keys:
                    scores = upcoming
                    n += 1
                    if n < len(units):
                        ni, nh, (nk, _, _) = units[n]
                        upcoming = head_scores(qs[ni], nk, nh)
                    if source is None:
                        top = jnp.max(scores, axis=0, keepdims=True)
                        shift = top
                    else:
                        shift = top + far[source, o]
                    weights.append(jnp.exp(scores - shift).astype(bf16))
                values = jnp.concatenate([head_values(k[0], h) for k in keys], axis=1)
                sums = dot(values, jnp.concatenate(weights, axis=0))
                if held:
                    sums = sums + before[0][slot + i, h * tall : (h + 1) * tall, :]
                if not last:
                    refs[0][i, h * tall : (h + 1) * tall, :] = sums
                    refs[1][i, h : h + 1, :] = top
                    continue
                total = sums[HEAD_DIM : HEAD_DIM + 1, :]
                worst = jnp.maximum(worst, jnp.where(total < SAFE_TOTAL, 0.0, 1.0))
                parts.append(sums[:HEAD_DIM, :] * (1.0 / total))
            if last:
                outs[i][...] = jnp.transpose(jnp.concatenate(parts, axis=0)).astype(bf16)
        if not last:
            return
        work, work_stat = refs[-2:]

        @pl.when(jnp.max(worst) > 0.0)
        def _():
            for i, (view, sources) in enumerate(plan):
                exact_add(qs[i], kvs[view], work, work_stat, heads, True)
                every = [(kvs[t], s, o) for t, s, o in sources_of(view, local_views, window)]
                every += [(far_kvs[name], s, o) for name, s, o in sources]
                for kv, source, o in every:

                    @pl.when(inter_ref[o, global_view(source)] > 0)
                    def _(i=i, kv=kv):
                        exact_add(qs[i], kv, work, work_stat, heads, False)

                parts = []
                for h in range(heads):
                    total = work_stat[h, 1:2, :]
                    parts.append(work[h * HEAD_DIM : (h + 1) * HEAD_DIM, :] * (1.0 / total))
                outs[i][...] = jnp.transpose(jnp.concatenate(parts, axis=0)).astype(bf16)

    if last:
        out_shape = [jax.ShapeDtypeStruct((tokens, sub), bf16)] * count
        if carry is not None:
            out_shape = [jax.ShapeDtypeStruct((1 + count, tokens, sub), bf16)]
        scratch = [pltpu.VMEM((sub, tokens), f32), pltpu.VMEM((heads, 8, tokens), f32)]
    else:
        out_shape = [
            jax.ShapeDtypeStruct((count, heads * tall, tokens), f32),
            jax.ShapeDtypeStruct((count, heads, tokens), f32),
        ]
        scratch = []
    pairs = sum(len(s) for _, s in plan)
    if not held:
        pairs += sum(1 + len(sources_of(v, local_views, window)) for v, _ in plan)
    return pl.pallas_call(
        body,
        in_specs=[SMEM_SPEC, SMEM_SPEC]
        + many(VMEM_SPEC, held + count + local_views + len(names) + (carry is not None)),
        out_specs=many(VMEM_SPEC, len(out_shape)),
        out_shape=out_shape,
        scratch_shapes=scratch,
        name="att",
        compiler_params=grant(12),
        cost_estimate=attention_cost(tokens, sub, pairs),
    )(
        meta,
        inter,
        *(earlier or ()),
        *queries,
        *[blocks[v] for v in range(local_views)],
        *[remote[name] for name in names],
        *(() if carry is None else (carry,)),
    )


def exact_add(q_ref, kv_ref, work, work_stat, heads, start):
    per = LANES // HEAD_DIM

    def one_head(h, _):
        base = pl.multiple_of((h // per) * LANES, LANES)
        queries = q_ref[pl.ds(base, LANES), :]
        owner = lax.broadcasted_iota(jnp.int32, queries.shape, 0) // HEAD_DIM
        queries = jnp.where(owner == h % per, queries.astype(f32), 0.0).astype(bf16)
        scores = dot(kv_ref[0, :, pl.ds(base, LANES)], queries)
        top = jnp.max(scores, axis=0, keepdims=True)
        rows = pl.ds(pl.multiple_of(h * HEAD_DIM, HEAD_DIM), HEAD_DIM)
        values = kv_ref[1, rows, :]
        if not start:
            old = work_stat[h, 0:1, :]
            top = jnp.maximum(old, top)
        weights = jnp.exp(scores - top)
        total = jnp.sum(weights, axis=0, keepdims=True)
        sums = dot(values, weights.astype(bf16))
        if not start:
            fade = jnp.exp(old - top)
            total = total + work_stat[h, 1:2, :] * fade
            sums = sums + work[rows, :] * fade
        work_stat[h, 0:1, :] = top
        work_stat[h, 1:2, :] = total
        work[rows, :] = sums
        return 0

    lax.fori_loop(0, heads, one_head, 0)


def partial_out(meta, attended, near, w_own, w_near, base):
    sub = attended.shape[-1]
    rows_all = attended.size // sub
    width = w_own.shape[1]
    half = width // 2

    def body(meta_ref, att, near_ref, own_ref, near_w_ref, *refs):
        keep, send = refs[-2:]
        side = meta_ref[1] // 2
        here = pl.ds(pl.multiple_of(side * half, half), half)
        away = pl.ds(pl.multiple_of((1 - side) * half, half), half)
        rows = jnp.concatenate([x[...].reshape(rows_all, sub) for x in (att, near_ref)], axis=1)

        def columns(at):
            return jnp.concatenate([own_ref[:, at], near_w_ref[:, at]], axis=0)

        send[...] = dot(rows, columns(away)).astype(bf16)
        total = dot(rows, columns(here))
        start = jnp.concatenate([ref[place] for ref, (_, place) in zip(refs, base)], axis=0)
        keep[...] = start.astype(f32) + total

    return pl.pallas_call(
        body,
        in_specs=[SMEM_SPEC] + many(VMEM_SPEC, 4 + len(base)),
        out_specs=many(VMEM_SPEC, 2),
        out_shape=[
            jax.ShapeDtypeStruct((rows_all, half), f32),
            jax.ShapeDtypeStruct((rows_all, half), bf16),
        ],
        name="part",
        compiler_params=grant(12),
        cost_estimate=cost(4 * rows_all * sub * width, 4 * sub * width + rows_all * width * 6),
    )(meta, attended, near, w_own, w_near, *[array for array, _ in base])


def merge_out(meta, keep, got):
    rows_all, half = keep.shape
    sub = half // 2

    def body(meta_ref, keep_ref, got_ref, own, other):
        layer = (keep_ref[...] + got_ref[...].astype(f32)).astype(bf16)
        low, high = layer[:, :sub], layer[:, sub:]
        odd = meta_ref[1] % 2 == 1
        own[...] = jnp.where(odd, high, low)
        other[...] = jnp.where(odd, low, high)

    return pl.pallas_call(
        body,
        in_specs=[SMEM_SPEC] + many(VMEM_SPEC, 2),
        out_specs=many(VMEM_SPEC, 2),
        out_shape=[jax.ShapeDtypeStruct((rows_all, sub), bf16)] * 2,
        name="merge",
        compiler_params=grant(8),
        cost_estimate=cost(rows_all * half * 2, rows_all * half * 8),
    )(meta, keep, got)


def prepare_requests(block_rows, token_rows, peers, capacity):
    strips, lanes = block_rows.shape

    def body(block_ref, token_ref, wanted_ref, code_ref):
        before = (
            lax.broadcasted_iota(jnp.int32, (lanes, lanes), 0)
            < lax.broadcasted_iota(jnp.int32, (lanes, lanes), 1)
        ).astype(bf16)
        peer_ids = lax.broadcasted_iota(jnp.int32, (peers, lanes), 0)
        carry = jnp.zeros((peers, 1), f32)
        slots, lefts = [], []
        for i in range(strips):
            block = block_ref[i : i + 1, :]
            hit = (peer_ids == block).astype(f32)
            rank = dot(hit.astype(bf16), before) + carry
            carry = carry + jnp.sum(hit, axis=1, keepdims=True)
            slot = jnp.sum(rank * hit, axis=0, keepdims=True)
            slots.append(slot)
            code_ref[i : i + 1, :] = block * capacity + slot.astype(jnp.int32)
            token = token_ref[i : i + 1, :]
            coarse = (token // 32).astype(f32)
            fine = (token % 32).astype(f32)
            lefts.append(jnp.concatenate([hit * coarse, hit * fine], axis=0).astype(bf16))
        columns = jnp.transpose(jnp.concatenate(slots, axis=0))
        place = lax.broadcasted_iota(jnp.int32, (lanes, capacity), 1).astype(f32)
        total = jnp.zeros((2 * peers, capacity), f32)
        for i in range(strips):
            spot = (columns[:, i : i + 1] == place).astype(bf16)
            total = total + dot(lefts[i], spot)
        wanted_ref[...] = (total[:peers] * 32.0 + total[peers:]).astype(jnp.int32)

    return pl.pallas_call(
        body,
        in_specs=[VMEM_SPEC, VMEM_SPEC],
        out_specs=[VMEM_SPEC, VMEM_SPEC],
        out_shape=[
            jax.ShapeDtypeStruct((peers, capacity), jnp.int32),
            jax.ShapeDtypeStruct((strips, lanes), jnp.int32),
        ],
        name="prep",
        compiler_params=grant(8),
        cost_estimate=cost(2 * strips * lanes * lanes * capacity, 3 * strips * lanes * 4),
    )(block_rows, token_rows)


def spread_picks(spread, shift, width):
    clamped = jnp.minimum(jnp.maximum(spread - shift, -1.0), float(width)).astype(bf16)
    wide = jnp.concatenate([clamped] * (width // LANES), axis=1) if width > LANES else clamped[:, :width]
    place = lax.broadcasted_iota(jnp.int32, wide.shape, 1).astype(f32).astype(bf16)
    return jnp.where(wide == place, jnp.ones_like(place), jnp.zeros_like(place))


def gather_rows(meta, wanted, pieces, masks, tokens):
    peers, capacity = int(round(wanted.shape[0] ** 0.5)), wanted.shape[1]
    whole = not isinstance(pieces, list)
    flat = [pieces] if whole else [p for _, *pair in pieces for p in pair]
    sub = flat[0].shape[1]
    rows = flat[0].shape[0] if whole else sum(p.shape[0] for p in flat[::2])
    local_views = rows // tokens

    def body(meta_ref, wanted_ref, *refs):
        ins, outs = refs[: len(flat)], refs[len(flat) :]
        if whole:
            layer = ins[0]
        else:
            layer, outs = outs[0], outs[1:]
            end = jnp.logical_or(meta_ref[1] == 0, meta_ref[1] == meta_ref[2] - 1)
            for c, (views, _, _) in enumerate(pieces):
                for i, v in enumerate(views):
                    at = slice(i * tokens, (i + 1) * tokens)
                    layer[v * tokens : (v + 1) * tokens, :] = jnp.where(
                        end, ins[2 * c + 1][at, :], ins[2 * c][at, :]
                    )
        lines = [wanted_ref[pl.ds(m * peers + meta_ref[0], 1), :] for m in masks]
        lines += [lines[0]] * (-len(lines) % 8)
        columns = jnp.transpose(jnp.concatenate(lines, axis=0).astype(f32))
        for n in range(len(masks)):
            spread = jnp.broadcast_to(columns[:, n : n + 1], (capacity, LANES))
            pick = jnp.concatenate(
                [spread_picks(spread, float(v * tokens), tokens) for v in range(local_views)], axis=1
            )
            outs[n][...] = dot(pick, layer[...]).astype(bf16)

    out_shape = [jax.ShapeDtypeStruct((capacity, sub), bf16)] * len(masks)
    if not whole:
        out_shape = [jax.ShapeDtypeStruct((rows, sub), bf16)] + out_shape
    return pl.pallas_call(
        body,
        in_specs=[SMEM_SPEC] + many(VMEM_SPEC, 1 + len(flat)),
        out_specs=many(VMEM_SPEC, len(out_shape)),
        out_shape=out_shape,
        name="gath",
        compiler_params=grant(12),
        cost_estimate=cost(
            2 * len(masks) * capacity * rows * sub, 2 * (rows + len(masks) * capacity) * sub * 2
        ),
    )(meta, wanted, *flat)


def fetched_part(meta_ref, code_spread, masks, reps, capacity):
    pick = jnp.concatenate(
        [
            spread_picks(
                code_spread, (lax.bitwise_xor(meta_ref[0], mask) * capacity).astype(f32), capacity
            )
            for mask in masks
        ],
        axis=1,
    )
    return dot(pick, jnp.concatenate([r[...] for r in reps], axis=0))


def spread_column(turned, g, per, lanes):
    return jnp.concatenate(
        [
            jnp.broadcast_to(turned[:, g * per + j : g * per + j + 1], (lanes, LANES))
            for j in range(per)
        ],
        axis=0,
    )


def first_replies(meta, code, replies, tokens):
    masks = sorted(replies)
    capacity, sub = replies[masks[0]].shape
    strips, lanes = code.shape
    rows = strips * lanes
    per = tokens // lanes

    def body(meta_ref, code_ref, *refs):
        codes = jnp.transpose(code_ref[...].astype(f32))
        for g in range(rows // tokens):
            refs[-1][g * tokens : (g + 1) * tokens, :] = fetched_part(
                meta_ref, spread_column(codes, g, per, lanes), masks, refs[:-1], capacity
            ).astype(bf16)

    return pl.pallas_call(
        body,
        in_specs=[SMEM_SPEC] + many(VMEM_SPEC, 1 + len(masks)),
        out_specs=VMEM_SPEC,
        out_shape=jax.ShapeDtypeStruct((rows, sub), bf16),
        name="first",
        compiler_params=grant(12),
        cost_estimate=cost(2 * len(masks) * capacity * rows * sub, rows * sub * 4),
    )(meta, code, *[replies[m] for m in masks])


def finish_rows(meta, code, confidence, layer, early, replies, tokens):
    rows, sub = layer.shape
    masks = sorted(replies)
    capacity = replies[masks[0]].shape[0]
    _, lanes = code.shape
    blocks = rows // tokens
    per = tokens // lanes

    def body(meta_ref, code_ref, conf_ref, layer_ref, early_ref, *refs):
        reps, (out_hbm, buffer, sems) = refs[: len(masks)], refs[len(masks) :]
        codes = jnp.transpose(code_ref[...].astype(f32))
        confs = jnp.transpose(conf_ref[...]) * coupling
        copies = []
        for g in range(blocks):
            at = slice(g * tokens, (g + 1) * tokens)
            fetched = early_ref[at, :].astype(f32) + fetched_part(
                meta_ref, spread_column(codes, g, per, lanes), masks, reps, capacity
            )
            wide = layer_ref[at, :].astype(f32)
            weight = jnp.concatenate([spread_column(confs, g, per, lanes)] * (sub // LANES), axis=1)
            buffer[g] = wide + weight * (fetched - wide)
            copies.append(
                pltpu.make_async_copy(
                    buffer.at[g], out_hbm.at[pl.ds(g * tokens, tokens), :], sems.at[g]
                )
            )
            copies[-1].start()
        for copy in copies:
            copy.wait()

    return pl.pallas_call(
        body,
        in_specs=[SMEM_SPEC] + many(VMEM_SPEC, 4 + len(masks)),
        out_specs=ANY_SPEC,
        out_shape=jax.ShapeDtypeStruct((rows, sub), f32),
        scratch_shapes=[
            pltpu.VMEM((blocks, tokens, sub), f32),
            pltpu.SemaphoreType.DMA((blocks,)),
        ],
        name="fin",
        compiler_params=grant(12),
        cost_estimate=cost(2 * len(masks) * capacity * rows * sub, rows * sub * 8),
    )(meta, code, confidence, layer, early, *[replies[m] for m in masks])


def per_device(latents, norm_gain, w_qkv, w_out, intersection, match_block, match_row, confidence):
    local_views, tokens, width = latents.shape
    window = intersection.shape[1]
    sub = w_qkv.shape[2]
    peers = lax.axis_size(VIEWS)
    ends = lax.axis_size(HEADS)
    rows = local_views * tokens
    capacity = 2 * rows // peers
    assert local_views == 4 and window == 2 and ends == 4 and tokens == sub
    view_at, head_at = lax.axis_index(VIEWS), lax.axis_index(HEADS)
    spot = jnp.arange(4, dtype=jnp.int32)
    meta = jnp.where(spot == 0, view_at, jnp.where(spot == 1, head_at, ends)).astype(jnp.int32)

    def along(x, by):
        return lax.ppermute(x, VIEWS, [(i, (i + by) % peers) for i in range(peers)])

    def partner(x, mask):
        return lax.ppermute(x, VIEWS, [(i, i ^ mask) for i in range(peers)])

    def across(x, pairs):
        return lax.ppermute(x, HEADS, pairs)

    def after(x, done):
        return lax.optimization_barrier((x, done))[0]

    beside, middle, back = [(0, 1), (3, 2)], [(1, 2), (2, 1)], [(1, 0), (2, 3)]
    gain = norm_gain.reshape(1, width)
    inter = intersection.T
    w_near = across(w_out, beside)
    far = {}
    projected, edge_halves, weights, inner_latents = project_views(
        meta, latents, gain, w_qkv, (0, 3), (1, 2)
    )
    far["n1"] = along(projected[0][1], -1)
    far["p1"] = along(projected[3][1], 1)
    more, inner_halves = project_views(meta, inner_latents, gain, weights, (1, 2))
    projected.update(more)
    queries = {v: projected[v][0] for v in range(local_views)}
    blocks = {v: projected[v][1] for v in range(local_views)}
    far["n2"] = along(blocks[1], -1)
    far["p2"] = along(blocks[2], 1)
    base = {0: (edge_halves, 0), 3: (edge_halves, 1), 1: (inner_halves, 0), 2: (inner_halves, 1)}

    inner_plan = [(1, [("p1", -1, 1)]), (2, [("n1", 2, 1)])]
    inner_queries = [queries[1], queries[2]]
    local = attend(
        meta, inter, inner_queries, blocks, {}, [(v, []) for v, _ in inner_plan], window, last=False
    )
    attended = {}
    inner = []
    for n in range(2):
        view, sources = inner_plan[n]
        query = inner_queries[n] if n == 0 else after(inner_queries[n], inner[0])
        inner += attend(
            meta,
            inter,
            [query],
            blocks,
            {s[0]: far[s[0]] for s in sources},
            [(view, sources)],
            window,
            earlier=tuple(local),
            slot=n,
        )
    attended["a"], second = inner

    def attend_outer(view, sources, done, carry=None):
        (result,) = attend(
            meta,
            inter,
            [after(queries[view], done)],
            blocks,
            {s[0]: far[s[0]] for s in sources},
            [(view, sources)],
            window,
            carry=carry,
        )
        return result

    keep, sent, got = {}, {}, {}

    def pass_on(c):
        near = across(attended[c], beside)
        keep[c], sent[c] = partial_out(
            meta,
            attended[c],
            near,
            w_out,
            w_near,
            [base[v] for v in CHUNKS[c]],
        )
        got[c] = across(sent[c], middle)

    attended["b"] = attend_outer(0, [("p1", -1, 0), ("p2", -2, 1)], attended["a"], second)
    pass_on("a")
    attended["c"] = attend_outer(3, [("n1", 3, 0), ("n2", 3, 1)], sent["a"])
    pass_on("b")
    pass_on("c")
    strips = rows // LANES
    wanted, code = prepare_requests(
        after(match_block.reshape(strips, LANES), sent["c"]),
        match_row.reshape(strips, LANES),
        peers,
        capacity,
    )
    mask = 1
    while mask < peers:
        wanted = jnp.concatenate([wanted, partner(wanted, mask)], axis=0)
        mask *= 2
    pieces = []
    for c in CHUNKS:
        own, other = merge_out(meta, keep[c], got[c])
        pieces.append((CHUNKS[c], own, across(other, back)))

    first_masks, last_masks = reply_order(peers)
    replies = {}

    def reply(masks, outgoing):
        for mask, rows_out in zip(masks, outgoing):
            replies[mask] = partner(rows_out, mask)

    layer, *outgoing = gather_rows(meta, wanted, pieces, first_masks, tokens)
    reply(first_masks, outgoing)
    *outgoing, own_rows = gather_rows(meta, wanted, layer, last_masks + [0], tokens)
    reply(last_masks, outgoing)
    late = [m for m in last_masks if m > 1]
    early = first_replies(
        meta, code, {0: own_rows, **{m: r for m, r in replies.items() if m not in late}}, tokens
    )
    refined = finish_rows(
        meta,
        code,
        confidence.reshape(strips, LANES),
        layer,
        early,
        {m: replies[m] for m in late},
        tokens,
    )
    return refined.reshape(local_views, tokens, sub)


def reply_order(peers):
    far_half = list(range(peers // 2, peers))
    far_half = far_half[len(far_half) // 2 :] + far_half[: len(far_half) // 2]
    pairs = zip(far_half[: len(far_half) // 2], far_half[len(far_half) // 2 :])
    return [m for pair in pairs for m in pair], list(range(2, peers // 2)) + [1]


def solution(mesh):
    in_specs = (
        P(VIEWS, None, None),
        P(),
        P(None, None, HEADS),
        P(HEADS, None),
        P(),
        P(VIEWS, None),
        P(VIEWS),
        P(VIEWS),
    )
    out_specs = P(VIEWS, None, HEADS)
    return jax.shard_map(
        per_device, mesh=mesh, in_specs=in_specs, out_specs=out_specs, check_vma=False
    )
```

```python
import jax
import jax.numpy as jnp
from jax import lax
from jax.experimental import pallas as pl
from jax.experimental.pallas import tpu as pltpu
from jax.sharding import PartitionSpec as P


VIEWS, HEADS = "views", "heads"
HEAD_DIM = 64
LANES = 128
STAGED = 3
GRANT_A, GRANT_B = 50, 40
CHUNKS = dict(a=(1,), b=(2, 0), c=(3,))

coupling = 0.5
epsilon = 1e-06

bf16 = jnp.bfloat16
f32 = jnp.float32


def cost(flops, bytes_accessed, transcendentals=0):
    return pl.CostEstimate(
        flops=int(flops), bytes_accessed=int(bytes_accessed), transcendentals=int(transcendentals)
    )


def dot(a, b):
    return jnp.dot(a, b, preferred_element_type=f32)


VMEM_SPEC = pl.BlockSpec(memory_space=pltpu.VMEM)
SMEM_SPEC = pl.BlockSpec(memory_space=pltpu.SMEM)
ANY_SPEC = pl.BlockSpec(memory_space=pl.ANY)


def grant(mib):
    return pltpu.CompilerParams(vmem_limit_bytes=mib << 20)


def many(spec, count):
    return [spec] * count


def project_views(meta, latents, gain, w_qkv, which, following=()):
    tokens, width = latents.shape[1:]
    sub = w_qkv.shape[2]
    count, ahead = len(which), len(following)
    scale = HEAD_DIM ** (-0.5)

    def body(meta_ref, lat_ref, gain_ref, w_ref, *refs):
        outs, refs = refs[: 2 * count], refs[2 * count :]
        halves, refs = refs[0], refs[1:]
        ws, source = (refs[0], refs[2]) if ahead else (w_ref, lat_ref)
        sems = refs[-1]
        here = pl.ds(pl.multiple_of((meta_ref[1] // 2) * (width // 2), width // 2), width // 2)
        kept = [
            pltpu.make_async_copy(source.at[i, :, here], halves.at[i], sems.at[i])
            for i in range(count)
        ]
        queue, loads, parts = [], [], []
        if ahead:
            loads = [
                pltpu.make_async_copy(lat_ref.at[v], source.at[i], sems.at[count + i])
                for i, v in enumerate(which)
            ]
            parts = [
                pltpu.make_async_copy(w_ref.at[p], ws.at[p], sems.at[2 * count + p]) for p in range(3)
            ]
            later = [
                pltpu.make_async_copy(lat_ref.at[v], refs[1].at[i], sems.at[2 * count + 3 + i])
                for i, v in enumerate(following)
            ]
            queue = loads + [parts[2], parts[1], parts[0]] + later
        for copy in queue[:STAGED]:
            copy.start()
        waiting = queue[STAGED:]

        def arrive(copy):
            copy.wait()
            if waiting:
                waiting.pop(0).start()

        normed = []
        for i in range(count):
            if ahead:
                arrive(loads[i])
            kept[i].start()
            wide = source[i].astype(f32)
            mean_square = jnp.mean(wide * wide, axis=-1, keepdims=True)
            normed.append((wide * lax.rsqrt(mean_square + epsilon) * gain_ref[...]).astype(bf16))
        for part in (2, 1, 0):
            if ahead:
                arrive(parts[part])
            for i in range(count):
                product = dot(normed[i], ws[part])
                if part == 2:
                    outs[2 * i + 1][1] = jnp.transpose(product).astype(bf16)
                elif part == 1:
                    outs[2 * i + 1][0] = product.astype(bf16)
                else:
                    outs[2 * i][...] = jnp.transpose(product).astype(bf16) * jnp.asarray(scale, bf16)
        for copy in kept + (later if ahead else []):
            copy.wait()

    out_shape = []
    for _ in which:
        out_shape += [
            jax.ShapeDtypeStruct((sub, tokens), bf16),
            jax.ShapeDtypeStruct((2, tokens, sub), bf16),
        ]
    out_shape.append(jax.ShapeDtypeStruct((count, tokens, width // 2), bf16))
    scratch = [pltpu.SemaphoreType.DMA((2 * count + 3 + ahead,))]
    if ahead:
        out_shape.append(jax.ShapeDtypeStruct(w_qkv.shape, bf16))
        out_shape.append(jax.ShapeDtypeStruct((ahead, tokens, width), bf16))
        scratch = [pltpu.VMEM((count, tokens, width), bf16)] + scratch
    big = ANY_SPEC if ahead else VMEM_SPEC
    outs = pl.pallas_call(
        body,
        in_specs=[SMEM_SPEC, big, VMEM_SPEC, big],
        out_specs=many(VMEM_SPEC, len(out_shape)),
        out_shape=out_shape,
        scratch_shapes=scratch,
        name="proj",
        compiler_params=grant(GRANT_A if ahead else GRANT_B),
        cost_estimate=cost(
            count * 6 * tokens * width * sub, count * tokens * (width + 3 * sub) * 2 + 6 * width * sub
        ),
    )(meta, latents, gain, w_qkv)
    views = {v: (outs[2 * i], outs[2 * i + 1]) for i, v in enumerate(which)}
    return views, *outs[2 * count :]


ONES = 16
SAFE_TOTAL = 1e30
FAR = 1e30


def head_scores(q_ref, kv_ref, h):
    per = LANES // HEAD_DIM
    j, slot = h // per, h % per
    own = q_ref[h * HEAD_DIM : (h + 1) * HEAD_DIM, :]
    zero = jnp.zeros_like(own)
    padded = jnp.concatenate([own if s == slot else zero for s in range(per)], axis=0)
    return dot(kv_ref[0, :, j * LANES : (j + 1) * LANES], padded)


def head_values(kv_ref, h):
    rows = kv_ref[1, h * HEAD_DIM : (h + 1) * HEAD_DIM, :]
    return jnp.concatenate([rows, jnp.ones((ONES, rows.shape[1]), bf16)], axis=0)


def attention_cost(tokens, sub, pairs):
    heads = sub // HEAD_DIM
    return cost(
        pairs * heads * tokens * tokens * 4 * LANES,
        pairs * tokens * sub * 8,
        pairs * heads * tokens * tokens,
    )


def far_if_absent(inter_ref, at, offset):
    return jnp.where(inter_ref[offset, at] > 0, 0.0, FAR).astype(f32)


def sources_of(view, local_views, window):
    found = []
    for o in range(window):
        if view + o + 1 < local_views:
            found.append((view + o + 1, view, o))
        if view - o - 1 >= 0:
            found.append((view - o - 1, view - o - 1, o))
    return found


def attend(
    meta, inter, queries, blocks, remote, plan, window, earlier=None, last=True, carry=None
):
    local_views = len(blocks)
    sub, tokens = queries[0].shape
    heads = sub // HEAD_DIM
    tall = HEAD_DIM + ONES
    views_total = inter.shape[1]
    names = sorted(remote)
    count = len(plan)
    held = 0 if earlier is None else 2

    def body(meta_ref, inter_ref, *refs):
        before, refs = refs[:held], refs[held:]
        qs, refs = refs[:count], refs[count:]
        kvs, refs = refs[:local_views], refs[local_views:]
        far_kvs, refs = dict(zip(names, refs[: len(names)])), refs[len(names) :]
        first = meta_ref[0] * local_views

        def global_view(source):
            at = first + source
            return jnp.where(at < 0, at + views_total, at) if source < 0 else at

        def keys_of(i):
            view, sources = plan[i]
            keys = [] if held else [(kvs[view], None, None)]
            if not held:
                keys += [(kvs[t], source, o) for t, source, o in sources_of(view, local_views, window)]
            return keys + [(far_kvs[name], source, o) for name, source, o in sources]

        if last and carry is not None:
            refs[1][0] = refs[0][...]
            outs, refs = [refs[1].at[1 + i] for i in range(count)], refs[1:]
        elif last:
            outs = refs[:count]
        units = [(i, h, k) for i in range(count) for h in range(heads) for k in keys_of(i)]
        far = {}
        for _, _, (_, source, o) in units:
            if source is not None and (source, o) not in far:
                far[source, o] = far_if_absent(inter_ref, global_view(source), o)
        upcoming = head_scores(qs[units[0][0]], units[0][2][0], units[0][1])
        worst = jnp.zeros((1, tokens), f32)
        n = 0
        for i, (view, _) in enumerate(plan):
            parts = []
            for h in range(heads):
                keys = keys_of(i)
                weights = []
                top = before[1][i, h : h + 1, :] if held else None
                for _, source, o in keys:
                    scores = upcoming
                    n += 1
                    if n < len(units):
                        ni, nh, (nk, _, _) = units[n]
                        upcoming = head_scores(qs[ni], nk, nh)
                    if source is None:
                        top = jnp.max(scores, axis=0, keepdims=True)
                        shift = top
                    else:
                        shift = top + far[source, o]
                    weights.append(jnp.exp(scores - shift).astype(bf16))
                values = jnp.concatenate([head_values(k[0], h) for k in keys], axis=1)
                sums = dot(values, jnp.concatenate(weights, axis=0))
                if held:
                    sums = sums + before[0][i, h * tall : (h + 1) * tall, :]
                if not last:
                    refs[0][i, h * tall : (h + 1) * tall, :] = sums
                    refs[1][i, h : h + 1, :] = top
                    continue
                total = sums[HEAD_DIM : HEAD_DIM + 1, :]
                worst = jnp.maximum(worst, jnp.where(total < SAFE_TOTAL, 0.0, 1.0))
                parts.append(sums[:HEAD_DIM, :] * (1.0 / total))
            if last:
                outs[i][...] = jnp.transpose(jnp.concatenate(parts, axis=0)).astype(bf16)
        if not last:
            return
        work, work_stat = refs[-2:]

        @pl.when(jnp.max(worst) > 0.0)
        def _():
            for i, (view, sources) in enumerate(plan):
                exact_add(qs[i], kvs[view], work, work_stat, heads, True)
                every = [(kvs[t], s, o) for t, s, o in sources_of(view, local_views, window)]
                every += [(far_kvs[name], s, o) for name, s, o in sources]
                for kv, source, o in every:

                    @pl.when(inter_ref[o, global_view(source)] > 0)
                    def _(i=i, kv=kv):
                        exact_add(qs[i], kv, work, work_stat, heads, False)

                parts = []
                for h in range(heads):
                    total = work_stat[h, 1:2, :]
                    parts.append(work[h * HEAD_DIM : (h + 1) * HEAD_DIM, :] * (1.0 / total))
                outs[i][...] = jnp.transpose(jnp.concatenate(parts, axis=0)).astype(bf16)

    if last:
        out_shape = [jax.ShapeDtypeStruct((tokens, sub), bf16)] * count
        if carry is not None:
            out_shape = [jax.ShapeDtypeStruct((1 + count, tokens, sub), bf16)]
        scratch = [pltpu.VMEM((sub, tokens), f32), pltpu.VMEM((heads, 8, tokens), f32)]
    else:
        out_shape = [
            jax.ShapeDtypeStruct((count, heads * tall, tokens), f32),
            jax.ShapeDtypeStruct((count, heads, tokens), f32),
        ]
        scratch = []
    pairs = sum(len(s) for _, s in plan)
    if not held:
        pairs += sum(1 + len(sources_of(v, local_views, window)) for v, _ in plan)
    return pl.pallas_call(
        body,
        in_specs=[SMEM_SPEC, SMEM_SPEC]
        + many(VMEM_SPEC, held + count + local_views + len(names) + (carry is not None)),
        out_specs=many(VMEM_SPEC, len(out_shape)),
        out_shape=out_shape,
        scratch_shapes=scratch,
        name="att",
        compiler_params=grant(12),
        cost_estimate=attention_cost(tokens, sub, pairs),
    )(
        meta,
        inter,
        *(earlier or ()),
        *queries,
        *[blocks[v] for v in range(local_views)],
        *[remote[name] for name in names],
        *(() if carry is None else (carry,)),
    )


def exact_add(q_ref, kv_ref, work, work_stat, heads, start):
    per = LANES // HEAD_DIM

    def one_head(h, _):
        base = pl.multiple_of((h // per) * LANES, LANES)
        queries = q_ref[pl.ds(base, LANES), :]
        owner = lax.broadcasted_iota(jnp.int32, queries.shape, 0) // HEAD_DIM
        queries = jnp.where(owner == h % per, queries.astype(f32), 0.0).astype(bf16)
        scores = dot(kv_ref[0, :, pl.ds(base, LANES)], queries)
        top = jnp.max(scores, axis=0, keepdims=True)
        rows = pl.ds(pl.multiple_of(h * HEAD_DIM, HEAD_DIM), HEAD_DIM)
        values = kv_ref[1, rows, :]
        if not start:
            old = work_stat[h, 0:1, :]
            top = jnp.maximum(old, top)
        weights = jnp.exp(scores - top)
        total = jnp.sum(weights, axis=0, keepdims=True)
        sums = dot(values, weights.astype(bf16))
        if not start:
            fade = jnp.exp(old - top)
            total = total + work_stat[h, 1:2, :] * fade
            sums = sums + work[rows, :] * fade
        work_stat[h, 0:1, :] = top
        work_stat[h, 1:2, :] = total
        work[rows, :] = sums
        return 0

    lax.fori_loop(0, heads, one_head, 0)


def partial_out(meta, attended, near, w_own, w_near, base):
    sub = attended.shape[-1]
    rows_all = attended.size // sub
    width = w_own.shape[1]
    half = width // 2

    def body(meta_ref, att, near_ref, own_ref, near_w_ref, *refs):
        keep, send = refs[-2:]
        side = meta_ref[1] // 2
        here = pl.ds(pl.multiple_of(side * half, half), half)
        away = pl.ds(pl.multiple_of((1 - side) * half, half), half)
        rows = jnp.concatenate([x[...].reshape(rows_all, sub) for x in (att, near_ref)], axis=1)

        def columns(at):
            return jnp.concatenate([own_ref[:, at], near_w_ref[:, at]], axis=0)

        send[...] = dot(rows, columns(away)).astype(bf16)
        total = dot(rows, columns(here))
        start = jnp.concatenate([ref[place] for ref, (_, place) in zip(refs, base)], axis=0)
        keep[...] = start.astype(f32) + total

    return pl.pallas_call(
        body,
        in_specs=[SMEM_SPEC] + many(VMEM_SPEC, 4 + len(base)),
        out_specs=many(VMEM_SPEC, 2),
        out_shape=[
            jax.ShapeDtypeStruct((rows_all, half), f32),
            jax.ShapeDtypeStruct((rows_all, half), bf16),
        ],
        name="part",
        compiler_params=grant(12),
        cost_estimate=cost(4 * rows_all * sub * width, 4 * sub * width + rows_all * width * 6),
    )(meta, attended, near, w_own, w_near, *[array for array, _ in base])


def merge_out(meta, keep, got):
    rows_all, half = keep.shape
    sub = half // 2

    def body(meta_ref, keep_ref, got_ref, own, other):
        layer = (keep_ref[...] + got_ref[...].astype(f32)).astype(bf16)
        low, high = layer[:, :sub], layer[:, sub:]
        odd = meta_ref[1] % 2 == 1
        own[...] = jnp.where(odd, high, low)
        other[...] = jnp.where(odd, low, high)

    return pl.pallas_call(
        body,
        in_specs=[SMEM_SPEC] + many(VMEM_SPEC, 2),
        out_specs=many(VMEM_SPEC, 2),
        out_shape=[jax.ShapeDtypeStruct((rows_all, sub), bf16)] * 2,
        name="merge",
        compiler_params=grant(8),
        cost_estimate=cost(rows_all * half * 2, rows_all * half * 8),
    )(meta, keep, got)


def prepare_requests(block_rows, token_rows, peers, capacity):
    strips, lanes = block_rows.shape

    def body(block_ref, token_ref, wanted_ref, code_ref):
        before = (
            lax.broadcasted_iota(jnp.int32, (lanes, lanes), 0)
            < lax.broadcasted_iota(jnp.int32, (lanes, lanes), 1)
        ).astype(bf16)
        peer_ids = lax.broadcasted_iota(jnp.int32, (peers, lanes), 0)
        carry = jnp.zeros((peers, 1), f32)
        slots, lefts = [], []
        for i in range(strips):
            block = block_ref[i : i + 1, :]
            hit = (peer_ids == block).astype(f32)
            rank = dot(hit.astype(bf16), before) + carry
            carry = carry + jnp.sum(hit, axis=1, keepdims=True)
            slot = jnp.sum(rank * hit, axis=0, keepdims=True)
            slots.append(slot)
            code_ref[i : i + 1, :] = block * capacity + slot.astype(jnp.int32)
            token = token_ref[i : i + 1, :]
            coarse = (token // 32).astype(f32)
            fine = (token % 32).astype(f32)
            lefts.append(jnp.concatenate([hit * coarse, hit * fine], axis=0).astype(bf16))
        columns = jnp.transpose(jnp.concatenate(slots, axis=0))
        place = lax.broadcasted_iota(jnp.int32, (lanes, capacity), 1).astype(f32)
        total = jnp.zeros((2 * peers, capacity), f32)
        for i in range(strips):
            spot = (columns[:, i : i + 1] == place).astype(bf16)
            total = total + dot(lefts[i], spot)
        wanted_ref[...] = (total[:peers] * 32.0 + total[peers:]).astype(jnp.int32)

    return pl.pallas_call(
        body,
        in_specs=[VMEM_SPEC, VMEM_SPEC],
        out_specs=[VMEM_SPEC, VMEM_SPEC],
        out_shape=[
            jax.ShapeDtypeStruct((peers, capacity), jnp.int32),
            jax.ShapeDtypeStruct((strips, lanes), jnp.int32),
        ],
        name="prep",
        compiler_params=grant(8),
        cost_estimate=cost(2 * strips * lanes * lanes * capacity, 3 * strips * lanes * 4),
    )(block_rows, token_rows)


def spread_picks(spread, shift, width):
    clamped = jnp.minimum(jnp.maximum(spread - shift, -1.0), float(width)).astype(bf16)
    wide = jnp.concatenate([clamped] * (width // LANES), axis=1) if width > LANES else clamped[:, :width]
    place = lax.broadcasted_iota(jnp.int32, wide.shape, 1).astype(f32).astype(bf16)
    return jnp.where(wide == place, jnp.ones_like(place), jnp.zeros_like(place))


def gather_rows(meta, wanted, pieces, masks, tokens):
    peers, capacity = int(round(wanted.shape[0] ** 0.5)), wanted.shape[1]
    whole = not isinstance(pieces, list)
    flat = [pieces] if whole else [p for _, *pair in pieces for p in pair]
    sub = flat[0].shape[1]
    rows = flat[0].shape[0] if whole else sum(p.shape[0] for p in flat[::2])
    local_views = rows // tokens

    def body(meta_ref, wanted_ref, *refs):
        ins, outs = refs[: len(flat)], refs[len(flat) :]
        if whole:
            layer = ins[0]
        else:
            layer, outs = outs[0], outs[1:]
            end = jnp.logical_or(meta_ref[1] == 0, meta_ref[1] == meta_ref[2] - 1)
            for c, (views, _, _) in enumerate(pieces):
                for i, v in enumerate(views):
                    at = slice(i * tokens, (i + 1) * tokens)
                    layer[v * tokens : (v + 1) * tokens, :] = jnp.where(
                        end, ins[2 * c + 1][at, :], ins[2 * c][at, :]
                    )
        lines = [wanted_ref[pl.ds(m * peers + meta_ref[0], 1), :] for m in masks]
        lines += [lines[0]] * (-len(lines) % 8)
        columns = jnp.transpose(jnp.concatenate(lines, axis=0).astype(f32))
        for n in range(len(masks)):
            spread = jnp.broadcast_to(columns[:, n : n + 1], (capacity, LANES))
            pick = jnp.concatenate(
                [spread_picks(spread, float(v * tokens), tokens) for v in range(local_views)], axis=1
            )
            outs[n][...] = dot(pick, layer[...]).astype(bf16)

    out_shape = [jax.ShapeDtypeStruct((capacity, sub), bf16)] * len(masks)
    if not whole:
        out_shape = [jax.ShapeDtypeStruct((rows, sub), bf16)] + out_shape
    return pl.pallas_call(
        body,
        in_specs=[SMEM_SPEC] + many(VMEM_SPEC, 1 + len(flat)),
        out_specs=many(VMEM_SPEC, len(out_shape)),
        out_shape=out_shape,
        name="gath",
        compiler_params=grant(12),
        cost_estimate=cost(
            2 * len(masks) * capacity * rows * sub, 2 * (rows + len(masks) * capacity) * sub * 2
        ),
    )(meta, wanted, *flat)


def fetched_part(meta_ref, code_spread, masks, reps, capacity):
    pick = jnp.concatenate(
        [
            spread_picks(
                code_spread, (lax.bitwise_xor(meta_ref[0], mask) * capacity).astype(f32), capacity
            )
            for mask in masks
        ],
        axis=1,
    )
    return dot(pick, jnp.concatenate([r[...] for r in reps], axis=0))


def spread_column(turned, g, per, lanes):
    return jnp.concatenate(
        [
            jnp.broadcast_to(turned[:, g * per + j : g * per + j + 1], (lanes, LANES))
            for j in range(per)
        ],
        axis=0,
    )


def first_replies(meta, code, replies, tokens):
    masks = sorted(replies)
    capacity, sub = replies[masks[0]].shape
    strips, lanes = code.shape
    rows = strips * lanes
    per = tokens // lanes

    def body(meta_ref, code_ref, *refs):
        codes = jnp.transpose(code_ref[...].astype(f32))
        for g in range(rows // tokens):
            refs[-1][g * tokens : (g + 1) * tokens, :] = fetched_part(
                meta_ref, spread_column(codes, g, per, lanes), masks, refs[:-1], capacity
            ).astype(bf16)

    return pl.pallas_call(
        body,
        in_specs=[SMEM_SPEC] + many(VMEM_SPEC, 1 + len(masks)),
        out_specs=VMEM_SPEC,
        out_shape=jax.ShapeDtypeStruct((rows, sub), bf16),
        name="first",
        compiler_params=grant(12),
        cost_estimate=cost(2 * len(masks) * capacity * rows * sub, rows * sub * 4),
    )(meta, code, *[replies[m] for m in masks])


def finish_rows(meta, code, confidence, layer, early, replies, tokens):
    rows, sub = layer.shape
    masks = sorted(replies)
    capacity = replies[masks[0]].shape[0]
    _, lanes = code.shape
    blocks = rows // tokens
    per = tokens // lanes

    def body(meta_ref, code_ref, conf_ref, layer_ref, early_ref, *refs):
        reps, (out_hbm, buffer, sems) = refs[: len(masks)], refs[len(masks) :]
        codes = jnp.transpose(code_ref[...].astype(f32))
        confs = jnp.transpose(conf_ref[...]) * coupling
        copies = []
        for g in range(blocks):
            at = slice(g * tokens, (g + 1) * tokens)
            fetched = early_ref[at, :].astype(f32) + fetched_part(
                meta_ref, spread_column(codes, g, per, lanes), masks, reps, capacity
            )
            wide = layer_ref[at, :].astype(f32)
            weight = jnp.concatenate([spread_column(confs, g, per, lanes)] * (sub // LANES), axis=1)
            buffer[g] = wide + weight * (fetched - wide)
            copies.append(
                pltpu.make_async_copy(
                    buffer.at[g], out_hbm.at[pl.ds(g * tokens, tokens), :], sems.at[g]
                )
            )
            copies[-1].start()
        for copy in copies:
            copy.wait()

    return pl.pallas_call(
        body,
        in_specs=[SMEM_SPEC] + many(VMEM_SPEC, 4 + len(masks)),
        out_specs=ANY_SPEC,
        out_shape=jax.ShapeDtypeStruct((rows, sub), f32),
        scratch_shapes=[
            pltpu.VMEM((blocks, tokens, sub), f32),
            pltpu.SemaphoreType.DMA((blocks,)),
        ],
        name="fin",
        compiler_params=grant(12),
        cost_estimate=cost(2 * len(masks) * capacity * rows * sub, rows * sub * 8),
    )(meta, code, confidence, layer, early, *[replies[m] for m in masks])


def per_device(latents, norm_gain, w_qkv, w_out, intersection, match_block, match_row, confidence):
    local_views, tokens, width = latents.shape
    window = intersection.shape[1]
    sub = w_qkv.shape[2]
    peers = lax.axis_size(VIEWS)
    ends = lax.axis_size(HEADS)
    rows = local_views * tokens
    capacity = 2 * rows // peers
    assert local_views == 4 and window == 2 and ends == 4 and tokens == sub
    view_at, head_at = lax.axis_index(VIEWS), lax.axis_index(HEADS)
    spot = jnp.arange(4, dtype=jnp.int32)
    meta = jnp.where(spot == 0, view_at, jnp.where(spot == 1, head_at, ends)).astype(jnp.int32)

    def along(x, by):
        return lax.ppermute(x, VIEWS, [(i, (i + by) % peers) for i in range(peers)])

    def partner(x, mask):
        return lax.ppermute(x, VIEWS, [(i, i ^ mask) for i in range(peers)])

    def across(x, pairs):
        return lax.ppermute(x, HEADS, pairs)

    def after(x, done):
        return lax.optimization_barrier((x, done))[0]

    beside, middle, back = [(0, 1), (3, 2)], [(1, 2), (2, 1)], [(1, 0), (2, 3)]
    gain = norm_gain.reshape(1, width)
    inter = intersection.T
    w_near = across(w_out, beside)
    far = {}
    projected, edge_halves, weights, inner_latents = project_views(
        meta, latents, gain, w_qkv, (0, 3), (1, 2)
    )
    far["n1"] = along(projected[0][1], -1)
    far["p1"] = along(projected[3][1], 1)
    more, inner_halves = project_views(meta, inner_latents, gain, weights, (1, 2))
    projected.update(more)
    queries = {v: projected[v][0] for v in range(local_views)}
    blocks = {v: projected[v][1] for v in range(local_views)}
    far["n2"] = along(blocks[1], -1)
    far["p2"] = along(blocks[2], 1)
    base = {0: (edge_halves, 0), 3: (edge_halves, 1), 1: (inner_halves, 0), 2: (inner_halves, 1)}

    inner_plan = [(1, [("p1", -1, 1)]), (2, [("n1", 2, 1)])]
    inner_queries = [queries[1], queries[2]]
    local = attend(
        meta, inter, inner_queries, blocks, {}, [(v, []) for v, _ in inner_plan], window, last=False
    )
    attended = {}
    attended["a"], second = attend(
        meta, inter, inner_queries, blocks, dict(n1=far["n1"], p1=far["p1"]), inner_plan, window,
        earlier=tuple(local),
    )

    def attend_outer(view, sources, done, carry=None):
        (result,) = attend(
            meta,
            inter,
            [after(queries[view], done)],
            blocks,
            {s[0]: far[s[0]] for s in sources},
            [(view, sources)],
            window,
            carry=carry,
        )
        return result

    keep, sent, got = {}, {}, {}

    def pass_on(c):
        near = across(attended[c], beside)
        keep[c], sent[c] = partial_out(
            meta,
            attended[c],
            near,
            w_out,
            w_near,
            [base[v] for v in CHUNKS[c]],
        )
        got[c] = across(sent[c], middle)

    attended["b"] = attend_outer(0, [("p1", -1, 0), ("p2", -2, 1)], attended["a"], second)
    pass_on("a")
    attended["c"] = attend_outer(3, [("n1", 3, 0), ("n2", 3, 1)], sent["a"])
    pass_on("b")
    pass_on("c")
    strips = rows // LANES
    wanted, code = prepare_requests(
        after(match_block.reshape(strips, LANES), sent["b"]),
        match_row.reshape(strips, LANES),
        peers,
        capacity,
    )
    mask = 1
    while mask < peers:
        wanted = jnp.concatenate([wanted, partner(wanted, mask)], axis=0)
        mask *= 2
    pieces = []
    for c in CHUNKS:
        own, other = merge_out(meta, keep[c], got[c])
        pieces.append((CHUNKS[c], own, across(other, back)))

    groups = reply_groups(peers)
    replies, layer = {}, pieces
    for n, masks in enumerate(groups):
        found = gather_rows(meta, wanted, layer, masks, tokens)
        if n == 0:
            layer, *found = found
        for mask, rows_out in zip(masks, found):
            replies[mask] = partner(rows_out, mask) if mask else rows_out
    late = late_masks(peers)
    early = first_replies(meta, code, {m: r for m, r in replies.items() if m not in late}, tokens)
    refined = finish_rows(
        meta,
        code,
        confidence.reshape(strips, LANES),
        layer,
        early,
        {m: replies[m] for m in late},
        tokens,
    )
    return refined.reshape(local_views, tokens, sub)


def late_masks(peers):
    return list(range(3 * peers // 4, peers))


def reply_groups(peers):
    quarter, half = list(range(peers // 4, peers // 2)), list(range(peers // 2, 3 * peers // 4))
    pairs = [m for pair in zip(half, quarter) for m in pair]
    return [pairs[: len(quarter)], pairs[len(quarter) :], late_masks(peers) + list(range(1, peers // 4)) + [0]]


def solution(mesh):
    in_specs = (
        P(VIEWS, None, None),
        P(),
        P(None, None, HEADS),
        P(HEADS, None),
        P(),
        P(VIEWS, None),
        P(VIEWS),
        P(VIEWS),
    )
    out_specs = P(VIEWS, None, HEADS)
    return jax.shard_map(
        per_device, mesh=mesh, in_specs=in_specs, out_specs=out_specs, check_vma=False
    )
```

```python
import jax
import jax.numpy as jnp
from jax import lax
from jax.experimental import pallas as pl
from jax.experimental.pallas import tpu as pltpu
from jax.sharding import PartitionSpec as P


VIEWS, HEADS = "views", "heads"
HEAD_DIM = 64
LANES = 128
STAGED = 3
GRANT_A, GRANT_B = 50, 40
CHUNKS = dict(a=(1,), b=(2, 0), c=(3,))

coupling = 0.5
epsilon = 1e-06

bf16 = jnp.bfloat16
f32 = jnp.float32


def cost(flops, bytes_accessed, transcendentals=0):
    return pl.CostEstimate(
        flops=int(flops), bytes_accessed=int(bytes_accessed), transcendentals=int(transcendentals)
    )


def dot(a, b):
    return jnp.dot(a, b, preferred_element_type=f32)


VMEM_SPEC = pl.BlockSpec(memory_space=pltpu.VMEM)
SMEM_SPEC = pl.BlockSpec(memory_space=pltpu.SMEM)
ANY_SPEC = pl.BlockSpec(memory_space=pl.ANY)


def grant(mib):
    return pltpu.CompilerParams(vmem_limit_bytes=mib << 20)


def many(spec, count):
    return [spec] * count


def project_views(meta, latents, gain, w_qkv, which, following=()):
    tokens, width = latents.shape[1:]
    sub = w_qkv.shape[2]
    count, ahead = len(which), len(following)
    scale = HEAD_DIM ** (-0.5)

    def body(meta_ref, lat_ref, gain_ref, w_ref, *refs):
        outs, refs = refs[: 2 * count], refs[2 * count :]
        halves, refs = refs[0], refs[1:]
        ws, source = (refs[0], refs[2]) if ahead else (w_ref, lat_ref)
        sems = refs[-1]
        here = pl.ds(pl.multiple_of((meta_ref[1] // 2) * (width // 2), width // 2), width // 2)
        kept = [
            pltpu.make_async_copy(source.at[i, :, here], halves.at[i], sems.at[i])
            for i in range(count)
        ]
        queue, loads, parts = [], [], []
        if ahead:
            loads = [
                pltpu.make_async_copy(lat_ref.at[v], source.at[i], sems.at[count + i])
                for i, v in enumerate(which)
            ]
            parts = [
                pltpu.make_async_copy(w_ref.at[p], ws.at[p], sems.at[2 * count + p]) for p in range(3)
            ]
            later = [
                pltpu.make_async_copy(lat_ref.at[v], refs[1].at[i], sems.at[2 * count + 3 + i])
                for i, v in enumerate(following)
            ]
            queue = loads + [parts[2], parts[1], parts[0]] + later
        for copy in queue[:STAGED]:
            copy.start()
        waiting = queue[STAGED:]

        def arrive(copy):
            copy.wait()
            if waiting:
                waiting.pop(0).start()

        normed = []
        for i in range(count):
            if ahead:
                arrive(loads[i])
            kept[i].start()
            wide = source[i].astype(f32)
            mean_square = jnp.mean(wide * wide, axis=-1, keepdims=True)
            normed.append((wide * lax.rsqrt(mean_square + epsilon) * gain_ref[...]).astype(bf16))
        for part in (2, 1, 0):
            if ahead:
                arrive(parts[part])
            for i in range(count):
                product = dot(normed[i], ws[part])
                if part == 2:
                    outs[2 * i + 1][1] = jnp.transpose(product).astype(bf16)
                elif part == 1:
                    outs[2 * i + 1][0] = product.astype(bf16)
                else:
                    outs[2 * i][...] = jnp.transpose(product).astype(bf16) * jnp.asarray(scale, bf16)
        for copy in kept + (later if ahead else []):
            copy.wait()

    out_shape = []
    for _ in which:
        out_shape += [
            jax.ShapeDtypeStruct((sub, tokens), bf16),
            jax.ShapeDtypeStruct((2, tokens, sub), bf16),
        ]
    out_shape.append(jax.ShapeDtypeStruct((count, tokens, width // 2), bf16))
    scratch = [pltpu.SemaphoreType.DMA((2 * count + 3 + ahead,))]
    if ahead:
        out_shape.append(jax.ShapeDtypeStruct(w_qkv.shape, bf16))
        out_shape.append(jax.ShapeDtypeStruct((ahead, tokens, width), bf16))
        scratch = [pltpu.VMEM((count, tokens, width), bf16)] + scratch
    big = ANY_SPEC if ahead else VMEM_SPEC
    outs = pl.pallas_call(
        body,
        in_specs=[SMEM_SPEC, big, VMEM_SPEC, big],
        out_specs=many(VMEM_SPEC, len(out_shape)),
        out_shape=out_shape,
        scratch_shapes=scratch,
        name="proj",
        compiler_params=grant(GRANT_A if ahead else GRANT_B),
        cost_estimate=cost(
            count * 6 * tokens * width * sub, count * tokens * (width + 3 * sub) * 2 + 6 * width * sub
        ),
    )(meta, latents, gain, w_qkv)
    views = {v: (outs[2 * i], outs[2 * i + 1]) for i, v in enumerate(which)}
    return views, *outs[2 * count :]


ONES = 16
SAFE_TOTAL = 1e30
FAR = 1e30


def head_scores(q_ref, kv_ref, h):
    per = LANES // HEAD_DIM
    j, slot = h // per, h % per
    own = q_ref[h * HEAD_DIM : (h + 1) * HEAD_DIM, :]
    zero = jnp.zeros_like(own)
    padded = jnp.concatenate([own if s == slot else zero for s in range(per)], axis=0)
    return dot(kv_ref[0, :, j * LANES : (j + 1) * LANES], padded)


def head_values(kv_ref, h):
    rows = kv_ref[1, h * HEAD_DIM : (h + 1) * HEAD_DIM, :]
    return jnp.concatenate([rows, jnp.ones((ONES, rows.shape[1]), bf16)], axis=0)


def attention_cost(tokens, sub, pairs):
    heads = sub // HEAD_DIM
    return cost(
        pairs * heads * tokens * tokens * 4 * LANES,
        pairs * tokens * sub * 8,
        pairs * heads * tokens * tokens,
    )


def far_if_absent(inter_ref, at, offset):
    return jnp.where(inter_ref[offset, at] > 0, 0.0, FAR).astype(f32)


def sources_of(view, local_views, window):
    found = []
    for o in range(window):
        if view + o + 1 < local_views:
            found.append((view + o + 1, view, o))
        if view - o - 1 >= 0:
            found.append((view - o - 1, view - o - 1, o))
    return found


def attend(
    meta, inter, queries, blocks, remote, plan, window, earlier=None, last=True, carry=None
):
    local_views = len(blocks)
    sub, tokens = queries[0].shape
    heads = sub // HEAD_DIM
    tall = HEAD_DIM + ONES
    views_total = inter.shape[1]
    names = sorted(remote)
    count = len(plan)
    held = 0 if earlier is None else 2

    def body(meta_ref, inter_ref, *refs):
        before, refs = refs[:held], refs[held:]
        qs, refs = refs[:count], refs[count:]
        kvs, refs = refs[:local_views], refs[local_views:]
        far_kvs, refs = dict(zip(names, refs[: len(names)])), refs[len(names) :]
        first = meta_ref[0] * local_views

        def global_view(source):
            at = first + source
            return jnp.where(at < 0, at + views_total, at) if source < 0 else at

        def keys_of(i):
            view, sources = plan[i]
            keys = [] if held else [(kvs[view], None, None)]
            if not held:
                keys += [(kvs[t], source, o) for t, source, o in sources_of(view, local_views, window)]
            return keys + [(far_kvs[name], source, o) for name, source, o in sources]

        if last and carry is not None:
            refs[1][0] = refs[0][...]
            outs, refs = [refs[1].at[1 + i] for i in range(count)], refs[1:]
        elif last:
            outs = refs[:count]
        units = [(i, h, k) for i in range(count) for h in range(heads) for k in keys_of(i)]
        far = {}
        for _, _, (_, source, o) in units:
            if source is not None and (source, o) not in far:
                far[source, o] = far_if_absent(inter_ref, global_view(source), o)
        upcoming = head_scores(qs[units[0][0]], units[0][2][0], units[0][1])
        worst = jnp.zeros((1, tokens), f32)
        n = 0
        for i, (view, _) in enumerate(plan):
            parts = []
            for h in range(heads):
                keys = keys_of(i)
                weights = []
                top = before[1][i, h : h + 1, :] if held else None
                for _, source, o in keys:
                    scores = upcoming
                    n += 1
                    if n < len(units):
                        ni, nh, (nk, _, _) = units[n]
                        upcoming = head_scores(qs[ni], nk, nh)
                    if source is None:
                        top = jnp.max(scores, axis=0, keepdims=True)
                        shift = top
                    else:
                        shift = top + far[source, o]
                    weights.append(jnp.exp(scores - shift).astype(bf16))
                values = jnp.concatenate([head_values(k[0], h) for k in keys], axis=1)
                sums = dot(values, jnp.concatenate(weights, axis=0))
                if held:
                    sums = sums + before[0][i, h * tall : (h + 1) * tall, :]
                if not last:
                    refs[0][i, h * tall : (h + 1) * tall, :] = sums
                    refs[1][i, h : h + 1, :] = top
                    continue
                total = sums[HEAD_DIM : HEAD_DIM + 1, :]
                worst = jnp.maximum(worst, jnp.where(total < SAFE_TOTAL, 0.0, 1.0))
                parts.append(sums[:HEAD_DIM, :] * (1.0 / total))
            if last:
                outs[i][...] = jnp.transpose(jnp.concatenate(parts, axis=0)).astype(bf16)
        if not last:
            return
        work, work_stat = refs[-2:]

        @pl.when(jnp.max(worst) > 0.0)
        def _():
            for i, (view, sources) in enumerate(plan):
                exact_add(qs[i], kvs[view], work, work_stat, heads, True)
                every = [(kvs[t], s, o) for t, s, o in sources_of(view, local_views, window)]
                every += [(far_kvs[name], s, o) for name, s, o in sources]
                for kv, source, o in every:

                    @pl.when(inter_ref[o, global_view(source)] > 0)
                    def _(i=i, kv=kv):
                        exact_add(qs[i], kv, work, work_stat, heads, False)

                parts = []
                for h in range(heads):
                    total = work_stat[h, 1:2, :]
                    parts.append(work[h * HEAD_DIM : (h + 1) * HEAD_DIM, :] * (1.0 / total))
                outs[i][...] = jnp.transpose(jnp.concatenate(parts, axis=0)).astype(bf16)

    if last:
        out_shape = [jax.ShapeDtypeStruct((tokens, sub), bf16)] * count
        if carry is not None:
            out_shape = [jax.ShapeDtypeStruct((1 + count, tokens, sub), bf16)]
        scratch = [pltpu.VMEM((sub, tokens), f32), pltpu.VMEM((heads, 8, tokens), f32)]
    else:
        out_shape = [
            jax.ShapeDtypeStruct((count, heads * tall, tokens), f32),
            jax.ShapeDtypeStruct((count, heads, tokens), f32),
        ]
        scratch = []
    pairs = sum(len(s) for _, s in plan)
    if not held:
        pairs += sum(1 + len(sources_of(v, local_views, window)) for v, _ in plan)
    return pl.pallas_call(
        body,
        in_specs=[SMEM_SPEC, SMEM_SPEC]
        + many(VMEM_SPEC, held + count + local_views + len(names) + (carry is not None)),
        out_specs=many(VMEM_SPEC, len(out_shape)),
        out_shape=out_shape,
        scratch_shapes=scratch,
        name="att",
        compiler_params=grant(12),
        cost_estimate=attention_cost(tokens, sub, pairs),
    )(
        meta,
        inter,
        *(earlier or ()),
        *queries,
        *[blocks[v] for v in range(local_views)],
        *[remote[name] for name in names],
        *(() if carry is None else (carry,)),
    )


def exact_add(q_ref, kv_ref, work, work_stat, heads, start):
    per = LANES // HEAD_DIM

    def one_head(h, _):
        base = pl.multiple_of((h // per) * LANES, LANES)
        queries = q_ref[pl.ds(base, LANES), :]
        owner = lax.broadcasted_iota(jnp.int32, queries.shape, 0) // HEAD_DIM
        queries = jnp.where(owner == h % per, queries.astype(f32), 0.0).astype(bf16)
        scores = dot(kv_ref[0, :, pl.ds(base, LANES)], queries)
        top = jnp.max(scores, axis=0, keepdims=True)
        rows = pl.ds(pl.multiple_of(h * HEAD_DIM, HEAD_DIM), HEAD_DIM)
        values = kv_ref[1, rows, :]
        if not start:
            old = work_stat[h, 0:1, :]
            top = jnp.maximum(old, top)
        weights = jnp.exp(scores - top)
        total = jnp.sum(weights, axis=0, keepdims=True)
        sums = dot(values, weights.astype(bf16))
        if not start:
            fade = jnp.exp(old - top)
            total = total + work_stat[h, 1:2, :] * fade
            sums = sums + work[rows, :] * fade
        work_stat[h, 0:1, :] = top
        work_stat[h, 1:2, :] = total
        work[rows, :] = sums
        return 0

    lax.fori_loop(0, heads, one_head, 0)


def partial_out(meta, attended, near, w_own, w_near, base):
    sub = attended.shape[-1]
    rows_all = attended.size // sub
    width = w_own.shape[1]
    half = width // 2

    def body(meta_ref, att, near_ref, own_ref, near_w_ref, *refs):
        keep, send = refs[-2:]
        side = meta_ref[1] // 2
        here = pl.ds(pl.multiple_of(side * half, half), half)
        away = pl.ds(pl.multiple_of((1 - side) * half, half), half)
        rows = jnp.concatenate([x[...].reshape(rows_all, sub) for x in (att, near_ref)], axis=1)

        def columns(at):
            return jnp.concatenate([own_ref[:, at], near_w_ref[:, at]], axis=0)

        send[...] = dot(rows, columns(away)).astype(bf16)
        total = dot(rows, columns(here))
        start = jnp.concatenate([ref[place] for ref, (_, place) in zip(refs, base)], axis=0)
        keep[...] = start.astype(f32) + total

    return pl.pallas_call(
        body,
        in_specs=[SMEM_SPEC] + many(VMEM_SPEC, 4 + len(base)),
        out_specs=many(VMEM_SPEC, 2),
        out_shape=[
            jax.ShapeDtypeStruct((rows_all, half), f32),
            jax.ShapeDtypeStruct((rows_all, half), bf16),
        ],
        name="part",
        compiler_params=grant(12),
        cost_estimate=cost(4 * rows_all * sub * width, 4 * sub * width + rows_all * width * 6),
    )(meta, attended, near, w_own, w_near, *[array for array, _ in base])


def merge_out(meta, keep, got):
    rows_all, half = keep.shape
    sub = half // 2

    def body(meta_ref, keep_ref, got_ref, own, other):
        layer = (keep_ref[...] + got_ref[...].astype(f32)).astype(bf16)
        low, high = layer[:, :sub], layer[:, sub:]
        odd = meta_ref[1] % 2 == 1
        own[...] = jnp.where(odd, high, low)
        other[...] = jnp.where(odd, low, high)

    return pl.pallas_call(
        body,
        in_specs=[SMEM_SPEC] + many(VMEM_SPEC, 2),
        out_specs=many(VMEM_SPEC, 2),
        out_shape=[jax.ShapeDtypeStruct((rows_all, sub), bf16)] * 2,
        name="merge",
        compiler_params=grant(8),
        cost_estimate=cost(rows_all * half * 2, rows_all * half * 8),
    )(meta, keep, got)


def prepare_requests(block_rows, token_rows, peers, capacity):
    strips, lanes = block_rows.shape

    def body(block_ref, token_ref, wanted_ref, code_ref):
        before = (
            lax.broadcasted_iota(jnp.int32, (lanes, lanes), 0)
            < lax.broadcasted_iota(jnp.int32, (lanes, lanes), 1)
        ).astype(bf16)
        peer_ids = lax.broadcasted_iota(jnp.int32, (peers, lanes), 0)
        carry = jnp.zeros((peers, 1), f32)
        slots, lefts = [], []
        for i in range(strips):
            block = block_ref[i : i + 1, :]
            hit = (peer_ids == block).astype(f32)
            rank = dot(hit.astype(bf16), before) + carry
            carry = carry + jnp.sum(hit, axis=1, keepdims=True)
            slot = jnp.sum(rank * hit, axis=0, keepdims=True)
            slots.append(slot)
            code_ref[i : i + 1, :] = block * capacity + slot.astype(jnp.int32)
            token = token_ref[i : i + 1, :]
            coarse = (token // 32).astype(f32)
            fine = (token % 32).astype(f32)
            lefts.append(jnp.concatenate([hit * coarse, hit * fine], axis=0).astype(bf16))
        columns = jnp.transpose(jnp.concatenate(slots, axis=0))
        place = lax.broadcasted_iota(jnp.int32, (lanes, capacity), 1).astype(f32)
        total = jnp.zeros((2 * peers, capacity), f32)
        for i in range(strips):
            spot = (columns[:, i : i + 1] == place).astype(bf16)
            total = total + dot(lefts[i], spot)
        wanted_ref[...] = (total[:peers] * 32.0 + total[peers:]).astype(jnp.int32)

    return pl.pallas_call(
        body,
        in_specs=[VMEM_SPEC, VMEM_SPEC],
        out_specs=[VMEM_SPEC, VMEM_SPEC],
        out_shape=[
            jax.ShapeDtypeStruct((peers, capacity), jnp.int32),
            jax.ShapeDtypeStruct((strips, lanes), jnp.int32),
        ],
        name="prep",
        compiler_params=grant(8),
        cost_estimate=cost(2 * strips * lanes * lanes * capacity, 3 * strips * lanes * 4),
    )(block_rows, token_rows)


def spread_picks(spread, shift, width):
    clamped = jnp.minimum(jnp.maximum(spread - shift, -1.0), float(width)).astype(bf16)
    wide = jnp.concatenate([clamped] * (width // LANES), axis=1) if width > LANES else clamped[:, :width]
    place = lax.broadcasted_iota(jnp.int32, wide.shape, 1).astype(f32).astype(bf16)
    return jnp.where(wide == place, jnp.ones_like(place), jnp.zeros_like(place))


def gather_rows(meta, wanted, pieces, masks, tokens):
    peers, capacity = int(round(wanted.shape[0] ** 0.5)), wanted.shape[1]
    whole = not isinstance(pieces, list)
    flat = [pieces] if whole else [p for _, *pair in pieces for p in pair]
    sub = flat[0].shape[1]
    rows = flat[0].shape[0] if whole else sum(p.shape[0] for p in flat[::2])
    local_views = rows // tokens

    def body(meta_ref, wanted_ref, *refs):
        ins, outs = refs[: len(flat)], refs[len(flat) :]
        if whole:
            layer = ins[0]
        else:
            layer, outs = outs[0], outs[1:]
            end = jnp.logical_or(meta_ref[1] == 0, meta_ref[1] == meta_ref[2] - 1)
            for c, (views, _, _) in enumerate(pieces):
                for i, v in enumerate(views):
                    at = slice(i * tokens, (i + 1) * tokens)
                    layer[v * tokens : (v + 1) * tokens, :] = jnp.where(
                        end, ins[2 * c + 1][at, :], ins[2 * c][at, :]
                    )
        lines = [wanted_ref[pl.ds(m * peers + meta_ref[0], 1), :] for m in masks]
        lines += [lines[0]] * (-len(lines) % 8)
        columns = jnp.transpose(jnp.concatenate(lines, axis=0).astype(f32))
        for n in range(len(masks)):
            spread = jnp.broadcast_to(columns[:, n : n + 1], (capacity, LANES))
            pick = jnp.concatenate(
                [spread_picks(spread, float(v * tokens), tokens) for v in range(local_views)], axis=1
            )
            outs[n][...] = dot(pick, layer[...]).astype(bf16)

    out_shape = [jax.ShapeDtypeStruct((capacity, sub), bf16)] * len(masks)
    if not whole:
        out_shape = [jax.ShapeDtypeStruct((rows, sub), bf16)] + out_shape
    return pl.pallas_call(
        body,
        in_specs=[SMEM_SPEC] + many(VMEM_SPEC, 1 + len(flat)),
        out_specs=many(VMEM_SPEC, len(out_shape)),
        out_shape=out_shape,
        name="gath",
        compiler_params=grant(12),
        cost_estimate=cost(
            2 * len(masks) * capacity * rows * sub, 2 * (rows + len(masks) * capacity) * sub * 2
        ),
    )(meta, wanted, *flat)


def fetched_part(meta_ref, code_spread, masks, reps, capacity):
    pick = jnp.concatenate(
        [
            spread_picks(
                code_spread, (lax.bitwise_xor(meta_ref[0], mask) * capacity).astype(f32), capacity
            )
            for mask in masks
        ],
        axis=1,
    )
    return dot(pick, jnp.concatenate([r[...] for r in reps], axis=0))


def spread_column(turned, g, per, lanes):
    return jnp.concatenate(
        [
            jnp.broadcast_to(turned[:, g * per + j : g * per + j + 1], (lanes, LANES))
            for j in range(per)
        ],
        axis=0,
    )


def first_replies(meta, code, replies, tokens):
    masks = sorted(replies)
    capacity, sub = replies[masks[0]].shape
    strips, lanes = code.shape
    rows = strips * lanes
    per = tokens // lanes

    def body(meta_ref, code_ref, *refs):
        codes = jnp.transpose(code_ref[...].astype(f32))
        for g in range(rows // tokens):
            refs[-1][g * tokens : (g + 1) * tokens, :] = fetched_part(
                meta_ref, spread_column(codes, g, per, lanes), masks, refs[:-1], capacity
            ).astype(bf16)

    return pl.pallas_call(
        body,
        in_specs=[SMEM_SPEC] + many(VMEM_SPEC, 1 + len(masks)),
        out_specs=VMEM_SPEC,
        out_shape=jax.ShapeDtypeStruct((rows, sub), bf16),
        name="first",
        compiler_params=grant(12),
        cost_estimate=cost(2 * len(masks) * capacity * rows * sub, rows * sub * 4),
    )(meta, code, *[replies[m] for m in masks])


def finish_rows(meta, code, confidence, layer, early, replies, tokens):
    rows, sub = layer.shape
    masks = sorted(replies)
    capacity = replies[masks[0]].shape[0]
    _, lanes = code.shape
    blocks = rows // tokens
    per = tokens // lanes

    def body(meta_ref, code_ref, conf_ref, layer_ref, early_ref, *refs):
        reps, (out_hbm, buffer, sems) = refs[: len(masks)], refs[len(masks) :]
        codes = jnp.transpose(code_ref[...].astype(f32))
        confs = jnp.transpose(conf_ref[...]) * coupling
        copies = []
        for g in range(blocks):
            at = slice(g * tokens, (g + 1) * tokens)
            fetched = early_ref[at, :].astype(f32) + fetched_part(
                meta_ref, spread_column(codes, g, per, lanes), masks, reps, capacity
            )
            wide = layer_ref[at, :].astype(f32)
            weight = jnp.concatenate([spread_column(confs, g, per, lanes)] * (sub // LANES), axis=1)
            buffer[g] = wide + weight * (fetched - wide)
            copies.append(
                pltpu.make_async_copy(
                    buffer.at[g], out_hbm.at[pl.ds(g * tokens, tokens), :], sems.at[g]
                )
            )
            copies[-1].start()
        for copy in copies:
            copy.wait()

    return pl.pallas_call(
        body,
        in_specs=[SMEM_SPEC] + many(VMEM_SPEC, 4 + len(masks)),
        out_specs=ANY_SPEC,
        out_shape=jax.ShapeDtypeStruct((rows, sub), f32),
        scratch_shapes=[
            pltpu.VMEM((blocks, tokens, sub), f32),
            pltpu.SemaphoreType.DMA((blocks,)),
        ],
        name="fin",
        compiler_params=grant(12),
        cost_estimate=cost(2 * len(masks) * capacity * rows * sub, rows * sub * 8),
    )(meta, code, confidence, layer, early, *[replies[m] for m in masks])


def per_device(latents, norm_gain, w_qkv, w_out, intersection, match_block, match_row, confidence):
    local_views, tokens, width = latents.shape
    window = intersection.shape[1]
    sub = w_qkv.shape[2]
    peers = lax.axis_size(VIEWS)
    ends = lax.axis_size(HEADS)
    rows = local_views * tokens
    capacity = 2 * rows // peers
    assert local_views == 4 and window == 2 and ends == 4 and tokens == sub
    view_at, head_at = lax.axis_index(VIEWS), lax.axis_index(HEADS)
    spot = jnp.arange(4, dtype=jnp.int32)
    meta = jnp.where(spot == 0, view_at, jnp.where(spot == 1, head_at, ends)).astype(jnp.int32)

    def along(x, by):
        return lax.ppermute(x, VIEWS, [(i, (i + by) % peers) for i in range(peers)])

    def partner(x, mask):
        return lax.ppermute(x, VIEWS, [(i, i ^ mask) for i in range(peers)])

    def across(x, pairs):
        return lax.ppermute(x, HEADS, pairs)

    def after(x, done):
        return lax.optimization_barrier((x, done))[0]

    beside, middle, back = [(0, 1), (3, 2)], [(1, 2), (2, 1)], [(1, 0), (2, 3)]
    gain = norm_gain.reshape(1, width)
    inter = intersection.T
    w_near = across(w_out, beside)
    far = {}
    projected, edge_halves, weights, inner_latents = project_views(
        meta, latents, gain, w_qkv, (0, 3), (1, 2)
    )
    far["n1"] = along(projected[0][1], -1)
    far["p1"] = along(projected[3][1], 1)
    more, inner_halves = project_views(meta, inner_latents, gain, weights, (1, 2))
    projected.update(more)
    queries = {v: projected[v][0] for v in range(local_views)}
    blocks = {v: projected[v][1] for v in range(local_views)}
    far["n2"] = along(blocks[1], -1)
    far["p2"] = along(blocks[2], 1)
    base = {0: (edge_halves, 0), 3: (edge_halves, 1), 1: (inner_halves, 0), 2: (inner_halves, 1)}

    inner_plan = [(1, [("p1", -1, 1)]), (2, [("n1", 2, 1)])]
    inner_queries = [queries[1], queries[2]]
    local = attend(
        meta, inter, inner_queries, blocks, {}, [(v, []) for v, _ in inner_plan], window, last=False
    )
    attended = {}
    attended["a"], second = attend(
        meta, inter, inner_queries, blocks, dict(n1=far["n1"], p1=far["p1"]), inner_plan, window,
        earlier=tuple(local),
    )

    def attend_outer(view, sources, done, carry=None):
        (result,) = attend(
            meta,
            inter,
            [after(queries[view], done)],
            blocks,
            {s[0]: far[s[0]] for s in sources},
            [(view, sources)],
            window,
            carry=carry,
        )
        return result

    keep, sent, got = {}, {}, {}

    def pass_on(c):
        near = across(attended[c], beside)
        keep[c], sent[c] = partial_out(
            meta,
            attended[c],
            near,
            w_out,
            w_near,
            [base[v] for v in CHUNKS[c]],
        )
        got[c] = across(sent[c], middle)

    attended["b"] = attend_outer(0, [("p1", -1, 0), ("p2", -2, 1)], attended["a"], second)
    pass_on("a")
    attended["c"] = attend_outer(3, [("n1", 3, 0), ("n2", 3, 1)], sent["a"])
    pass_on("b")
    pass_on("c")
    strips = rows // LANES
    wanted, code = prepare_requests(
        after(match_block.reshape(strips, LANES), sent["b"]),
        match_row.reshape(strips, LANES),
        peers,
        capacity,
    )
    mask = 1
    while mask < peers:
        wanted = jnp.concatenate([wanted, partner(wanted, mask)], axis=0)
        mask *= 2
    pieces = []
    for c in CHUNKS:
        own, other = merge_out(meta, keep[c], got[c])
        pieces.append((CHUNKS[c], own, across(other, back)))

    first_masks, last_masks = reply_order(peers)
    replies = {}

    def reply(masks, outgoing):
        for mask, rows_out in zip(masks, outgoing):
            replies[mask] = partner(rows_out, mask)

    layer, *outgoing = gather_rows(meta, wanted, pieces, first_masks, tokens)
    reply(first_masks, outgoing)
    *outgoing, own_rows = gather_rows(meta, wanted, layer, last_masks + [0], tokens)
    reply(last_masks, outgoing)
    late = [m for m in first_masks if m < 3 * peers // 4]
    early = first_replies(
        meta, code, {0: own_rows, **{m: r for m, r in replies.items() if m not in late}}, tokens
    )
    refined = finish_rows(
        meta,
        code,
        confidence.reshape(strips, LANES),
        layer,
        early,
        {m: replies[m] for m in late},
        tokens,
    )
    return refined.reshape(local_views, tokens, sub)


def reply_order(peers):
    far_half = list(range(peers // 2, peers))
    far_half = far_half[len(far_half) // 2 :] + far_half[: len(far_half) // 2]
    pairs = zip(far_half[: len(far_half) // 2], far_half[len(far_half) // 2 :])
    return [m for pair in pairs for m in pair], list(range(2, peers // 2)) + [1]


def solution(mesh):
    in_specs = (
        P(VIEWS, None, None),
        P(),
        P(None, None, HEADS),
        P(HEADS, None),
        P(),
        P(VIEWS, None),
        P(VIEWS),
        P(VIEWS),
    )
    out_specs = P(VIEWS, None, HEADS)
    return jax.shard_map(
        per_device, mesh=mesh, in_specs=in_specs, out_specs=out_specs, check_vma=False
    )
```

```python
import jax
import jax.numpy as jnp
from jax import lax
from jax.experimental import pallas as pl
from jax.experimental.pallas import tpu as pltpu
from jax.sharding import PartitionSpec as P


VIEWS, HEADS = "views", "heads"
HEAD_DIM = 64
LANES = 128
STAGED = 3
GRANT_A, GRANT_B = 50, 40
CHUNKS = dict(a=(1,), b=(2, 0), c=(3,))

coupling = 0.5
epsilon = 1e-06

bf16 = jnp.bfloat16
f32 = jnp.float32


def cost(flops, bytes_accessed, transcendentals=0):
    return pl.CostEstimate(
        flops=int(flops), bytes_accessed=int(bytes_accessed), transcendentals=int(transcendentals)
    )


def dot(a, b):
    return jnp.dot(a, b, preferred_element_type=f32)


VMEM_SPEC = pl.BlockSpec(memory_space=pltpu.VMEM)
SMEM_SPEC = pl.BlockSpec(memory_space=pltpu.SMEM)
ANY_SPEC = pl.BlockSpec(memory_space=pl.ANY)


def grant(mib):
    return pltpu.CompilerParams(vmem_limit_bytes=mib << 20)


def many(spec, count):
    return [spec] * count


def project_views(meta, latents, gain, w_qkv, which, following=()):
    tokens, width = latents.shape[1:]
    sub = w_qkv.shape[2]
    count, ahead = len(which), len(following)
    scale = HEAD_DIM ** (-0.5)

    def body(meta_ref, lat_ref, gain_ref, w_ref, *refs):
        outs, refs = refs[: 2 * count], refs[2 * count :]
        halves, refs = refs[0], refs[1:]
        ws, source = (refs[0], refs[2]) if ahead else (w_ref, lat_ref)
        sems = refs[-1]
        here = pl.ds(pl.multiple_of((meta_ref[1] // 2) * (width // 2), width // 2), width // 2)
        kept = [
            pltpu.make_async_copy(source.at[i, :, here], halves.at[i], sems.at[i])
            for i in range(count)
        ]
        queue, loads, parts = [], [], []
        if ahead:
            loads = [
                pltpu.make_async_copy(lat_ref.at[v], source.at[i], sems.at[count + i])
                for i, v in enumerate(which)
            ]
            parts = [
                pltpu.make_async_copy(w_ref.at[p], ws.at[p], sems.at[2 * count + p]) for p in range(3)
            ]
            later = [
                pltpu.make_async_copy(lat_ref.at[v], refs[1].at[i], sems.at[2 * count + 3 + i])
                for i, v in enumerate(following)
            ]
            queue = loads + [parts[2], parts[1], parts[0]] + later
        for copy in queue[:STAGED]:
            copy.start()
        waiting = queue[STAGED:]

        def arrive(copy):
            copy.wait()
            if waiting:
                waiting.pop(0).start()

        normed = []
        for i in range(count):
            if ahead:
                arrive(loads[i])
            kept[i].start()
            wide = source[i].astype(f32)
            mean_square = jnp.mean(wide * wide, axis=-1, keepdims=True)
            normed.append((wide * lax.rsqrt(mean_square + epsilon) * gain_ref[...]).astype(bf16))
        for part in (2, 1, 0):
            if ahead:
                arrive(parts[part])
            for i in range(count):
                product = dot(normed[i], ws[part])
                if part == 2:
                    outs[2 * i + 1][1] = jnp.transpose(product).astype(bf16)
                elif part == 1:
                    outs[2 * i + 1][0] = product.astype(bf16)
                else:
                    outs[2 * i][...] = jnp.transpose(product).astype(bf16) * jnp.asarray(scale, bf16)
        for copy in kept + (later if ahead else []):
            copy.wait()

    out_shape = []
    for _ in which:
        out_shape += [
            jax.ShapeDtypeStruct((sub, tokens), bf16),
            jax.ShapeDtypeStruct((2, tokens, sub), bf16),
        ]
    out_shape.append(jax.ShapeDtypeStruct((count, tokens, width // 2), bf16))
    scratch = [pltpu.SemaphoreType.DMA((2 * count + 3 + ahead,))]
    if ahead:
        out_shape.append(jax.ShapeDtypeStruct(w_qkv.shape, bf16))
        out_shape.append(jax.ShapeDtypeStruct((ahead, tokens, width), bf16))
        scratch = [pltpu.VMEM((count, tokens, width), bf16)] + scratch
    big = ANY_SPEC if ahead else VMEM_SPEC
    outs = pl.pallas_call(
        body,
        in_specs=[SMEM_SPEC, big, VMEM_SPEC, big],
        out_specs=many(VMEM_SPEC, len(out_shape)),
        out_shape=out_shape,
        scratch_shapes=scratch,
        name="proj",
        compiler_params=grant(GRANT_A if ahead else GRANT_B),
        cost_estimate=cost(
            count * 6 * tokens * width * sub, count * tokens * (width + 3 * sub) * 2 + 6 * width * sub
        ),
    )(meta, latents, gain, w_qkv)
    views = {v: (outs[2 * i], outs[2 * i + 1]) for i, v in enumerate(which)}
    return views, *outs[2 * count :]


ONES = 16
SAFE_TOTAL = 1e30
FAR = 1e30


def head_scores(q_ref, kv_ref, h):
    per = LANES // HEAD_DIM
    j, slot = h // per, h % per
    own = q_ref[h * HEAD_DIM : (h + 1) * HEAD_DIM, :]
    zero = jnp.zeros_like(own)
    padded = jnp.concatenate([own if s == slot else zero for s in range(per)], axis=0)
    return dot(kv_ref[0, :, j * LANES : (j + 1) * LANES], padded)


def head_values(kv_ref, h):
    rows = kv_ref[1, h * HEAD_DIM : (h + 1) * HEAD_DIM, :]
    return jnp.concatenate([rows, jnp.ones((ONES, rows.shape[1]), bf16)], axis=0)


def attention_cost(tokens, sub, pairs):
    heads = sub // HEAD_DIM
    return cost(
        pairs * heads * tokens * tokens * 4 * LANES,
        pairs * tokens * sub * 8,
        pairs * heads * tokens * tokens,
    )


def far_if_absent(inter_ref, at, offset):
    return jnp.where(inter_ref[offset, at] > 0, 0.0, FAR).astype(f32)


def sources_of(view, local_views, window):
    found = []
    for o in range(window):
        if view + o + 1 < local_views:
            found.append((view + o + 1, view, o))
        if view - o - 1 >= 0:
            found.append((view - o - 1, view - o - 1, o))
    return found


def attend(
    meta, inter, queries, blocks, remote, plan, window, earlier=None, last=True, carry=None
):
    local_views = len(blocks)
    sub, tokens = queries[0].shape
    heads = sub // HEAD_DIM
    tall = HEAD_DIM + ONES
    views_total = inter.shape[1]
    names = sorted(remote)
    count = len(plan)
    held = 0 if earlier is None else 2

    def body(meta_ref, inter_ref, *refs):
        before, refs = refs[:held], refs[held:]
        qs, refs = refs[:count], refs[count:]
        kvs, refs = refs[:local_views], refs[local_views:]
        far_kvs, refs = dict(zip(names, refs[: len(names)])), refs[len(names) :]
        first = meta_ref[0] * local_views

        def global_view(source):
            at = first + source
            return jnp.where(at < 0, at + views_total, at) if source < 0 else at

        def keys_of(i):
            view, sources = plan[i]
            keys = [] if held else [(kvs[view], None, None)]
            if not held:
                keys += [(kvs[t], source, o) for t, source, o in sources_of(view, local_views, window)]
            return keys + [(far_kvs[name], source, o) for name, source, o in sources]

        if last and carry is not None:
            refs[1][0] = refs[0][...]
            outs, refs = [refs[1].at[1 + i] for i in range(count)], refs[1:]
        elif last:
            outs = refs[:count]
        units = [(i, h, k) for i in range(count) for h in range(heads) for k in keys_of(i)]
        far = {}
        for _, _, (_, source, o) in units:
            if source is not None and (source, o) not in far:
                far[source, o] = far_if_absent(inter_ref, global_view(source), o)
        upcoming = head_scores(qs[units[0][0]], units[0][2][0], units[0][1])
        worst = jnp.zeros((1, tokens), f32)
        n = 0
        for i, (view, _) in enumerate(plan):
            parts = []
            for h in range(heads):
                keys = keys_of(i)
                weights = []
                top = before[1][i, h : h + 1, :] if held else None
                for _, source, o in keys:
                    scores = upcoming
                    n += 1
                    if n < len(units):
                        ni, nh, (nk, _, _) = units[n]
                        upcoming = head_scores(qs[ni], nk, nh)
                    if source is None:
                        top = jnp.max(scores, axis=0, keepdims=True)
                        shift = top
                    else:
                        shift = top + far[source, o]
                    weights.append(jnp.exp(scores - shift).astype(bf16))
                values = jnp.concatenate([head_values(k[0], h) for k in keys], axis=1)
                sums = dot(values, jnp.concatenate(weights, axis=0))
                if held:
                    sums = sums + before[0][i, h * tall : (h + 1) * tall, :]
                if not last:
                    refs[0][i, h * tall : (h + 1) * tall, :] = sums
                    refs[1][i, h : h + 1, :] = top
                    continue
                total = sums[HEAD_DIM : HEAD_DIM + 1, :]
                worst = jnp.maximum(worst, jnp.where(total < SAFE_TOTAL, 0.0, 1.0))
                parts.append(sums[:HEAD_DIM, :] * (1.0 / total))
            if last:
                outs[i][...] = jnp.transpose(jnp.concatenate(parts, axis=0)).astype(bf16)
        if not last:
            return
        work, work_stat = refs[-2:]

        @pl.when(jnp.max(worst) > 0.0)
        def _():
            for i, (view, sources) in enumerate(plan):
                exact_add(qs[i], kvs[view], work, work_stat, heads, True)
                every = [(kvs[t], s, o) for t, s, o in sources_of(view, local_views, window)]
                every += [(far_kvs[name], s, o) for name, s, o in sources]
                for kv, source, o in every:

                    @pl.when(inter_ref[o, global_view(source)] > 0)
                    def _(i=i, kv=kv):
                        exact_add(qs[i], kv, work, work_stat, heads, False)

                parts = []
                for h in range(heads):
                    total = work_stat[h, 1:2, :]
                    parts.append(work[h * HEAD_DIM : (h + 1) * HEAD_DIM, :] * (1.0 / total))
                outs[i][...] = jnp.transpose(jnp.concatenate(parts, axis=0)).astype(bf16)

    if last:
        out_shape = [jax.ShapeDtypeStruct((tokens, sub), bf16)] * count
        if carry is not None:
            out_shape = [jax.ShapeDtypeStruct((1 + count, tokens, sub), bf16)]
        scratch = [pltpu.VMEM((sub, tokens), f32), pltpu.VMEM((heads, 8, tokens), f32)]
    else:
        out_shape = [
            jax.ShapeDtypeStruct((count, heads * tall, tokens), f32),
            jax.ShapeDtypeStruct((count, heads, tokens), f32),
        ]
        scratch = []
    pairs = sum(len(s) for _, s in plan)
    if not held:
        pairs += sum(1 + len(sources_of(v, local_views, window)) for v, _ in plan)
    return pl.pallas_call(
        body,
        in_specs=[SMEM_SPEC, SMEM_SPEC]
        + many(VMEM_SPEC, held + count + local_views + len(names) + (carry is not None)),
        out_specs=many(VMEM_SPEC, len(out_shape)),
        out_shape=out_shape,
        scratch_shapes=scratch,
        name="att",
        compiler_params=grant(12),
        cost_estimate=attention_cost(tokens, sub, pairs),
    )(
        meta,
        inter,
        *(earlier or ()),
        *queries,
        *[blocks[v] for v in range(local_views)],
        *[remote[name] for name in names],
        *(() if carry is None else (carry,)),
    )


def exact_add(q_ref, kv_ref, work, work_stat, heads, start):
    per = LANES // HEAD_DIM

    def one_head(h, _):
        base = pl.multiple_of((h // per) * LANES, LANES)
        queries = q_ref[pl.ds(base, LANES), :]
        owner = lax.broadcasted_iota(jnp.int32, queries.shape, 0) // HEAD_DIM
        queries = jnp.where(owner == h % per, queries.astype(f32), 0.0).astype(bf16)
        scores = dot(kv_ref[0, :, pl.ds(base, LANES)], queries)
        top = jnp.max(scores, axis=0, keepdims=True)
        rows = pl.ds(pl.multiple_of(h * HEAD_DIM, HEAD_DIM), HEAD_DIM)
        values = kv_ref[1, rows, :]
        if not start:
            old = work_stat[h, 0:1, :]
            top = jnp.maximum(old, top)
        weights = jnp.exp(scores - top)
        total = jnp.sum(weights, axis=0, keepdims=True)
        sums = dot(values, weights.astype(bf16))
        if not start:
            fade = jnp.exp(old - top)
            total = total + work_stat[h, 1:2, :] * fade
            sums = sums + work[rows, :] * fade
        work_stat[h, 0:1, :] = top
        work_stat[h, 1:2, :] = total
        work[rows, :] = sums
        return 0

    lax.fori_loop(0, heads, one_head, 0)


def partial_out(meta, attended, near, w_own, w_near, base):
    sub = attended.shape[-1]
    rows_all = attended.size // sub
    width = w_own.shape[1]
    half = width // 2

    def body(meta_ref, att, near_ref, own_ref, near_w_ref, *refs):
        keep, send = refs[-2:]
        side = meta_ref[1] // 2
        here = pl.ds(pl.multiple_of(side * half, half), half)
        away = pl.ds(pl.multiple_of((1 - side) * half, half), half)
        rows = jnp.concatenate([x[...].reshape(rows_all, sub) for x in (att, near_ref)], axis=1)

        def columns(at):
            return jnp.concatenate([own_ref[:, at], near_w_ref[:, at]], axis=0)

        send[...] = dot(rows, columns(away)).astype(bf16)
        total = dot(rows, columns(here))
        start = jnp.concatenate([ref[place] for ref, (_, place) in zip(refs, base)], axis=0)
        keep[...] = start.astype(f32) + total

    return pl.pallas_call(
        body,
        in_specs=[SMEM_SPEC] + many(VMEM_SPEC, 4 + len(base)),
        out_specs=many(VMEM_SPEC, 2),
        out_shape=[
            jax.ShapeDtypeStruct((rows_all, half), f32),
            jax.ShapeDtypeStruct((rows_all, half), bf16),
        ],
        name="part",
        compiler_params=grant(12),
        cost_estimate=cost(4 * rows_all * sub * width, 4 * sub * width + rows_all * width * 6),
    )(meta, attended, near, w_own, w_near, *[array for array, _ in base])


def merge_out(meta, keep, got):
    rows_all, half = keep.shape
    sub = half // 2

    def body(meta_ref, keep_ref, got_ref, own, other):
        layer = (keep_ref[...] + got_ref[...].astype(f32)).astype(bf16)
        low, high = layer[:, :sub], layer[:, sub:]
        odd = meta_ref[1] % 2 == 1
        own[...] = jnp.where(odd, high, low)
        other[...] = jnp.where(odd, low, high)

    return pl.pallas_call(
        body,
        in_specs=[SMEM_SPEC] + many(VMEM_SPEC, 2),
        out_specs=many(VMEM_SPEC, 2),
        out_shape=[jax.ShapeDtypeStruct((rows_all, sub), bf16)] * 2,
        name="merge",
        compiler_params=grant(8),
        cost_estimate=cost(rows_all * half * 2, rows_all * half * 8),
    )(meta, keep, got)


def prepare_requests(block_rows, token_rows, peers, capacity):
    strips, lanes = block_rows.shape

    def body(block_ref, token_ref, wanted_ref, code_ref):
        before = (
            lax.broadcasted_iota(jnp.int32, (lanes, lanes), 0)
            < lax.broadcasted_iota(jnp.int32, (lanes, lanes), 1)
        ).astype(bf16)
        peer_ids = lax.broadcasted_iota(jnp.int32, (peers, lanes), 0)
        carry = jnp.zeros((peers, 1), f32)
        slots, lefts = [], []
        for i in range(strips):
            block = block_ref[i : i + 1, :]
            hit = (peer_ids == block).astype(f32)
            rank = dot(hit.astype(bf16), before) + carry
            carry = carry + jnp.sum(hit, axis=1, keepdims=True)
            slot = jnp.sum(rank * hit, axis=0, keepdims=True)
            slots.append(slot)
            code_ref[i : i + 1, :] = block * capacity + slot.astype(jnp.int32)
            token = token_ref[i : i + 1, :]
            coarse = (token // 32).astype(f32)
            fine = (token % 32).astype(f32)
            lefts.append(jnp.concatenate([hit * coarse, hit * fine], axis=0).astype(bf16))
        columns = jnp.transpose(jnp.concatenate(slots, axis=0))
        place = lax.broadcasted_iota(jnp.int32, (lanes, capacity), 1).astype(f32)
        total = jnp.zeros((2 * peers, capacity), f32)
        for i in range(strips):
            spot = (columns[:, i : i + 1] == place).astype(bf16)
            total = total + dot(lefts[i], spot)
        wanted_ref[...] = (total[:peers] * 32.0 + total[peers:]).astype(jnp.int32)

    return pl.pallas_call(
        body,
        in_specs=[VMEM_SPEC, VMEM_SPEC],
        out_specs=[VMEM_SPEC, VMEM_SPEC],
        out_shape=[
            jax.ShapeDtypeStruct((peers, capacity), jnp.int32),
            jax.ShapeDtypeStruct((strips, lanes), jnp.int32),
        ],
        name="prep",
        compiler_params=grant(8),
        cost_estimate=cost(2 * strips * lanes * lanes * capacity, 3 * strips * lanes * 4),
    )(block_rows, token_rows)


def spread_picks(spread, shift, width):
    clamped = jnp.minimum(jnp.maximum(spread - shift, -1.0), float(width)).astype(bf16)
    wide = jnp.concatenate([clamped] * (width // LANES), axis=1) if width > LANES else clamped[:, :width]
    place = lax.broadcasted_iota(jnp.int32, wide.shape, 1).astype(f32).astype(bf16)
    return jnp.where(wide == place, jnp.ones_like(place), jnp.zeros_like(place))


def gather_rows(meta, wanted, pieces, masks, tokens):
    peers, capacity = int(round(wanted.shape[0] ** 0.5)), wanted.shape[1]
    whole = not isinstance(pieces, list)
    flat = [pieces] if whole else [p for _, *pair in pieces for p in pair]
    sub = flat[0].shape[1]
    rows = flat[0].shape[0] if whole else sum(p.shape[0] for p in flat[::2])
    local_views = rows // tokens

    def body(meta_ref, wanted_ref, *refs):
        ins, outs = refs[: len(flat)], refs[len(flat) :]
        if whole:
            layer = ins[0]
        else:
            layer, outs = outs[0], outs[1:]
            end = jnp.logical_or(meta_ref[1] == 0, meta_ref[1] == meta_ref[2] - 1)
            for c, (views, _, _) in enumerate(pieces):
                for i, v in enumerate(views):
                    at = slice(i * tokens, (i + 1) * tokens)
                    layer[v * tokens : (v + 1) * tokens, :] = jnp.where(
                        end, ins[2 * c + 1][at, :], ins[2 * c][at, :]
                    )
        lines = [wanted_ref[pl.ds(m * peers + meta_ref[0], 1), :] for m in masks]
        lines += [lines[0]] * (-len(lines) % 8)
        columns = jnp.transpose(jnp.concatenate(lines, axis=0).astype(f32))
        for n in range(len(masks)):
            spread = jnp.broadcast_to(columns[:, n : n + 1], (capacity, LANES))
            pick = jnp.concatenate(
                [spread_picks(spread, float(v * tokens), tokens) for v in range(local_views)], axis=1
            )
            outs[n][...] = dot(pick, layer[...]).astype(bf16)

    out_shape = [jax.ShapeDtypeStruct((capacity, sub), bf16)] * len(masks)
    if not whole:
        out_shape = [jax.ShapeDtypeStruct((rows, sub), bf16)] + out_shape
    return pl.pallas_call(
        body,
        in_specs=[SMEM_SPEC] + many(VMEM_SPEC, 1 + len(flat)),
        out_specs=many(VMEM_SPEC, len(out_shape)),
        out_shape=out_shape,
        name="gath",
        compiler_params=grant(12),
        cost_estimate=cost(
            2 * len(masks) * capacity * rows * sub, 2 * (rows + len(masks) * capacity) * sub * 2
        ),
    )(meta, wanted, *flat)


def fetched_part(meta_ref, code_spread, masks, reps, capacity):
    pick = jnp.concatenate(
        [
            spread_picks(
                code_spread, (lax.bitwise_xor(meta_ref[0], mask) * capacity).astype(f32), capacity
            )
            for mask in masks
        ],
        axis=1,
    )
    return dot(pick, jnp.concatenate([r[...] for r in reps], axis=0))


def spread_column(turned, g, per, lanes):
    return jnp.concatenate(
        [
            jnp.broadcast_to(turned[:, g * per + j : g * per + j + 1], (lanes, LANES))
            for j in range(per)
        ],
        axis=0,
    )


def first_replies(meta, code, replies, tokens):
    masks = sorted(replies)
    capacity, sub = replies[masks[0]].shape
    strips, lanes = code.shape
    rows = strips * lanes
    per = tokens // lanes

    def body(meta_ref, code_ref, *refs):
        codes = jnp.transpose(code_ref[...].astype(f32))
        for g in range(rows // tokens):
            refs[-1][g * tokens : (g + 1) * tokens, :] = fetched_part(
                meta_ref, spread_column(codes, g, per, lanes), masks, refs[:-1], capacity
            ).astype(bf16)

    return pl.pallas_call(
        body,
        in_specs=[SMEM_SPEC] + many(VMEM_SPEC, 1 + len(masks)),
        out_specs=VMEM_SPEC,
        out_shape=jax.ShapeDtypeStruct((rows, sub), bf16),
        name="first",
        compiler_params=grant(12),
        cost_estimate=cost(2 * len(masks) * capacity * rows * sub, rows * sub * 4),
    )(meta, code, *[replies[m] for m in masks])


def finish_rows(meta, code, confidence, layer, early, replies, tokens):
    rows, sub = layer.shape
    masks = sorted(replies)
    capacity = replies[masks[0]].shape[0]
    _, lanes = code.shape
    blocks = rows // tokens
    per = tokens // lanes

    def body(meta_ref, code_ref, conf_ref, layer_ref, early_ref, *refs):
        reps, (out_hbm, buffer, sems) = refs[: len(masks)], refs[len(masks) :]
        codes = jnp.transpose(code_ref[...].astype(f32))
        confs = jnp.transpose(conf_ref[...]) * coupling
        copies = []
        for g in range(blocks):
            at = slice(g * tokens, (g + 1) * tokens)
            fetched = early_ref[at, :].astype(f32) + fetched_part(
                meta_ref, spread_column(codes, g, per, lanes), masks, reps, capacity
            )
            wide = layer_ref[at, :].astype(f32)
            weight = jnp.concatenate([spread_column(confs, g, per, lanes)] * (sub // LANES), axis=1)
            buffer[g] = wide + weight * (fetched - wide)
            copies.append(
                pltpu.make_async_copy(
                    buffer.at[g], out_hbm.at[pl.ds(g * tokens, tokens), :], sems.at[g]
                )
            )
            copies[-1].start()
        for copy in copies:
            copy.wait()

    return pl.pallas_call(
        body,
        in_specs=[SMEM_SPEC] + many(VMEM_SPEC, 4 + len(masks)),
        out_specs=ANY_SPEC,
        out_shape=jax.ShapeDtypeStruct((rows, sub), f32),
        scratch_shapes=[
            pltpu.VMEM((blocks, tokens, sub), f32),
            pltpu.SemaphoreType.DMA((blocks,)),
        ],
        name="fin",
        compiler_params=grant(12),
        cost_estimate=cost(2 * len(masks) * capacity * rows * sub, rows * sub * 8),
    )(meta, code, confidence, layer, early, *[replies[m] for m in masks])


def per_device(latents, norm_gain, w_qkv, w_out, intersection, match_block, match_row, confidence):
    local_views, tokens, width = latents.shape
    window = intersection.shape[1]
    sub = w_qkv.shape[2]
    peers = lax.axis_size(VIEWS)
    ends = lax.axis_size(HEADS)
    rows = local_views * tokens
    capacity = 2 * rows // peers
    assert local_views == 4 and window == 2 and ends == 4 and tokens == sub
    view_at, head_at = lax.axis_index(VIEWS), lax.axis_index(HEADS)
    spot = jnp.arange(4, dtype=jnp.int32)
    meta = jnp.where(spot == 0, view_at, jnp.where(spot == 1, head_at, ends)).astype(jnp.int32)

    def along(x, by):
        return lax.ppermute(x, VIEWS, [(i, (i + by) % peers) for i in range(peers)])

    def partner(x, mask):
        return lax.ppermute(x, VIEWS, [(i, i ^ mask) for i in range(peers)])

    def across(x, pairs):
        return lax.ppermute(x, HEADS, pairs)

    def after(x, done):
        return lax.optimization_barrier((x, done))[0]

    beside, middle, back = [(0, 1), (3, 2)], [(1, 2), (2, 1)], [(1, 0), (2, 3)]
    gain = norm_gain.reshape(1, width)
    inter = intersection.T
    w_near = across(w_out, beside)
    far = {}
    projected, edge_halves, weights, inner_latents = project_views(
        meta, latents, gain, w_qkv, (0, 3), (1, 2)
    )
    far["n1"] = along(projected[0][1], -1)
    far["p1"] = along(projected[3][1], 1)
    more, inner_halves = project_views(meta, inner_latents, gain, weights, (1, 2))
    projected.update(more)
    queries = {v: projected[v][0] for v in range(local_views)}
    blocks = {v: projected[v][1] for v in range(local_views)}
    far["n2"] = along(blocks[1], -1)
    far["p2"] = along(blocks[2], 1)
    base = {0: (edge_halves, 0), 3: (edge_halves, 1), 1: (inner_halves, 0), 2: (inner_halves, 1)}

    inner_plan = [(1, [("p1", -1, 1)]), (2, [("n1", 2, 1)])]
    inner_queries = [queries[1], queries[2]]
    local = attend(
        meta, inter, inner_queries, blocks, {}, [(v, []) for v, _ in inner_plan], window, last=False
    )
    attended = {}
    attended["a"], second = attend(
        meta, inter, inner_queries, blocks, dict(n1=far["n1"], p1=far["p1"]), inner_plan, window,
        earlier=tuple(local),
    )

    def attend_outer(view, sources, done, carry=None):
        (result,) = attend(
            meta,
            inter,
            [after(queries[view], done)],
            blocks,
            {s[0]: far[s[0]] for s in sources},
            [(view, sources)],
            window,
            carry=carry,
        )
        return result

    keep, sent, got = {}, {}, {}

    def pass_on(c):
        near = across(attended[c], beside)
        keep[c], sent[c] = partial_out(
            meta,
            attended[c],
            near,
            w_out,
            w_near,
            [base[v] for v in CHUNKS[c]],
        )
        got[c] = across(sent[c], middle)

    attended["b"] = attend_outer(0, [("p1", -1, 0), ("p2", -2, 1)], attended["a"], second)
    pass_on("a")
    attended["c"] = attend_outer(3, [("n1", 3, 0), ("n2", 3, 1)], sent["a"])
    pass_on("b")
    pass_on("c")
    strips = rows // LANES
    wanted, code = prepare_requests(
        after(match_block.reshape(strips, LANES), sent["b"]),
        match_row.reshape(strips, LANES),
        peers,
        capacity,
    )
    mask = 1
    while mask < peers:
        wanted = jnp.concatenate([wanted, partner(wanted, mask)], axis=0)
        mask *= 2
    pieces = []
    for c in CHUNKS:
        own, other = merge_out(meta, keep[c], got[c])
        pieces.append((CHUNKS[c], own, across(other, back)))

    first_masks, last_masks = reply_order(peers)
    replies = {}

    def reply(masks, outgoing):
        for mask, rows_out in zip(masks, outgoing):
            replies[mask] = partner(rows_out, mask)

    layer, *outgoing = gather_rows(meta, wanted, pieces, first_masks, tokens)
    reply(first_masks, outgoing)
    *outgoing, own_rows = gather_rows(meta, wanted, layer, last_masks + [0], tokens)
    reply(last_masks, outgoing)
    late = late_masks(peers)
    early = first_replies(
        meta, code, {0: own_rows, **{m: r for m, r in replies.items() if m not in late}}, tokens
    )
    refined = finish_rows(
        meta,
        code,
        confidence.reshape(strips, LANES),
        layer,
        early,
        {m: replies[m] for m in late},
        tokens,
    )
    return refined.reshape(local_views, tokens, sub)


def reply_order(peers):
    far_half = list(range(peers // 2, peers))
    far_half = far_half[len(far_half) // 2 :] + far_half[: len(far_half) // 2]
    pairs = zip(far_half[: len(far_half) // 2], far_half[len(far_half) // 2 :])
    return [m for pair in pairs for m in pair], list(range(2, peers // 2)) + [1]


def late_masks(peers):
    first_masks, last_masks = reply_order(peers)
    straight = [m for m in first_masks if m < 3 * peers // 4]
    beside = [m for m in last_masks if m > 1]
    return straight[len(straight) // 2 :] + beside[len(beside) // 2 :]


def solution(mesh):
    in_specs = (
        P(VIEWS, None, None),
        P(),
        P(None, None, HEADS),
        P(HEADS, None),
        P(),
        P(VIEWS, None),
        P(VIEWS),
        P(VIEWS),
    )
    out_specs = P(VIEWS, None, HEADS)
    return jax.shard_map(
        per_device, mesh=mesh, in_specs=in_specs, out_specs=out_specs, check_vma=False
    )
```
